256 devices in a mesh: gx: 8 (over x, core), gy: 32 (over z, y).
Axes of the slice: x: 4, y: 4, z: 8, core: 2. Of those that a mesh axis runs over, the one named last changes fastest.
Arguments:
- residual: float32 [1024, 1024, 256], P('gx', 'gy'), may hold values from -6 to 6
- local_x: bfloat16 [136, 136], replicated, may hold values from -0.5 to 0.5
- local_y: bfloat16 [40, 40], replicated, may hold values from -1 to 1
- local_z: bfloat16 [256, 256], replicated, may hold values from -0.375 to 0.375
- eig_x: float32 [136], replicated, may hold values from 0.1 to 2
- eig_y: float32 [40], replicated, may hold values from 0.1 to 2
- eig_z: float32 [256], replicated, may hold values from 0.1 to 2
- coarse_x: bfloat16 [128, 4], replicated, may hold values from -0.5 to 0.5
- coarse_y: bfloat16 [32, 4], replicated, may hold values from -1 to 1
- coarse_z: bfloat16 [256, 4], replicated, may hold values from -0.375 to 0.375
- mode_x: float32 [32, 32], replicated, may hold values from -1 to 1
- mode_y: float32 [128, 128], replicated, may hold values from -0.5 to 0.5
- mode_z: float32 [4, 4], replicated, may hold values from -3 to 3
- coarse_eig_x: float32 [32], replicated, may hold values from 0.002 to 0.02
- coarse_eig_y: float32 [128], replicated, may hold values from 0.002 to 0.02
- coarse_eig_z: float32 [4], replicated, may hold values from 0.002 to 0.02
Outputs:
- preconditioned: float32 [1024, 1024, 256], P('gx', 'gy')
The draws below stay inside these ranges and needn't reach their ends.
All inputs are finite; a program needn't handle non-finite values.
Results may differ from the reference program's by a relative error of at most 0.0045.
Values may be sent and summed in bfloat16 or wider, within the bound.
No kernel may reach another device: no remote copies, remote signals or barrier semaphores. Data moves between devices by JAX's collectives and lax.ppermute only.
A program may use at most 64 MiB of HBM per device.

```python
import math
import jax
import jax.numpy as jnp
from jax import lax

CX = 128
CY = 32
NZ = 256
OV = 4
MODES = 4
EX = 136
EY = 40
NX = 1024
NY = 1024
GXM = 32
GYM = 128
N_GX = 8
N_GY = 32


def shard_levels(key, dims, pieces, low, largest):
    gain = 1.0
    for position, shards_of in pieces:
        heights = jax.random.uniform(jax.random.fold_in(jax.random.fold_in(key, 6), position), (shards_of,), jnp.float32, low / len(pieces), largest / len(pieces))
        gain = gain * jnp.repeat(jnp.exp(heights), dims[position] // shards_of).reshape((-1,) + (1,) * (len(dims) - 1 - position))
    return gain


def centred(own_key, extent, scale, most, shards=(), kind=jnp.bfloat16):
    gain = shard_levels(own_key, extent, shards, -0.22, 0.18) if shards else 1.0
    array = jax.random.normal(own_key, extent, jnp.float32) * scale * gain
    return jnp.minimum(jnp.maximum(array, -most), most).astype(kind)


def setup_inputs(seed: int = 0) -> dict:
    streams_of = jax.random.split(jax.random.key(seed), 17)
    return {
        "residual": centred(streams_of[0], (NX, NY, NZ), 1.0, 6.0, ((0, 8), (1, 32)), jnp.float32),
        "local_x": centred(streams_of[1], (EX, EX), EX ** -0.5, 0.5),
        "local_y": centred(streams_of[2], (EY, EY), EY ** -0.5, 1.0),
        "local_z": centred(streams_of[3], (NZ, NZ), NZ ** -0.5, 0.375),
        "eig_x": jnp.clip(jnp.exp(jax.random.uniform(streams_of[4], (EX,), jnp.float32, math.log(0.1), math.log(2.0))), 0.1, 2.0),
        "eig_y": jnp.clip(jnp.exp(jax.random.uniform(streams_of[5], (EY,), jnp.float32, math.log(0.1), math.log(2.0))), 0.1, 2.0),
        "eig_z": jnp.clip(jnp.exp(jax.random.uniform(streams_of[6], (NZ,), jnp.float32, math.log(0.1), math.log(2.0))), 0.1, 2.0),
        "coarse_x": centred(streams_of[7], (CX, MODES), CX ** -0.5, 0.5),
        "coarse_y": centred(streams_of[8], (CY, MODES), CY ** -0.5, 1.0),
        "coarse_z": centred(streams_of[9], (NZ, MODES), NZ ** -0.5, 0.375),
        "mode_x": centred(streams_of[10], (GXM, GXM), GXM ** -0.5, 1.0, (), jnp.float32),
        "mode_y": centred(streams_of[11], (GYM, GYM), GYM ** -0.5, 0.5, (), jnp.float32),
        "mode_z": centred(streams_of[12], (MODES, MODES), MODES ** -0.5, 3.0, (), jnp.float32),
        "coarse_eig_x": jnp.clip(jnp.exp(jax.random.uniform(streams_of[13], (GXM,), jnp.float32, math.log(0.002), math.log(0.02))), 0.002, 0.02),
        "coarse_eig_y": jnp.clip(jnp.exp(jax.random.uniform(streams_of[14], (GYM,), jnp.float32, math.log(0.002), math.log(0.02))), 0.002, 0.02),
        "coarse_eig_z": jnp.clip(jnp.exp(jax.random.uniform(streams_of[15], (MODES,), jnp.float32, math.log(0.002), math.log(0.02))), 0.002, 0.02),
    }


def solve_local(block, local_x, local_y, local_z, scales):
    lx = local_x.astype(jnp.float32)
    ly = local_y.astype(jnp.float32)
    lz = local_z.astype(jnp.float32)
    first_x = jnp.einsum('xa,xyz->ayz', lx, block.astype(jnp.float32)).astype(jnp.bfloat16)
    first_y = jnp.einsum('yb,ayz->abz', ly, first_x.astype(jnp.float32)).astype(jnp.bfloat16)
    along = jnp.einsum('zc,abz->abc', lz, first_y.astype(jnp.float32))
    spectral = (along / scales).astype(jnp.bfloat16)
    back_z = jnp.einsum('zc,abc->abz', lz, spectral.astype(jnp.float32)).astype(jnp.bfloat16)
    back_y = jnp.einsum('yb,abz->ayz', ly, back_z.astype(jnp.float32)).astype(jnp.bfloat16)
    return jnp.einsum('xa,ayz->xyz', lx, back_y.astype(jnp.float32))


def reference(residual, local_x, local_y, local_z, eig_x, eig_y, eig_z, coarse_x, coarse_y, coarse_z, mode_x, mode_y, mode_z, coarse_eig_x, coarse_eig_y, coarse_eig_z):
    rounded = residual.astype(jnp.bfloat16)
    padded = jnp.pad(rounded, ((OV, OV), (OV, OV), (0, 0)), mode="wrap")
    scales = eig_x[:, None, None] + eig_y[None, :, None] + eig_z[None, None, :]
    total = jnp.zeros((NX + 2 * OV, NY + 2 * OV, NZ), jnp.float32)
    zero_index = jnp.zeros((), jnp.int32)

    def visit(number, total):
        number = jnp.asarray(number).astype(jnp.int32)
        row_start = ((number // N_GY) * CX).astype(jnp.int32)
        col_start = ((number % N_GY) * CY).astype(jnp.int32)
        block = lax.dynamic_slice(padded, (row_start, col_start, zero_index), (CX + 2 * OV, CY + 2 * OV, NZ))
        fix = solve_local(block, local_x, local_y, local_z, scales)
        former = lax.dynamic_slice(total, (row_start, col_start, zero_index), (CX + 2 * OV, CY + 2 * OV, NZ))
        return lax.dynamic_update_slice(total, former + fix, (row_start, col_start, zero_index))

    total = lax.fori_loop(0, N_GX * N_GY, visit, total)
    rows = total[OV:OV + NX]
    rows = rows.at[:OV].add(total[OV + NX:])
    rows = rows.at[NX - OV:].add(total[:OV])
    fine = rows[:, OV:OV + NY]
    fine = fine.at[:, :OV].add(rows[:, OV + NY:])
    fine = fine.at[:, NY - OV:].add(rows[:, :OV])

    along_z = jnp.dot(rounded.reshape(-1, NZ), coarse_z, preferred_element_type=jnp.float32)
    along_z = along_z.reshape(N_GX, CX, N_GY, CY, MODES)
    basis_x = coarse_x.astype(jnp.float32)
    basis_y = coarse_y.astype(jnp.float32)
    coarse_res = jnp.einsum('ixjyp,xm,yn->imjnp', along_z, basis_x, basis_y, precision=lax.Precision.HIGHEST)
    coarse_res = coarse_res.reshape(GXM, GYM, MODES)
    coarse_hat = jnp.einsum('IJp,Ia,Jb,pc->abc', coarse_res, mode_x, mode_y, mode_z, precision=lax.Precision.HIGHEST)
    coarse_hat = coarse_hat / (coarse_eig_x[:, None, None] + coarse_eig_y[None, :, None] + coarse_eig_z[None, None, :])
    coarse_sol = jnp.einsum('abc,Ia,Jb,pc->IJp', coarse_hat, mode_x, mode_y, mode_z, precision=lax.Precision.HIGHEST)
    coarse_sol = coarse_sol.reshape(N_GX, MODES, N_GY, MODES, MODES)
    spread = jnp.einsum('imjnp,xm,yn->ixjyp', coarse_sol, basis_x, basis_y, precision=lax.Precision.HIGHEST)
    coarse_fix = jnp.dot(spread.reshape(-1, MODES), coarse_z.astype(jnp.float32).T, precision=lax.Precision.HIGHEST)
    return fine + coarse_fix.reshape(NX, NY, NZ)
```

```python
import jax
import jax.numpy as jnp
from jax import lax
from jax.experimental import pallas as pl
from jax.experimental.pallas import tpu as pltpu
from jax.sharding import PartitionSpec as P

OV = 4
MODES = 4
CX = 128
CY = 32
NZ = 256
EX = 136
EY = 40
GX = 4
ROWS = GX * EY
BLOCKS = CX // GX
BB = 8
HI = lax.Precision.HIGHEST
f32 = jnp.float32
bf16 = jnp.bfloat16


def dot(a, b):
    return jnp.dot(a, b, preferred_element_type=f32)


def solve_kernel(
    own, xlo, xhi, ylo, yhi, wy, wyt, wx, wxt, lz, lzt, ex, ey, ez,
    fix, out_xlo, out_xhi, out_ylo, out_yhi, field, mid,
):
    own_rows = GX * CY
    halo_rows = GX * OV

    def put(rows, value):
        field[0, rows, :] = value[:, :128]
        field[1, rows, :] = value[:, 128:]

    def take(rows):
        return jnp.concatenate([field[0, rows, :], field[1, rows, :]], 1)

    def forward_y(main, k):
        low = ylo[pl.ds(pl.multiple_of(k * halo_rows, halo_rows), halo_rows), :]
        high = yhi[pl.ds(pl.multiple_of(k * halo_rows, halo_rows), halo_rows), :]
        data = jnp.concatenate([main, low, high], 0)
        put(pl.ds(pl.multiple_of(k * ROWS, ROWS), ROWS), dot(wy[...], data))

    def first(k, carry):
        forward_y(own[pl.ds(pl.multiple_of(k * own_rows, own_rows), own_rows), :], k)
        return carry

    lax.fori_loop(0, BLOCKS, first, 0, unroll=4)
    forward_y(xlo[...], BLOCKS)
    forward_y(xhi[...], BLOCKS + 1)

    def middle(step, carry):
        base = step * BB
        for i in range(BB):
            plane = take(pl.ds(base + i, EX, stride=EY)).astype(bf16)
            mid[i * EX : (i + 1) * EX, :] = dot(wx[...], plane).astype(bf16)
        for i in range(BB):
            rows = slice(i * EX, (i + 1) * EX)
            along = dot(mid[rows, :], lz[...])
            spectral = (along / (ex[...] + (ez[...] + ey[base + i]))).astype(bf16)
            mid[rows, :] = dot(spectral, lzt[...]).astype(bf16)
        for i in range(BB):
            put(pl.ds(base + i, EX, stride=EY), dot(wxt[...], mid[i * EX : (i + 1) * EX, :]))
        return carry

    lax.fori_loop(0, EY // BB, middle, 0)

    def backward_y(k):
        rows = take(pl.ds(pl.multiple_of(k * ROWS, ROWS), ROWS)).astype(bf16)
        return dot(wyt[...], rows)

    def last(k, carry):
        out = backward_y(k)
        fix[pl.ds(pl.multiple_of(k * own_rows, own_rows), own_rows), :] = out[:own_rows]
        at = pl.ds(pl.multiple_of(k * halo_rows, halo_rows), halo_rows)
        out_ylo[at, :] = out[own_rows : own_rows + halo_rows].astype(bf16)
        out_yhi[at, :] = out[own_rows + halo_rows :].astype(bf16)
        return carry

    lax.fori_loop(0, BLOCKS, last, 0, unroll=4)
    out_xlo[...] = backward_y(BLOCKS).astype(bf16)
    out_xhi[...] = backward_y(BLOCKS + 1).astype(bf16)


VM = pl.BlockSpec(memory_space=pltpu.VMEM)
SM = pl.BlockSpec(memory_space=pltpu.SMEM)


def solve(own, xlo, xhi, ylo, yhi, wy, wx, local_z, eig_x, eig_y, eig_z):
    sds = jax.ShapeDtypeStruct
    return pl.pallas_call(
        solve_kernel,
        out_shape=(
            sds((CX * CY, NZ), f32),
            sds((ROWS, NZ), bf16),
            sds((ROWS, NZ), bf16),
            sds((CX * OV, NZ), bf16),
            sds((CX * OV, NZ), bf16),
        ),
        in_specs=[VM] * 12 + [SM, VM],
        out_specs=(VM,) * 5,
        scratch_shapes=[
            pltpu.VMEM((2, EX * EY, NZ // 2), f32),
            pltpu.VMEM((BB * EX, NZ), bf16),
        ],
        name="solve",
    )(
        own, xlo, xhi, ylo, yhi, wy, wy.T, wx, wx.T, local_z, local_z.T,
        eig_x[:, None], eig_y, eig_z[None, :],
    )


def halo_order(w, overlap):
    inner = w.shape[0] - overlap
    return jnp.concatenate([w[overlap:inner], w[:overlap], w[inner:]], 0)


def y_matrix(local_y):
    eye = jnp.eye(GX, dtype=bf16)
    parts = [
        jnp.einsum("ij,yb->ibjy", eye, part).reshape(ROWS, -1)
        for part in (local_y[OV : EY - OV], local_y[:OV], local_y[EY - OV :])
    ]
    return jnp.concatenate(parts, 1)


def split(x):
    high = x.astype(bf16)
    return high, (x - high.astype(f32)).astype(bf16)


def restrict_kernel(residual, basis, own, acc):
    step = pl.program_id(0)

    @pl.when(step == 0)
    def _():
        acc[...] = jnp.zeros_like(acc)

    rounded = residual[...].astype(bf16)
    own[...] = rounded
    acc[...] += dot(basis[...], rounded)


def restrict(residual, basis):
    steps = 8
    rows = CX * CY // steps
    sds = jax.ShapeDtypeStruct
    return pl.pallas_call(
        restrict_kernel,
        grid=(steps,),
        out_shape=(sds((CX * CY, NZ), bf16), sds((32, NZ), f32)),
        in_specs=[
            pl.BlockSpec((rows, NZ), lambda i: (i, 0)),
            pl.BlockSpec((32, rows), lambda i: (0, i)),
        ],
        out_specs=(
            pl.BlockSpec((rows, NZ), lambda i: (i, 0)),
            pl.BlockSpec((32, NZ), lambda i: (0, 0)),
        ),
        name="restrict",
    )(residual, basis)


def combine_kernel(fix, basis, shape, rxlo, rxhi, rylo, ryhi, out):
    step = pl.program_id(0)
    total = fix[...] + dot(basis[...], shape[...])
    planes = total.reshape(-1, CY, NZ)
    low = rylo[...].astype(f32).reshape(-1, OV, NZ)
    high = ryhi[...].astype(f32).reshape(-1, OV, NZ)
    zeros = jnp.zeros((planes.shape[0], CY - 2 * OV, NZ), f32)
    planes = planes + jnp.concatenate([low, zeros, high], 1)
    out[...] = planes.reshape(-1, NZ)

    @pl.when(step == 0)
    def _():
        out[: GX * CY, :] += rxlo[: GX * CY, :].astype(f32)

    @pl.when(step == pl.num_programs(0) - 1)
    def _():
        out[out.shape[0] - GX * CY :, :] += rxhi[: GX * CY, :].astype(f32)


def combine(fix, basis, shape, rxlo, rxhi, rylo, ryhi):
    steps = 8
    rows = CX * CY // steps
    rim = CX * OV // steps
    whole = lambda i: (0, 0)
    part = lambda i: (i, 0)
    return pl.pallas_call(
        combine_kernel,
        grid=(steps,),
        out_shape=jax.ShapeDtypeStruct((CX * CY, NZ), f32),
        in_specs=[
            pl.BlockSpec((rows, NZ), part),
            pl.BlockSpec((rows, 64), part),
            pl.BlockSpec((64, NZ), whole),
            pl.BlockSpec((ROWS, NZ), whole),
            pl.BlockSpec((ROWS, NZ), whole),
            pl.BlockSpec((rim, NZ), part),
            pl.BlockSpec((rim, NZ), part),
        ],
        out_specs=pl.BlockSpec((rows, NZ), part),
        name="combine",
    )(fix, basis, shape, rxlo, rxhi, rylo, ryhi)


def shift(x, axis, step):
    size = lax.axis_size(axis)
    return lax.ppermute(x, axis, [(i, (i + step) % size) for i in range(size)])


def gather(x, axis):
    size = lax.axis_size(axis)
    return lax.all_to_all(jnp.broadcast_to(x[None], (size,) + x.shape), axis, 0, 0)


def local(
    residual, local_x, local_y, local_z, eig_x, eig_y, eig_z, coarse_x, coarse_y, coarse_z,
    mode_x, mode_y, mode_z, coarse_eig_x, coarse_eig_y, coarse_eig_z,
):
    low_x = residual[:OV].astype(bf16).reshape(OV * CY, NZ)
    high_x = residual[CX - OV :].astype(bf16).reshape(OV * CY, NZ)
    xlo = shift(high_x, "gx", 1)
    xhi = shift(low_x, "gx", -1)

    def rim(lo, hi, at):
        cut = slice(0, OV) if at == 0 else slice(CY - OV, CY)
        own_rim = residual[:, cut].astype(bf16).reshape(CX * OV, NZ)
        parts = [part.reshape(OV, CY, NZ)[:, cut].reshape(OV * OV, NZ) for part in (lo, hi)]
        return jnp.concatenate([own_rim] + parts, 0)

    ylo = shift(rim(xlo, xhi, 1), "gy", 1)
    yhi = shift(rim(xlo, xhi, 0), "gy", -1)

    basis = (
        coarse_x.astype(f32)[:, None, :, None] * coarse_y.astype(f32)[None, :, None, :]
    ).reshape(CX * CY, MODES * MODES)
    basis_high, basis_low = split(basis)
    both = jnp.concatenate([basis_high, basis_low], 1)
    own, acc = restrict(residual.reshape(CX * CY, NZ), both.T)
    own_coarse = jnp.dot(acc[:16] + acc[16:], coarse_z.astype(f32), precision=HI)
    own_coarse = own_coarse.reshape(MODES, MODES, MODES).transpose(1, 0, 2).reshape(MODES, 16)
    modes_xz = jnp.einsum("Ia,pc->Ipac", mode_x, mode_z, precision=HI).reshape(128, 128)
    rows_x = gather(own_coarse, "gx")
    rows_x = rows_x.transpose(1, 0, 2).reshape(MODES, 128)
    part = jnp.dot(rows_x, modes_xz, precision=HI)

    wy = y_matrix(local_y)
    wx = halo_order(local_x, OV).T
    fix, out_xlo, out_xhi, out_ylo, out_yhi = solve(
        own, xlo, xhi, ylo, yhi, wy, wx, local_z, eig_x, eig_y, eig_z
    )

    rxlo = shift(out_xhi, "gx", 1)
    rxhi = shift(out_xlo, "gx", -1)
    edge = GX * CY
    width = GX * OV

    def folded(strip, start):
        rows = slice(start, start + width)
        strip = strip.astype(f32)
        strip = strip.at[:width].add(rxlo[rows].astype(f32))
        strip = strip.at[CX * OV - width :].add(rxhi[rows].astype(f32))
        return strip.astype(bf16)

    rylo = shift(folded(out_yhi, edge + width), "gy", 1)
    ryhi = shift(folded(out_ylo, edge), "gy", -1)

    columns = gather(part, "gy").reshape(128, 128)
    row_index = lax.axis_index("gx")
    col_index = lax.axis_index("gy")
    rows_y = lax.dynamic_slice_in_dim(mode_y, col_index * MODES, MODES, 0)
    eig_xz = (coarse_eig_x[:, None] + coarse_eig_z[None, :]).reshape(1, 128)
    hat = jnp.dot(mode_y.T, columns, precision=HI) / (coarse_eig_y[:, None] + eig_xz)
    rows_xz = lax.dynamic_slice_in_dim(modes_xz, row_index * 16, 16, 0)
    sol = jnp.dot(rows_y, jnp.dot(hat, rows_xz.T, precision=HI), precision=HI)
    sol = sol.reshape(MODES, MODES, MODES).transpose(1, 0, 2).reshape(16, MODES)
    shape = jnp.dot(sol, coarse_z.astype(f32).T, precision=HI)
    shape_high, shape_low = split(shape)
    shape4 = jnp.concatenate([shape_high, shape_low, shape_high, shape_low], 0)
    basis4 = jnp.concatenate([basis_high, basis_high, basis_low, basis_low], 1)

    out = combine(fix, basis4, shape4, rxlo, rxhi, rylo, ryhi)
    return out.reshape(CX, CY, NZ)


def solution(mesh):
    placed = (P("gx", "gy", None),) + (P(),) * 15
    return jax.shard_map(
        local, mesh=mesh, in_specs=placed, out_specs=P("gx", "gy", None), check_vma=False
    )
```

```python
import jax
import jax.numpy as jnp
from jax import lax
from jax.experimental import pallas as pl
from jax.experimental.pallas import tpu as pltpu
from jax.sharding import Mesh, PartitionSpec as P

OV = 4
MODES = 4
CX = 128
CY = 32
NZ = 256
EX = 136
EY = 40
GX = 4
ROWS = GX * EY
OWN = GX * CY
RIM = GX * OV
BLOCKS = CX // GX
CELLS = CX * CY
CHUNKS = 8
HI = lax.Precision.HIGHEST
f32 = jnp.float32
bf16 = jnp.bfloat16
sds = jax.ShapeDtypeStruct

VM = pl.BlockSpec(memory_space=pltpu.VMEM)
SM = pl.BlockSpec(memory_space=pltpu.SMEM)
ANY = pl.BlockSpec(memory_space=pl.ANY)


def dot(a, b):
    return jnp.dot(a, b, preferred_element_type=f32)


def dot_t(a, b):
    return lax.dot_general(a, b, (((1,), (1,)), ((), ())), preferred_element_type=f32)


def dot_hi(a, b):
    return jnp.dot(a, b, preferred_element_type=f32, precision=HI)


def dot_t_hi(a, b):
    dims = (((1,), (1,)), ((), ()))
    return lax.dot_general(a, b, dims, preferred_element_type=f32, precision=HI)


def split(x):
    high = x.astype(bf16)
    return high, (x - high.astype(f32)).astype(bf16)


def iotas(shape):
    return lax.broadcasted_iota(jnp.int32, shape, 0), lax.broadcasted_iota(jnp.int32, shape, 1)


def pick(mask, kind=bf16):
    return jnp.where(mask, 1.0, 0.0).astype(kind)


def call(kernel, name, out_shape, in_specs, mib, out_specs=None, scratch=()):
    if out_specs is None:
        out_specs = jax.tree.map(lambda _: VM, out_shape)
    return pl.pallas_call(
        kernel,
        out_shape=out_shape,
        in_specs=in_specs,
        out_specs=out_specs,
        scratch_shapes=list(scratch),
        compiler_params=pltpu.CompilerParams(vmem_limit_bytes=mib << 20),
        name=name,
    )


def tile(ref, k, rows):
    return ref[pl.ds(pl.multiple_of(k * rows, rows), rows), :]


def selection(cy):
    row, col = iotas((3 * RIM, OWN))
    k, y = iotas((OWN, CY))
    spread = dot(pick((k & 31) == y), cy).astype(bf16)
    row4, n = iotas((3 * RIM, MODES))
    modes = dot_t(pick((row4 & 3) == n), spread)
    plane = ((row >> 2) & 3) == (col >> 5)
    inner = col & 31
    target = jnp.where(row < RIM, row & 3, CY - OV + (row & 3))
    ones = jnp.where(inner == target, 1.0, 0.0)
    value = jnp.where(row < 2 * RIM, ones, modes)
    return jnp.where(plane, value, 0.0).astype(bf16)


def load_kernel(residual, cy, own, first_x, last_x, rim_lo, rim_hi, along_y, sel, buf, sems):
    rows = CELLS // CHUNKS

    def copy(c):
        at = pl.ds(c * rows, rows)
        return pltpu.make_async_copy(residual.at[at, :], buf.at[at, :], sems.at[c])

    for c in range(CHUNKS):
        copy(c).start()
    take = selection(cy[...])
    sel[...] = take
    for c in range(CHUNKS):
        copy(c).wait()
        for b in range(rows // OWN):
            k = c * (rows // OWN) + b
            data = buf[k * OWN : (k + 1) * OWN, :].astype(bf16)
            own[k * OWN : (k + 1) * OWN, :] = data
            if k == 0:
                first_x[...] = data
            if k == BLOCKS - 1:
                last_x[...] = data
            out = dot(take, data)
            at = slice(k * RIM, (k + 1) * RIM)
            rim_lo[at, :] = out[:RIM].astype(bf16)
            rim_hi[at, :] = out[RIM : 2 * RIM].astype(bf16)
            along_y[at, :] = out[2 * RIM :]


def load(residual, coarse_y):
    rim = sds((CX * OV, NZ), bf16)
    return call(
        load_kernel,
        "load",
        (
            sds((CELLS, NZ), bf16), sds((OWN, NZ), bf16), sds((OWN, NZ), bf16), rim, rim,
            sds((CX * MODES, NZ), f32), sds((3 * RIM, OWN), bf16),
        ),
        [ANY, VM],
        16,
        scratch=[pltpu.VMEM((CELLS, NZ), f32), pltpu.SemaphoreType.DMA((CHUNKS,))],
    )(residual, coarse_y)


def corners_kernel(sel, rim_lo, rim_hi, xlo, xhi, down, up):
    down[: CX * OV, :] = rim_lo[...]
    up[: CX * OV, :] = rim_hi[...]
    for i, strip in enumerate((xlo, xhi)):
        out = dot(sel[: 2 * RIM, :], strip[...]).astype(bf16)
        at = slice(CX * OV + i * RIM, CX * OV + (i + 1) * RIM)
        down[at, :] = out[:RIM]
        up[at, :] = out[RIM:]


def corners(sel, rim_lo, rim_hi, xlo, xhi):
    side = sds((EX * OV, NZ), bf16)
    return call(corners_kernel, "corners", (side, side), [VM] * 5, 8)(sel, rim_lo, rim_hi, xlo, xhi)


def prepare_kernel(
    lx, ly, lz, eig_x, cx, cy, mode_x, mode_y, mode_z, ceig_x, ceig_z,
    wy, wyt, wx, wxt, lzt, ex, bx, bxt, spread, modes_xz, mode_yt, ceig_xz,
):
    def cell(k):
        y = jnp.where(k < OWN, OV + (k & 31), jnp.where(k < OWN + RIM, k & 3, EY - OV + (k & 3)))
        plane = jnp.where(k < OWN, k >> 5, ((k - OWN) >> 2) & 3)
        return y, plane

    def mode(j):
        plane = (j >= EY).astype(jnp.int32) + (j >= 2 * EY) + (j >= 3 * EY)
        return j - EY * plane, plane

    k, y = iotas((ROWS, EY))
    by_cell = dot(pick(cell(k)[0] == y), ly[...]).astype(bf16)
    b, j = iotas((EY, ROWS))
    k, col = iotas((ROWS, ROWS))
    value = dot(by_cell, pick(mode(j)[0] == b))
    wyt[...] = jnp.where(cell(k)[1] == mode(col)[1], value, 0.0).astype(bf16)
    j, b = iotas((ROWS, EY))
    value = dot_t(pick(mode(j)[0] == b), by_cell)
    wy[...] = jnp.where(mode(k)[1] == cell(col)[1], value, 0.0).astype(bf16)

    k, x = iotas((EX, EX))
    source = jnp.where(k < CX, k + OV, jnp.where(k < CX + OV, k - CX, k))
    moved = dot(pick(source == x), lx[...]).astype(bf16)
    wxt[...] = moved
    wx[...] = dot_t(pick(k == x), moved).astype(bf16)
    ex[...] = jnp.sum(jnp.where(k == x, eig_x[...], 0.0), axis=1, keepdims=True)
    c, z = iotas((NZ, NZ))
    lzt[...] = dot_t(pick(c == z), lz[...]).astype(bf16)

    row, x = iotas((CX * MODES, CX))
    by_row = dot(pick((row >> 2) == x), cx[...]).astype(bf16)
    m, col = iotas((MODES, 16))
    row, col16 = iotas((CX * MODES, 16))
    value = dot(by_row, pick((col >> 2) == m))
    half = jnp.where((row & 3) == (col16 & 3), value, 0.0).astype(bf16)
    bxt[...] = jnp.concatenate([half, half], 1)
    col, m = iotas((16, MODES))
    value = dot_t(pick((col >> 2) == m), by_row)
    col, row = iotas((16, CX * MODES))
    bx[...] = jnp.where((row & 3) == (col & 3), value, 0.0).astype(bf16)

    k, y = iotas((OWN, CY))
    by_k = dot(pick((k & 31) == y), cy[...]).astype(bf16)
    n, col = iotas((MODES, 4 * RIM))
    value = dot(by_k, pick((col & 3) == n))
    k, col = iotas((OWN, 4 * RIM))
    inner = k & 31
    plane = (k >> 5) == ((col >> 2) & 3)
    target = jnp.where(col < 3 * RIM, col & 3, CY - OV + (col & 3))
    ones = jnp.where(inner == target, 1.0, 0.0)
    value = jnp.where(col < 2 * RIM, value, ones)
    spread[...] = jnp.where(plane, value, 0.0).astype(bf16)

    r, i = iotas((128, 32))
    a, col = iotas((32, 128))
    to_a = pick((col >> 2) == a, f32)
    part_x = dot_hi(dot_hi(pick((r >> 2) == i, f32), mode_x[...]), to_a)
    r, p = iotas((128, MODES))
    c, col = iotas((MODES, 128))
    to_c = pick((col & 3) == c, f32)
    part_z = dot_hi(dot_hi(pick((r & 3) == p, f32), mode_z[...]), to_c)
    modes_xz[...] = part_x * part_z
    mode_yt[...] = mode_y[...].T
    eight_x = jnp.broadcast_to(ceig_x[...], (8, 32))
    eight_z = jnp.broadcast_to(ceig_z[...], (8, MODES))
    ceig_xz[...] = dot_hi(eight_x, to_a) + dot_hi(eight_z, to_c)


def prepare(lx, ly, lz, eig_x, cx, cy, mode_x, mode_y, mode_z, ceig_x, ceig_z):
    return call(
        prepare_kernel,
        "prepare",
        (
            sds((ROWS, ROWS), bf16), sds((ROWS, ROWS), bf16), sds((EX, EX), bf16),
            sds((EX, EX), bf16), sds((NZ, NZ), bf16), sds((EX, 1), f32),
            sds((16, CX * MODES), bf16), sds((CX * MODES, 32), bf16), sds((OWN, 64), bf16),
            sds((128, 128), f32), sds((128, 128), f32), sds((8, 128), f32),
        ),
        [VM] * 11,
        8,
    )(
        lx, ly, lz, eig_x[None, :], cx, cy, mode_x, mode_y, mode_z,
        ceig_x[None, :], ceig_z[None, :],
    )


def solve_kernel(
    own, xlo, xhi, ylo, yhi, wy, wyt, wx, wxt, lz, lzt, ex, ey, ez,
    fix, out_xlo, out_xhi, out_ylo, out_yhi, field, mid,
):
    def put(rows, value):
        field[0, rows, :] = value[:, :128]
        field[1, rows, :] = value[:, 128:]

    def take(rows):
        return jnp.concatenate([field[0, rows, :], field[1, rows, :]], 1)

    def forward_y(main, k):
        data = jnp.concatenate([main, tile(ylo, k, RIM), tile(yhi, k, RIM)], 0)
        put(pl.ds(pl.multiple_of(k * ROWS, ROWS), ROWS), dot(wy[...], data))

    def first(k, carry):
        forward_y(tile(own, k, OWN), k)
        return carry

    lax.fori_loop(0, BLOCKS, first, 0, unroll=4)
    forward_y(xlo[...], BLOCKS)
    forward_y(xhi[...], BLOCKS + 1)

    def mid_rows(b):
        return pl.ds(pl.multiple_of(b * EX, 8), EX)

    def forward_x(b, carry):
        plane = take(pl.ds(b, EX, stride=EY)).astype(bf16)
        mid[mid_rows(b), :] = dot(wx[...], plane)
        return carry

    lax.fori_loop(0, EY, forward_x, 0, unroll=8)

    def both_z(i, carry):
        at = pl.ds(pl.multiple_of(i * 4 * EX, 8), 4 * EX)
        along = dot(mid[at, :].astype(bf16), lz[...])
        parts = []
        for q in range(4):
            scale = ex[...] + (ez[...] + ey[i * 4 + q])
            parts.append((along[q * EX : (q + 1) * EX] / scale))
        spectral = jnp.concatenate(parts, 0).astype(bf16)
        mid[at, :] = dot(spectral, lzt[...])
        return carry

    lax.fori_loop(0, EY // 4, both_z, 0)

    def backward_x(b, carry):
        put(pl.ds(b, EX, stride=EY), dot(wxt[...], mid[mid_rows(b), :].astype(bf16)))
        return carry

    lax.fori_loop(0, EY, backward_x, 0, unroll=8)

    def backward_y(k):
        rows = take(pl.ds(pl.multiple_of(k * ROWS, ROWS), ROWS)).astype(bf16)
        return dot(wyt[...], rows)

    def last(k, carry):
        out = backward_y(k)
        fix[pl.ds(pl.multiple_of(k * OWN, OWN), OWN), :] = out[:OWN]
        at = pl.ds(pl.multiple_of(k * RIM, RIM), RIM)
        out_ylo[at, :] = out[OWN : OWN + RIM].astype(bf16)
        out_yhi[at, :] = out[OWN + RIM :].astype(bf16)
        return carry

    lax.fori_loop(0, BLOCKS, last, 0, unroll=4)
    out_xlo[...] = backward_y(BLOCKS).astype(bf16)
    out_xhi[...] = backward_y(BLOCKS + 1).astype(bf16)


def solve(own, xlo, xhi, ylo, yhi, weights, lz, ey, ez):
    strip = sds((ROWS, NZ), bf16)
    rim = sds((CX * OV, NZ), bf16)
    wy, wyt, wx, wxt, lzt, ex = weights
    return call(
        solve_kernel,
        "solve",
        (sds((CELLS, NZ), f32), strip, strip, rim, rim),
        [VM] * 12 + [SM, VM],
        32,
        scratch=[pltpu.VMEM((2, EX * EY, NZ // 2), f32), pltpu.VMEM((EX * EY, NZ), f32)],
    )(own, xlo, xhi, ylo, yhi, wy, wyt, wx, wxt, lz, lzt, ex, ey, ez[None, :])


def fold_kernel(out_ylo, out_yhi, rxlo, rxhi, down, up):
    end = CX * OV
    for strip, start, out in ((out_ylo, OWN, down), (out_yhi, OWN + RIM, up)):
        rows = slice(start, start + RIM)
        out[...] = strip[...]
        low = strip[:RIM, :].astype(f32) + rxlo[rows, :].astype(f32)
        high = strip[end - RIM :, :].astype(f32) + rxhi[rows, :].astype(f32)
        out[:RIM, :] = low.astype(bf16)
        out[end - RIM :, :] = high.astype(bf16)


def fold(out_ylo, out_yhi, rxlo, rxhi):
    rim = sds((CX * OV, NZ), bf16)
    return call(fold_kernel, "fold", (rim, rim), [VM] * 4, 8)(out_ylo, out_yhi, rxlo, rxhi)


def restrict_kernel(along_y, bx, cz, out):
    high, low = split(along_y[...])
    both = dot(bx[...], high) + dot(bx[...], low)
    own = dot_hi(both, cz[...].astype(f32))
    for i in range(out.shape[0]):
        for m in range(MODES):
            out[i, :, m * MODES : (m + 1) * MODES] = own[m * MODES : (m + 1) * MODES, :]


def coarse_x_kernel(rows, modes_xz, out):
    part = sum(dot_hi(rows[i], modes_xz[16 * i : 16 * i + 16, :]) for i in range(8))
    for i in range(out.shape[0]):
        out[i] = part


def coarse_y_kernel(rows, out):
    for i in range(out.shape[0]):
        for j in range(rows.shape[0]):
            out[i, MODES * j : MODES * (j + 1), :] = rows[j]


def coarse_kernel(place, rows, modes_xz, mode_y, mode_yt, ceig_xz, ceig_y, cz, bxt, out):
    hat = dot_hi(mode_yt[...], rows[...].reshape(128, 128))
    hat = hat / (ceig_y[...] + ceig_xz[:1, :])
    row, col = iotas((8, 128))
    mine = pick(col == place[1] * MODES + row, f32)
    rows_y = dot_hi(mine, mode_y[...])
    rows_xz = modes_xz[pl.ds(pl.multiple_of(place[0] * 16, 16), 16), :]
    sol = dot_t_hi(dot_hi(rows_y, hat), rows_xz)
    levels = cz[...].astype(f32)
    shape = jnp.concatenate(
        [dot_t_hi(sol[:, m * MODES : (m + 1) * MODES], levels)[:MODES] for m in range(MODES)], 0
    )
    high, low = split(shape)
    value = dot(bxt[...], jnp.concatenate([high, low], 0))
    high, low = split(value)
    for k in range(BLOCKS):
        at = slice(k * RIM, (k + 1) * RIM)
        out[2 * k * RIM : (2 * k + 1) * RIM, :] = high[at]
        out[(2 * k + 1) * RIM : (2 * k + 2) * RIM, :] = low[at]


def combine_kernel(fix, spread, shape, rxlo, rxhi, rylo, ryhi, out, buf, sems):
    rows = CELLS // CHUNKS

    def copy(c):
        at = pl.ds(c * rows, rows)
        return pltpu.make_async_copy(buf.at[at, :], out.at[at, :], sems.at[c])

    for c in range(CHUNKS):
        for b in range(rows // OWN):
            k = c * (rows // OWN) + b
            rim = slice(k * RIM, (k + 1) * RIM)
            data = jnp.concatenate(
                [shape[2 * k * RIM : 2 * (k + 1) * RIM, :], rylo[rim, :], ryhi[rim, :]], 0
            )
            total = fix[k * OWN : (k + 1) * OWN, :] + dot(spread[...], data)
            if k == 0:
                total = total + rxlo[:OWN, :].astype(f32)
            if k == BLOCKS - 1:
                total = total + rxhi[:OWN, :].astype(f32)
            buf[k * OWN : (k + 1) * OWN, :] = total
        copy(c).start()
    for c in range(CHUNKS):
        copy(c).wait()


def combine(*args):
    return call(
        combine_kernel,
        "combine",
        sds((CELLS, NZ), f32),
        [VM] * 7,
        16,
        out_specs=ANY,
        scratch=[pltpu.VMEM((CELLS, NZ), f32), pltpu.SemaphoreType.DMA((CHUNKS,))],
    )(*args)


GY = ("gz", "gw")


def shift(x, axis, step):
    size = lax.axis_size(axis)
    return lax.ppermute(x, axis, [(i, (i + step) % size) for i in range(size)])


def exchange(x, axis):
    return lax.all_to_all(x, axis, 0, 0)


def local(
    residual, local_x, local_y, local_z, eig_x, eig_y, eig_z, coarse_x, coarse_y, coarse_z,
    mode_x, mode_y, mode_z, coarse_eig_x, coarse_eig_y, coarse_eig_z,
):
    own, first_x, last_x, rim_lo, rim_hi, along_y, sel = load(
        residual.reshape(CELLS, NZ), coarse_y
    )
    xlo = shift(last_x, "gx", 1)
    xhi = shift(first_x, "gx", -1)
    wy, wyt, wx, wxt, lzt, ex, bx, bxt, spread, modes_xz, mode_yt, ceig_xz = prepare(
        local_x, local_y, local_z, eig_x, coarse_x, coarse_y, mode_x, mode_y, mode_z,
        coarse_eig_x, coarse_eig_z,
    )
    own_coarse = call(
        restrict_kernel, "restrict", sds((8, MODES, 16), f32), [VM] * 3, 8
    )(along_y, bx, coarse_z)
    down, up = corners(sel, rim_lo, rim_hi, xlo, xhi)
    ylo = shift(up, GY, 1)
    yhi = shift(down, GY, -1)

    rows = exchange(own_coarse, "gx")
    rows = call(coarse_x_kernel, "coarse_x", sds((4, MODES, 128), f32), [VM] * 2, 4)(
        rows, modes_xz
    )

    fix, out_xlo, out_xhi, out_ylo, out_yhi = solve(
        own, xlo, xhi, ylo, yhi, (wy, wyt, wx, wxt, lzt, ex), local_z, eig_y, eig_z
    )

    rxlo = shift(out_xhi, "gx", 1)
    rxhi = shift(out_xlo, "gx", -1)
    down, up = fold(out_ylo, out_yhi, rxlo, rxhi)
    rylo = shift(up, GY, 1)
    ryhi = shift(down, GY, -1)

    rows = exchange(rows, "gw")
    rows = call(coarse_y_kernel, "coarse_y", sds((8, 16, 128), f32), [VM], 4)(rows)
    rows = exchange(rows, "gz")
    place = jnp.stack([lax.axis_index("gx"), lax.axis_index(GY)]).astype(jnp.int32)
    shape = call(
        coarse_kernel, "coarse", sds((2 * CX * MODES, NZ), bf16), [SM] + [VM] * 8, 8
    )(place, rows, modes_xz, mode_y, mode_yt, ceig_xz, coarse_eig_y[:, None], coarse_z, bxt)

    out = combine(fix, spread, shape, rxlo, rxhi, rylo, ryhi)
    return out.reshape(CX, CY, NZ)


def solution(mesh):
    fine = Mesh(mesh.devices.reshape(8, 8, 4), ("gx", "gz", "gw"))
    split_y = P("gx", ("gz", "gw"), None)
    return jax.shard_map(
        local, mesh=fine, in_specs=(split_y,) + (P(),) * 15, out_specs=split_y, check_vma=False
    )
```

```python
import jax
import jax.numpy as jnp
from jax import lax
from jax.experimental import pallas as pl
from jax.experimental.pallas import tpu as pltpu
from jax.sharding import PartitionSpec as P

OV = 4
MODES = 4
CX = 128
CY = 32
NZ = 256
EX = 136
EY = 40
GX = 4
ROWS = GX * EY
OWN = GX * CY
RIM = GX * OV
BLOCKS = CX // GX
CELLS = CX * CY
CHUNKS = 8
HI = lax.Precision.HIGHEST
f32 = jnp.float32
bf16 = jnp.bfloat16
sds = jax.ShapeDtypeStruct

VM = pl.BlockSpec(memory_space=pltpu.VMEM)
SM = pl.BlockSpec(memory_space=pltpu.SMEM)
ANY = pl.BlockSpec(memory_space=pl.ANY)
HBM = pl.BlockSpec(memory_space=pltpu.HBM)


def dot(a, b):
    return jnp.dot(a, b, preferred_element_type=f32)


def dot_t(a, b):
    return lax.dot_general(a, b, (((1,), (1,)), ((), ())), preferred_element_type=f32)


def dot_hi(a, b):
    return jnp.dot(a, b, preferred_element_type=f32, precision=HI)


def dot_t_hi(a, b):
    dims = (((1,), (1,)), ((), ()))
    return lax.dot_general(a, b, dims, preferred_element_type=f32, precision=HI)


def split(x):
    high = x.astype(bf16)
    return high, (x - high.astype(f32)).astype(bf16)


def iotas(shape):
    return lax.broadcasted_iota(jnp.int32, shape, 0), lax.broadcasted_iota(jnp.int32, shape, 1)


def pick(mask, kind=bf16):
    return jnp.where(mask, 1.0, 0.0).astype(kind)


def call(kernel, name, out_shape, in_specs, mib, out_specs=None, scratch=()):
    if out_specs is None:
        out_specs = jax.tree.map(lambda _: VM, out_shape)
    return pl.pallas_call(
        kernel,
        out_shape=out_shape,
        in_specs=in_specs,
        out_specs=out_specs,
        scratch_shapes=list(scratch),
        compiler_params=pltpu.CompilerParams(vmem_limit_bytes=mib << 20),
        name=name,
    )


def tile(ref, k, rows):
    return ref[pl.ds(pl.multiple_of(k * rows, rows), rows), :]


def selection(cyt):
    row, col = iotas((3 * RIM, OWN))
    y, k = iotas((CY, OWN))
    spread = dot(cyt, pick((k & 31) == y)).astype(bf16)
    row4, n = iotas((3 * RIM, MODES))
    modes = dot(pick((row4 & 3) == n), spread)
    plane = ((row >> 2) & 3) == (col >> 5)
    inner = col & 31
    target = jnp.where(row < RIM, row & 3, CY - OV + (row & 3))
    ones = jnp.where(inner == target, 1.0, 0.0)
    value = jnp.where(row < 2 * RIM, ones, modes)
    return jnp.where(plane, value, 0.0).astype(bf16)


def load_kernel(residual, cyt, own, first_x, last_x, rim_lo, rim_hi, along_y, sel, buf, sems, cyt_buf, sem):
    rows = CELLS // CHUNKS

    def copy(c):
        at = pl.ds(c * rows, rows)
        return pltpu.make_async_copy(residual.at[at, :], buf.at[at, :], sems.at[c])

    for c in range(CHUNKS):
        copy(c).start()
    small = pltpu.make_async_copy(cyt, cyt_buf, sem)
    small.start()
    small.wait()
    take = selection(cyt_buf[...])
    sel[...] = take
    for c in range(CHUNKS):
        copy(c).wait()
        for b in range(rows // OWN):
            k = c * (rows // OWN) + b
            data = buf[k * OWN : (k + 1) * OWN, :].astype(bf16)
            own[k * OWN : (k + 1) * OWN, :] = data
            if k == 0:
                first_x[...] = data
            if k == BLOCKS - 1:
                last_x[...] = data
            out = dot(take, data)
            at = slice(k * RIM, (k + 1) * RIM)
            rim_lo[at, :] = out[:RIM].astype(bf16)
            rim_hi[at, :] = out[RIM : 2 * RIM].astype(bf16)
            along_y[at, :] = out[2 * RIM :]


def load(residual, coarse_y):
    rim = sds((CX * OV, NZ), bf16)
    return call(
        load_kernel,
        "load",
        (
            sds((CELLS, NZ), bf16), sds((OWN, NZ), bf16), sds((OWN, NZ), bf16), rim, rim,
            sds((CX * MODES, NZ), f32), sds((3 * RIM, OWN), bf16),
        ),
        [HBM, HBM],
        16,
        scratch=[
            pltpu.VMEM((CELLS, NZ), f32), pltpu.SemaphoreType.DMA((CHUNKS,)),
            pltpu.VMEM((MODES, CY), bf16), pltpu.SemaphoreType.DMA,
        ],
    )(residual, coarse_y.T)


def corners_kernel(sel, rim_lo, rim_hi, xlo, xhi, after, down, up):
    down[: CX * OV, :] = rim_lo[...]
    up[: CX * OV, :] = rim_hi[...]
    for i, strip in enumerate((xlo, xhi)):
        out = dot(sel[: 2 * RIM, :], strip[...]).astype(bf16)
        at = slice(CX * OV + i * RIM, CX * OV + (i + 1) * RIM)
        down[at, :] = out[:RIM]
        up[at, :] = out[RIM:]


def corners(*args):
    side = sds((EX * OV, NZ), bf16)
    return call(corners_kernel, "corners", (side, side), [VM] * 5 + [ANY], 8)(*args)


PARAMS = (
    ((EX, EX), bf16), ((EY, EY), bf16), ((NZ, NZ), bf16), ((1, EX), f32), ((1, EY), f32),
    ((1, NZ), f32), ((MODES, CX), bf16), ((MODES, CY), bf16), ((MODES, NZ), bf16),
    ((32, 32), f32), ((128, 128), f32), ((MODES, MODES), f32), ((1, 32), f32), ((1, 128), f32),
    ((1, MODES), f32),
)
WEIGHTS = (
    ((ROWS, ROWS), bf16), ((ROWS, ROWS), bf16), ((OWN, ROWS + 2 * RIM), bf16),
    ((OWN, 2 * RIM), bf16), ((EX, EX), bf16), ((EX, EX), bf16), ((NZ, NZ), bf16),
    ((NZ, NZ), bf16), ((EX, NZ), f32), ((EY, NZ), f32), ((16, CX * MODES), bf16),
    ((CX * MODES, 32), bf16), ((MODES, NZ), f32), ((128, 128), f32), ((128, 128), f32),
    ((128, 128), f32), ((128, 128), f32),
)


def prepare_kernel(*refs):
    n = len(PARAMS)
    sources, outs, bufs, sems = (
        refs[:n], refs[n : n + len(WEIGHTS)], refs[n + len(WEIGHTS) : -1], refs[-1]
    )
    copies = [
        pltpu.make_async_copy(source, buf, sems.at[i])
        for i, (source, buf) in enumerate(zip(sources, bufs))
    ]
    for copy in copies:
        copy.start()
    for copy in copies:
        copy.wait()
    (
        lx, ly, lz, eig_x, eig_y, eig_z, cxt, cyt, czt, mode_x, mode_y, mode_z,
        ceig_x, ceig_y, ceig_z,
    ) = bufs
    (
        wy, wyt, wfin, spread, wx, wxt, lz_out, lzt, exb, eyz, bx, bxt, czf, modes_xz,
        mode_y_out, mode_yt, ceig,
    ) = outs

    def cell(k):
        y = jnp.where(k < OWN, OV + (k & 31), jnp.where(k < OWN + RIM, k & 3, EY - OV + (k & 3)))
        plane = jnp.where(k < OWN, k >> 5, ((k - OWN) >> 2) & 3)
        return y, plane

    def mode(j):
        plane = (j >= EY).astype(jnp.int32) + (j >= 2 * EY) + (j >= 3 * EY)
        return j - EY * plane, plane

    k, y = iotas((ROWS, EY))
    by_cell = dot(pick(cell(k)[0] == y), ly[...]).astype(bf16)
    b, j = iotas((EY, ROWS))
    k, col = iotas((ROWS, ROWS))
    value = dot(by_cell, pick(mode(j)[0] == b))
    value = jnp.where(cell(k)[1] == mode(col)[1], value, 0.0).astype(bf16)
    wyt[...] = value
    j, b = iotas((ROWS, EY))
    back = dot_t(pick(mode(j)[0] == b), by_cell)
    wy[...] = jnp.where(mode(k)[1] == cell(col)[1], back, 0.0).astype(bf16)

    y, k = iotas((CY, OWN))
    by_k = dot(cyt[...], pick((k & 31) == y)).astype(bf16)
    k, own = iotas((OWN, OWN))
    turned = dot_t(pick(k == own), by_k).astype(bf16)
    n, col = iotas((MODES, 2 * RIM))
    coarse = dot(turned, pick((col & 3) == n))
    k, col = iotas((OWN, 2 * RIM))
    inner = k & 31
    plane = (k >> 5) == ((col >> 2) & 3)
    coarse = jnp.where(plane, coarse, 0.0).astype(bf16)
    wfin[...] = jnp.concatenate([value[:OWN], coarse], 1)
    target = jnp.where(col < RIM, col & 3, CY - OV + (col & 3))
    spread[...] = jnp.where(plane, jnp.where(inner == target, 1.0, 0.0), 0.0).astype(bf16)

    k, x = iotas((EX, EX))
    source = jnp.where(k < CX, k + OV, jnp.where(k < CX + OV, k - CX, k))
    moved = dot(pick(source == x), lx[...]).astype(bf16)
    wxt[...] = moved
    wx[...] = dot_t(pick(k == x), moved).astype(bf16)
    column = jnp.sum(jnp.where(k == x, eig_x[...], 0.0), axis=1, keepdims=True)
    exb[...] = jnp.broadcast_to(column, (EX, NZ))
    b, y = iotas((EY, EY))
    column = jnp.sum(jnp.where(b == y, eig_y[...], 0.0), axis=1, keepdims=True)
    eyz[...] = column + eig_z[...]
    c, z = iotas((NZ, NZ))
    lz_out[...] = lz[...]
    lzt[...] = dot_t(pick(c == z), lz[...]).astype(bf16)
    czf[...] = czt[...].astype(f32)

    x, row = iotas((CX, CX * MODES))
    by_row = dot(cxt[...], pick((row >> 2) == x)).astype(bf16)
    col, m = iotas((16, MODES))
    value = dot(pick((col >> 2) == m), by_row)
    col, row = iotas((16, CX * MODES))
    flat = jnp.where((row & 3) == (col & 3), value, 0.0).astype(bf16)
    bx[...] = flat
    col, i = iotas((32, 16))
    twice = dot(pick((col & 15) == i), flat)
    bxt[...] = twice.T.astype(bf16)

    r, i = iotas((128, 32))
    a, col = iotas((32, 128))
    to_a = pick((col >> 2) == a, f32)
    part_x = dot_hi(dot_hi(pick((r >> 2) == i, f32), mode_x[...]), to_a)
    r, p = iotas((128, MODES))
    c, col = iotas((MODES, 128))
    to_c = pick((col & 3) == c, f32)
    part_z = dot_hi(dot_hi(pick((r & 3) == p, f32), mode_z[...]), to_c)
    modes_xz[...] = part_x * part_z
    mode_y_out[...] = mode_y[...]
    mode_yt[...] = mode_y[...].T
    eight_x = jnp.broadcast_to(ceig_x[...], (8, 32))
    eight_z = jnp.broadcast_to(ceig_z[...], (8, MODES))
    row = (dot_hi(eight_x, to_a) + dot_hi(eight_z, to_c))[:1]
    r, b = iotas((128, 128))
    column = jnp.sum(jnp.where(r == b, ceig_y[...], 0.0), axis=1, keepdims=True)
    ceig[...] = column + row


def prepare(*params):
    return call(
        prepare_kernel,
        "prepare",
        tuple(sds(*w) for w in WEIGHTS),
        [HBM] * len(PARAMS),
        8,
        scratch=[pltpu.VMEM(*p) for p in PARAMS] + [pltpu.SemaphoreType.DMA((len(PARAMS),))],
    )(*params)


def solve_kernel(
    own, xlo, xhi, ylo, yhi, wy, wyt, wx, wxt, lz, lzt, exb, eyz, after,
    field, out_xlo, out_xhi, out_ylo, out_yhi, mid,
):
    def put(rows, value):
        field[0, rows, :] = value[:, :128]
        field[1, rows, :] = value[:, 128:]

    def take(rows):
        return jnp.concatenate([field[0, rows, :], field[1, rows, :]], 1)

    def forward_y(main, k):
        data = jnp.concatenate([main, tile(ylo, k, RIM), tile(yhi, k, RIM)], 0)
        put(pl.ds(pl.multiple_of(k * ROWS, ROWS), ROWS), dot(wy[...], data))

    def first(k, carry):
        forward_y(tile(own, k, OWN), k)
        return carry

    lax.fori_loop(0, BLOCKS, first, 0, unroll=4)
    forward_y(xlo[...], BLOCKS)
    forward_y(xhi[...], BLOCKS + 1)

    def mid_rows(b):
        return pl.ds(pl.multiple_of(b * EX, 8), EX)

    def forward_x(b, carry):
        plane = take(pl.ds(b, EX, stride=EY)).astype(bf16)
        mid[mid_rows(b), :] = dot(wx[...], plane)
        return carry

    lax.fori_loop(0, EY, forward_x, 0, unroll=8)

    def both_z(i, carry):
        at = pl.ds(pl.multiple_of(i * 4 * EX, 8), 4 * EX)
        along = dot(mid[at, :].astype(bf16), lz[...])
        parts = []
        for q in range(4):
            scale = exb[...] + eyz[pl.ds(i * 4 + q, 1), :]
            parts.append((along[q * EX : (q + 1) * EX] / scale))
        spectral = jnp.concatenate(parts, 0).astype(bf16)
        mid[at, :] = dot(spectral, lzt[...])
        return carry

    lax.fori_loop(0, EY // 4, both_z, 0)

    def backward_x(b, carry):
        put(pl.ds(b, EX, stride=EY), dot(wxt[...], mid[mid_rows(b), :].astype(bf16)))
        return carry

    lax.fori_loop(0, EY, backward_x, 0, unroll=8)

    def planes(k):
        return take(pl.ds(pl.multiple_of(k * ROWS, ROWS), ROWS)).astype(bf16)

    def last(k, carry):
        out = dot(wyt[OWN:, :], planes(k)).astype(bf16)
        at = pl.ds(pl.multiple_of(k * RIM, RIM), RIM)
        out_ylo[at, :] = out[:RIM]
        out_yhi[at, :] = out[RIM:]
        return carry

    out_xlo[...] = dot(wyt[...], planes(BLOCKS)).astype(bf16)
    out_xhi[...] = dot(wyt[...], planes(BLOCKS + 1)).astype(bf16)
    lax.fori_loop(0, BLOCKS, last, 0, unroll=4)


def solve(*args):
    strip = sds((ROWS, NZ), bf16)
    rim = sds((CX * OV, NZ), bf16)
    return call(
        solve_kernel,
        "solve",
        (sds((2, EX * EY, NZ // 2), f32), strip, strip, rim, rim),
        [VM] * 13 + [ANY],
        16,
        scratch=[pltpu.VMEM((EX * EY, NZ), f32)],
    )(*args)


def fold_kernel(out_ylo, out_yhi, rxlo, rxhi, after, down, up):
    end = CX * OV
    for strip, start, out in ((out_ylo, OWN, down), (out_yhi, OWN + RIM, up)):
        rows = slice(start, start + RIM)
        out[...] = strip[...]
        low = strip[:RIM, :].astype(f32) + rxlo[rows, :].astype(f32)
        high = strip[end - RIM :, :].astype(f32) + rxhi[rows, :].astype(f32)
        out[:RIM, :] = low.astype(bf16)
        out[end - RIM :, :] = high.astype(bf16)


def fold(*args):
    rim = sds((CX * OV, NZ), bf16)
    return call(fold_kernel, "fold", (rim, rim), [VM] * 4 + [ANY], 8)(*args)


def restrict_kernel(along_y, bx, czf, out):
    high, low = split(along_y[...])
    both = dot(bx[...], high) + dot(bx[...], low)
    own = dot_t_hi(both, czf[...])
    flat = jnp.concatenate([own[m * MODES : (m + 1) * MODES] for m in range(MODES)], 1)
    for i in range(out.shape[0]):
        out[i] = flat


def coarse_x_kernel(rows, modes_xz, out):
    part = sum(dot_hi(rows[i], modes_xz[16 * i : 16 * i + 16, :]) for i in range(8))
    for i in range(out.shape[0]):
        out[i] = part


def coarse_kernel(rows, modes_xz, mode_y, mode_yt, ceig, czf, bxt, out):
    columns = jnp.concatenate([rows[j] for j in range(rows.shape[0])], 0)
    hat = dot_hi(mode_yt[...], columns) / ceig[...]
    row, col = iotas((8, 128))
    mine = pick(col == lax.axis_index("gy") * MODES + row, f32)
    rows_y = dot_hi(mine, mode_y[...])
    rows_xz = modes_xz[pl.ds(pl.multiple_of(lax.axis_index("gx") * 16, 16), 16), :]
    sol = dot_t_hi(dot_hi(rows_y, hat), rows_xz)
    shape = jnp.concatenate(
        [dot_hi(sol[:, m * MODES : (m + 1) * MODES], czf[...])[:MODES] for m in range(MODES)], 0
    )
    high, low = split(shape)
    value = dot(bxt[...], jnp.concatenate([high, low], 0))
    high, low = split(value)
    for k in range(BLOCKS):
        at = slice(k * RIM, (k + 1) * RIM)
        out[2 * k * RIM : (2 * k + 1) * RIM, :] = high[at]
        out[(2 * k + 1) * RIM : (2 * k + 2) * RIM, :] = low[at]


def finish_kernel(field, wfin, shape, after, fix):
    def step(k, carry):
        at = pl.ds(pl.multiple_of(k * ROWS, ROWS), ROWS)
        planes = jnp.concatenate([field[0, at, :], field[1, at, :]], 1).astype(bf16)
        data = jnp.concatenate([planes, tile(shape, k, 2 * RIM)], 0)
        fix[pl.ds(pl.multiple_of(k * OWN, OWN), OWN), :] = dot(wfin[...], data)
        return carry

    lax.fori_loop(0, BLOCKS, step, 0, unroll=4)


def combine_kernel(fix, spread, rxlo, rxhi, rylo, ryhi, out, buf, sems):
    rows = CELLS // CHUNKS

    def copy(c):
        at = pl.ds(c * rows, rows)
        return pltpu.make_async_copy(buf.at[at, :], out.at[at, :], sems.at[c])

    for c in range(CHUNKS):
        for b in range(rows // OWN):
            k = c * (rows // OWN) + b
            rim = slice(k * RIM, (k + 1) * RIM)
            data = jnp.concatenate([rylo[rim, :], ryhi[rim, :]], 0)
            total = fix[k * OWN : (k + 1) * OWN, :] + dot(spread[...], data)
            if k == 0:
                total = total + rxlo[:OWN, :].astype(f32)
            if k == BLOCKS - 1:
                total = total + rxhi[:OWN, :].astype(f32)
            buf[k * OWN : (k + 1) * OWN, :] = total
        copy(c).start()
    for c in range(CHUNKS):
        copy(c).wait()


def combine(*args):
    return call(
        combine_kernel,
        "combine",
        sds((CELLS, NZ), f32),
        [VM] * 6,
        16,
        out_specs=HBM,
        scratch=[pltpu.VMEM((CELLS, NZ), f32), pltpu.SemaphoreType.DMA((CHUNKS,))],
    )(*args)


def shift(x, axis, step):
    size = lax.axis_size(axis)
    return lax.ppermute(x, axis, [(i, (i + step) % size) for i in range(size)])


def exchange(x, axis):
    return lax.all_to_all(x, axis, 0, 0)


def local(
    residual, local_x, local_y, local_z, eig_x, eig_y, eig_z, coarse_x, coarse_y, coarse_z,
    mode_x, mode_y, mode_z, coarse_eig_x, coarse_eig_y, coarse_eig_z,
):
    own, first_x, last_x, rim_lo, rim_hi, along_y, sel = load(
        residual.reshape(CELLS, NZ), coarse_y
    )
    xlo = shift(last_x, "gx", 1)
    xhi = shift(first_x, "gx", -1)
    (
        wy, wyt, wfin, spread, wx, wxt, lz, lzt, exb, eyz, bx, bxt, czf, modes_xz,
        mode_y, mode_yt, ceig,
    ) = prepare(
        local_x, local_y, local_z, eig_x[None], eig_y[None], eig_z[None], coarse_x.T, coarse_y.T,
        coarse_z.T, mode_x, mode_y, mode_z, coarse_eig_x[None], coarse_eig_y[None],
        coarse_eig_z[None],
    )
    own_coarse = call(
        restrict_kernel, "restrict", sds((8, MODES, 16), f32), [VM] * 3, 8
    )(along_y, bx, czf)
    rows = exchange(own_coarse, "gx")
    down, up = corners(sel, rim_lo, rim_hi, xlo, xhi, own_coarse)
    ylo = shift(up, "gy", 1)
    yhi = shift(down, "gy", -1)
    part = call(coarse_x_kernel, "coarse_x", sds((32, MODES, 128), f32), [VM] * 2, 4)(
        rows, modes_xz
    )
    rows = exchange(part, "gy")

    field, out_xlo, out_xhi, out_ylo, out_yhi = solve(
        own, xlo, xhi, ylo, yhi, wy, wyt, wx, wxt, lz, lzt, exb, eyz, part
    )

    rxlo = shift(out_xhi, "gx", 1)
    rxhi = shift(out_xlo, "gx", -1)
    shape = call(
        coarse_kernel, "coarse", sds((2 * CX * MODES, NZ), bf16), [VM] * 7, 8
    )(rows, modes_xz, mode_y, mode_yt, ceig, czf, bxt)
    down, up = fold(out_ylo, out_yhi, rxlo, rxhi, shape)
    rylo = shift(up, "gy", 1)
    ryhi = shift(down, "gy", -1)
    fix = call(
        finish_kernel, "finish", sds((CELLS, NZ), f32), [VM] * 3 + [ANY], 16
    )(field, wfin, shape, up)
    out = combine(fix, spread, rxlo, rxhi, rylo, ryhi)
    return out.reshape(CX, CY, NZ)


def solution(mesh):
    placed = (P("gx", "gy", None),) + (P(),) * 15
    return jax.shard_map(
        local, mesh=mesh, in_specs=placed, out_specs=P("gx", "gy", None), check_vma=False
    )
```

```python
import jax
import jax.numpy as jnp
from jax import lax
from jax.experimental import pallas as pl
from jax.experimental.pallas import tpu as pltpu
from jax.sharding import PartitionSpec as P


OV = 4
MODES = 4
CX = 128
CY = 32
NZ = 256
EX = 136
EY = 40
GX = 4
ROWS = GX * EY
OWN = GX * CY
RIM = GX * OV
BLOCKS = CX // GX
CELLS = CX * CY
CHUNKS = 8
HI = lax.Precision.HIGHEST
f32 = jnp.float32
bf16 = jnp.bfloat16
sds = jax.ShapeDtypeStruct

VM = pl.BlockSpec(memory_space=pltpu.VMEM)
SM = pl.BlockSpec(memory_space=pltpu.SMEM)
ANY = pl.BlockSpec(memory_space=pl.ANY)
HBM = pl.BlockSpec(memory_space=pltpu.HBM)


def dot(a, b):
    return jnp.dot(a, b, preferred_element_type=f32)


def dot_t(a, b):
    return lax.dot_general(a, b, (((1,), (1,)), ((), ())), preferred_element_type=f32)


def dot_hi(a, b):
    return jnp.dot(a, b, preferred_element_type=f32, precision=HI)


def dot_t_hi(a, b):
    dims = (((1,), (1,)), ((), ()))
    return lax.dot_general(a, b, dims, preferred_element_type=f32, precision=HI)


def split(x):
    high = x.astype(bf16)
    return high, (x - high.astype(f32)).astype(bf16)


def iotas(shape):
    return lax.broadcasted_iota(jnp.int32, shape, 0), lax.broadcasted_iota(jnp.int32, shape, 1)


def pick(mask, kind=bf16):
    return jnp.where(mask, 1.0, 0.0).astype(kind)


def call(kernel, out_shape, in_specs, mib, out_specs=None, scratch=()):
    if out_specs is None:
        out_specs = jax.tree.map(lambda _: VM, out_shape)
    return pl.pallas_call(
        kernel,
        out_shape=out_shape,
        in_specs=in_specs,
        out_specs=out_specs,
        scratch_shapes=list(scratch),
        compiler_params=pltpu.CompilerParams(vmem_limit_bytes=mib << 20),
    )


def tile(ref, k, rows):
    return ref[pl.ds(pl.multiple_of(k * rows, rows), rows), :]


def selection(cyt):
    row, col = iotas((3 * RIM, OWN))
    y, k = iotas((CY, OWN))
    spread = dot(cyt, pick((k & 31) == y)).astype(bf16)
    row4, n = iotas((3 * RIM, MODES))
    modes = dot(pick((row4 & 3) == n), spread)
    plane = ((row >> 2) & 3) == (col >> 5)
    inner = col & 31
    target = jnp.where(row < RIM, row & 3, CY - OV + (row & 3))
    ones = jnp.where(inner == target, 1.0, 0.0)
    value = jnp.where(row < 2 * RIM, ones, modes)
    return jnp.where(plane, value, 0.0).astype(bf16)


def load_kernel(residual, cyt, own, first_x, last_x, rim_lo, rim_hi, along_y, sel, buf, sems, cyt_buf, sem):
    rows = CELLS // CHUNKS

    def copy(c):
        at = pl.ds(c * rows, rows)
        return pltpu.make_async_copy(residual.at[at, :], buf.at[at, :], sems.at[c])

    for c in range(CHUNKS):
        copy(c).start()
    small = pltpu.make_async_copy(cyt, cyt_buf, sem)
    small.start()
    small.wait()
    take = selection(cyt_buf[...])
    sel[...] = take
    for c in range(CHUNKS):
        copy(c).wait()
        for b in range(rows // OWN):
            k = c * (rows // OWN) + b
            data = buf[k * OWN : (k + 1) * OWN, :].astype(bf16)
            own[k * OWN : (k + 1) * OWN, :] = data
            if k == 0:
                first_x[...] = data
            if k == BLOCKS - 1:
                last_x[...] = data
            out = dot(take, data)
            at = slice(k * RIM, (k + 1) * RIM)
            rim_lo[at, :] = out[:RIM].astype(bf16)
            rim_hi[at, :] = out[RIM : 2 * RIM].astype(bf16)
            along_y[at, :] = out[2 * RIM :]


def load(residual, coarse_y):
    rim = sds((CX * OV, NZ), bf16)
    return call(
        load_kernel,
        (
            sds((CELLS, NZ), bf16), sds((OWN, NZ), bf16), sds((OWN, NZ), bf16), rim, rim,
            sds((CX * MODES, NZ), f32), sds((3 * RIM, OWN), bf16),
        ),
        [HBM, HBM],
        16,
        scratch=[
            pltpu.VMEM((CELLS, NZ), f32), pltpu.SemaphoreType.DMA((CHUNKS,)),
            pltpu.VMEM((MODES, CY), bf16), pltpu.SemaphoreType.DMA,
        ],
    )(residual, coarse_y.T)


def corners_kernel(sel, rim_lo, rim_hi, xlo, xhi, after, down, up):
    down[: CX * OV, :] = rim_lo[...]
    up[: CX * OV, :] = rim_hi[...]
    for i, strip in enumerate((xlo, xhi)):
        out = dot(sel[: 2 * RIM, :], strip[...]).astype(bf16)
        at = slice(CX * OV + i * RIM, CX * OV + (i + 1) * RIM)
        down[at, :] = out[:RIM]
        up[at, :] = out[RIM:]


def corners(*args):
    side = sds((EX * OV, NZ), bf16)
    return call(corners_kernel, (side, side), [VM] * 5 + [ANY], 8)(*args)


PARAMS = (
    ((EX, EX), bf16), ((EY, EY), bf16), ((NZ, NZ), bf16), ((1, EX), f32), ((1, EY), f32),
    ((1, NZ), f32), ((MODES, CY), bf16),
)
WEIGHTS = (
    ((ROWS, ROWS), bf16), ((ROWS, ROWS), bf16), ((OWN, ROWS + 2 * RIM), bf16),
    ((OWN, 2 * RIM), bf16), ((EX, EX), bf16), ((EX, EX), bf16), ((NZ, NZ), bf16),
    ((NZ, NZ), bf16), ((EX, NZ), f32), ((EY, NZ), f32),
)


def basis_x(cxt):
    x, row = iotas((CX, CX * MODES))
    by_row = dot(cxt, pick((row >> 2) == x)).astype(bf16)
    col, m = iotas((16, MODES))
    value = dot(pick((col >> 2) == m), by_row)
    col, row = iotas((16, CX * MODES))
    return jnp.where((row & 3) == (col & 3), value, 0.0).astype(bf16)


def modes_a():
    a, col = iotas((32, 128))
    c, col4 = iotas((MODES, 128))
    return pick((col >> 2) == a, f32), pick((col4 & 3) == c, f32)


def prepare_kernel(*refs):
    n = len(PARAMS)
    sources, outs, bufs, sems = (
        refs[:n], refs[n + 1 : n + 1 + len(WEIGHTS)], refs[n + 1 + len(WEIGHTS) : -1], refs[-1]
    )
    copies = [
        pltpu.make_async_copy(source, buf, sems.at[i])
        for i, (source, buf) in enumerate(zip(sources, bufs))
    ]
    for copy in copies:
        copy.start()
    for copy in copies:
        copy.wait()
    lx, ly, lz, eig_x, eig_y, eig_z, cyt = bufs
    wy, wyt, wfin, spread, wx, wxt, lz_out, lzt, exb, eyz = outs

    def cell(k):
        y = jnp.where(k < OWN, OV + (k & 31), jnp.where(k < OWN + RIM, k & 3, EY - OV + (k & 3)))
        plane = jnp.where(k < OWN, k >> 5, ((k - OWN) >> 2) & 3)
        return y, plane

    def mode(j):
        plane = (j >= EY).astype(jnp.int32) + (j >= 2 * EY) + (j >= 3 * EY)
        return j - EY * plane, plane

    k, y = iotas((ROWS, EY))
    by_cell = dot(pick(cell(k)[0] == y), ly[...]).astype(bf16)
    b, j = iotas((EY, ROWS))
    k, col = iotas((ROWS, ROWS))
    value = dot(by_cell, pick(mode(j)[0] == b))
    value = jnp.where(cell(k)[1] == mode(col)[1], value, 0.0).astype(bf16)
    wyt[...] = value
    j, b = iotas((ROWS, EY))
    back = dot_t(pick(mode(j)[0] == b), by_cell)
    wy[...] = jnp.where(mode(k)[1] == cell(col)[1], back, 0.0).astype(bf16)

    y, k = iotas((CY, OWN))
    by_k = dot(cyt[...], pick((k & 31) == y)).astype(bf16)
    k, own = iotas((OWN, OWN))
    turned = dot_t(pick(k == own), by_k).astype(bf16)
    n, col = iotas((MODES, 2 * RIM))
    coarse = dot(turned, pick((col & 3) == n))
    k, col = iotas((OWN, 2 * RIM))
    inner = k & 31
    plane = (k >> 5) == ((col >> 2) & 3)
    coarse = jnp.where(plane, coarse, 0.0).astype(bf16)
    wfin[...] = jnp.concatenate([value[:OWN], coarse], 1)
    target = jnp.where(col < RIM, col & 3, CY - OV + (col & 3))
    spread[...] = jnp.where(plane, jnp.where(inner == target, 1.0, 0.0), 0.0).astype(bf16)

    k, x = iotas((EX, EX))
    source = jnp.where(k < CX, k + OV, jnp.where(k < CX + OV, k - CX, k))
    moved = dot(pick(source == x), lx[...]).astype(bf16)
    wxt[...] = moved
    wx[...] = dot_t(pick(k == x), moved).astype(bf16)
    column = jnp.sum(jnp.where(k == x, eig_x[...], 0.0), axis=1, keepdims=True)
    exb[...] = jnp.broadcast_to(column, (EX, NZ))
    b, y = iotas((EY, EY))
    column = jnp.sum(jnp.where(b == y, eig_y[...], 0.0), axis=1, keepdims=True)
    eyz[...] = column + eig_z[...]
    c, z = iotas((NZ, NZ))
    lz_out[...] = lz[...]
    lzt[...] = dot_t(pick(c == z), lz[...]).astype(bf16)


def prepare(*params):
    return call(
        prepare_kernel,
        tuple(sds(*w) for w in WEIGHTS),
        [HBM] * len(PARAMS) + [ANY],
        8,
        scratch=[pltpu.VMEM(*p) for p in PARAMS] + [pltpu.SemaphoreType.DMA((len(PARAMS),))],
    )(*params)


def solve_kernel(
    own, xlo, xhi, ylo, yhi, wy, wyt, wx, wxt, lz, lzt, exb, eyz, after,
    kept, out_xlo, out_xhi, out_ylo, out_yhi, field, mid, buf, sems,
):
    def put(rows, value):
        field[0, rows, :] = value[:, :128]
        field[1, rows, :] = value[:, 128:]

    def take(rows):
        return jnp.concatenate([field[0, rows, :], field[1, rows, :]], 1)

    def forward_y(main, k):
        data = jnp.concatenate([main, tile(ylo, k, RIM), tile(yhi, k, RIM)], 0)
        put(pl.ds(pl.multiple_of(k * ROWS, ROWS), ROWS), dot(wy[...], data))

    def first(k, carry):
        forward_y(tile(own, k, OWN), k)
        return carry

    lax.fori_loop(0, BLOCKS, first, 0, unroll=4)
    forward_y(xlo[...], BLOCKS)
    forward_y(xhi[...], BLOCKS + 1)

    def mid_rows(b):
        return pl.ds(pl.multiple_of(b * EX, 8), EX)

    def forward_x(b, carry):
        plane = take(pl.ds(b, EX, stride=EY)).astype(bf16)
        mid[mid_rows(b), :] = dot(wx[...], plane)
        return carry

    lax.fori_loop(0, EY, forward_x, 0, unroll=8)

    def both_z(i, carry):
        at = pl.ds(pl.multiple_of(i * 4 * EX, 8), 4 * EX)
        along = dot(mid[at, :].astype(bf16), lz[...])
        parts = []
        for q in range(4):
            scale = exb[...] + eyz[pl.ds(i * 4 + q, 1), :]
            parts.append((along[q * EX : (q + 1) * EX] / scale))
        spectral = jnp.concatenate(parts, 0).astype(bf16)
        mid[at, :] = dot(spectral, lzt[...])
        return carry

    lax.fori_loop(0, EY // 4, both_z, 0)

    def backward_x(b, carry):
        put(pl.ds(b, EX, stride=EY), dot(wxt[...], mid[mid_rows(b), :].astype(bf16)))
        return carry

    lax.fori_loop(0, EY, backward_x, 0, unroll=8)

    def planes(k):
        return take(pl.ds(pl.multiple_of(k * ROWS, ROWS), ROWS)).astype(bf16)

    out_xlo[...] = dot(wyt[...], planes(BLOCKS)).astype(bf16)
    out_xhi[...] = dot(wyt[...], planes(BLOCKS + 1)).astype(bf16)
    rows = BLOCKS * ROWS // CHUNKS
    per = BLOCKS // CHUNKS

    def copy(c):
        at = pl.ds(pl.multiple_of(c * rows, rows), rows)
        return pltpu.make_async_copy(buf.at[at, :], kept.at[at, :], sems.at[c])

    def last(c, carry):
        for b in range(per):
            k = c * per + b
            data = planes(k)
            buf[pl.ds(pl.multiple_of(k * ROWS, ROWS), ROWS), :] = data
            out = dot(wyt[OWN:, :], data).astype(bf16)
            at = pl.ds(pl.multiple_of(k * RIM, RIM), RIM)
            out_ylo[at, :] = out[:RIM]
            out_yhi[at, :] = out[RIM:]
        copy(c).start()
        return carry

    lax.fori_loop(0, CHUNKS, last, 0)
    for c in range(CHUNKS):
        copy(c).wait()


def solve(*args):
    strip = sds((ROWS, NZ), bf16)
    rim = sds((CX * OV, NZ), bf16)
    return call(
        solve_kernel,
        (sds((BLOCKS * ROWS, NZ), bf16), strip, strip, rim, rim),
        [VM] * 13 + [ANY],
        24,
        out_specs=(ANY, VM, VM, VM, VM),
        scratch=[
            pltpu.VMEM((2, EX * EY, NZ // 2), f32), pltpu.VMEM((EX * EY, NZ), f32),
            pltpu.VMEM((BLOCKS * ROWS, NZ), bf16), pltpu.SemaphoreType.DMA((CHUNKS,)),
        ],
    )(*args)


def fold_kernel(out_ylo, out_yhi, rxlo, rxhi, after, down, up):
    end = CX * OV
    for strip, start, out in ((out_ylo, OWN, down), (out_yhi, OWN + RIM, up)):
        rows = slice(start, start + RIM)
        out[...] = strip[...]
        low = strip[:RIM, :].astype(f32) + rxlo[rows, :].astype(f32)
        high = strip[end - RIM :, :].astype(f32) + rxhi[rows, :].astype(f32)
        out[:RIM, :] = low.astype(bf16)
        out[end - RIM :, :] = high.astype(bf16)


def fold(*args):
    rim = sds((CX * OV, NZ), bf16)
    return call(fold_kernel, (rim, rim), [VM] * 4 + [ANY], 8)(*args)


def restrict_kernel(along_y, cxt, czt, mode_x, mode_z, out, modes_xz):
    bx = basis_x(cxt[...])
    high, low = split(along_y[...])
    both = dot(bx, high) + dot(bx, low)
    own = dot_t_hi(both, czt[...].astype(f32))
    flat = jnp.concatenate([own[m * MODES : (m + 1) * MODES] for m in range(MODES)], 1)
    for i in range(out.shape[0]):
        out[i] = flat
    to_a, to_c = modes_a()
    r, i = iotas((128, 32))
    part_x = dot_hi(dot_hi(pick((r >> 2) == i, f32), mode_x[...]), to_a)
    r, p = iotas((128, MODES))
    part_z = dot_hi(dot_hi(pick((r & 3) == p, f32), mode_z[...]), to_c)
    modes_xz[...] = part_x * part_z


def coarse_x_kernel(rows, modes_xz, out):
    part = sum(dot_hi(rows[i], modes_xz[16 * i : 16 * i + 16, :]) for i in range(8))
    for i in range(out.shape[0]):
        out[i] = part


def coarse_kernel(rows, modes_xz, mode_y, ceig_x, ceig_y, ceig_z, cxt, czt, out):
    to_a, to_c = modes_a()
    eight_x = jnp.broadcast_to(ceig_x[...], (8, 32))
    eight_z = jnp.broadcast_to(ceig_z[...], (8, MODES))
    row = (dot_hi(eight_x, to_a) + dot_hi(eight_z, to_c))[:1]
    r, b = iotas((128, 128))
    column = jnp.sum(jnp.where(r == b, ceig_y[...], 0.0), axis=1, keepdims=True)
    columns = jnp.concatenate([rows[j] for j in range(rows.shape[0])], 0)
    hat = dot_hi(mode_y[...].T, columns) / (column + row)
    row, col = iotas((8, 128))
    mine = pick(col == lax.axis_index("gy") * MODES + row, f32)
    rows_y = dot_hi(mine, mode_y[...])
    rows_xz = modes_xz[pl.ds(pl.multiple_of(lax.axis_index("gx") * 16, 16), 16), :]
    sol = dot_t_hi(dot_hi(rows_y, hat), rows_xz)
    levels = czt[...].astype(f32)
    shape = jnp.concatenate(
        [dot_hi(sol[:, m * MODES : (m + 1) * MODES], levels)[:MODES] for m in range(MODES)], 0
    )
    high, low = split(shape)
    col, i = iotas((32, 16))
    twice = dot(pick((col & 15) == i), basis_x(cxt[...]))
    value = dot(twice.T.astype(bf16), jnp.concatenate([high, low], 0))
    high, low = split(value)
    for k in range(BLOCKS):
        at = slice(k * RIM, (k + 1) * RIM)
        out[2 * k * RIM : (2 * k + 1) * RIM, :] = high[at]
        out[(2 * k + 1) * RIM : (2 * k + 2) * RIM, :] = low[at]


def finish_kernel(field, wfin, shape, after, fix, buf, sems):
    rows = BLOCKS * ROWS // CHUNKS
    per = BLOCKS // CHUNKS

    def copy(c):
        at = pl.ds(pl.multiple_of(c * rows, rows), rows)
        return pltpu.make_async_copy(field.at[at, :], buf.at[at, :], sems.at[c])

    for c in range(CHUNKS):
        copy(c).start()

    def step(c, carry):
        copy(c).wait()
        for b in range(per):
            k = c * per + b
            data = jnp.concatenate([tile(buf, k, ROWS), tile(shape, k, 2 * RIM)], 0)
            fix[pl.ds(pl.multiple_of(k * OWN, OWN), OWN), :] = dot(wfin[...], data)
        return carry

    lax.fori_loop(0, CHUNKS, step, 0)


def combine_kernel(fix, spread, rxlo, rxhi, rylo, ryhi, out, buf, sems):
    rows = CELLS // CHUNKS

    def copy(c):
        at = pl.ds(c * rows, rows)
        return pltpu.make_async_copy(buf.at[at, :], out.at[at, :], sems.at[c])

    for c in range(CHUNKS):
        for b in range(rows // OWN):
            k = c * (rows // OWN) + b
            rim = slice(k * RIM, (k + 1) * RIM)
            data = jnp.concatenate([rylo[rim, :], ryhi[rim, :]], 0)
            total = fix[k * OWN : (k + 1) * OWN, :] + dot(spread[...], data)
            if k == 0:
                total = total + rxlo[:OWN, :].astype(f32)
            if k == BLOCKS - 1:
                total = total + rxhi[:OWN, :].astype(f32)
            buf[k * OWN : (k + 1) * OWN, :] = total
        copy(c).start()
    for c in range(CHUNKS):
        copy(c).wait()


def combine(*args):
    return call(
        combine_kernel,
        sds((CELLS, NZ), f32),
        [VM] * 6,
        16,
        out_specs=HBM,
        scratch=[pltpu.VMEM((CELLS, NZ), f32), pltpu.SemaphoreType.DMA((CHUNKS,))],
    )(*args)


def shift(x, axis, step):
    size = lax.axis_size(axis)
    return lax.ppermute(x, axis, [(i, (i + step) % size) for i in range(size)])


def exchange(x, axis):
    return lax.all_to_all(x, axis, 0, 0)


def local(
    residual, local_x, local_y, local_z, eig_x, eig_y, eig_z, coarse_x, coarse_y, coarse_z,
    mode_x, mode_y, mode_z, coarse_eig_x, coarse_eig_y, coarse_eig_z,
):
    own, first_x, last_x, rim_lo, rim_hi, along_y, sel = load(
        residual.reshape(CELLS, NZ), coarse_y
    )
    xlo = shift(last_x, "gx", 1)
    xhi = shift(first_x, "gx", -1)
    own_coarse, modes_xz = call(
        restrict_kernel, (sds((8, MODES, 16), f32), sds((128, 128), f32)), [VM] * 5, 8
    )(along_y, coarse_x.T, coarse_z.T, mode_x, mode_z)
    rows = exchange(own_coarse, "gx")
    down, up = corners(sel, rim_lo, rim_hi, xlo, xhi, own_coarse)
    ylo = shift(up, "gy", 1)
    yhi = shift(down, "gy", -1)
    part = call(coarse_x_kernel, sds((32, MODES, 128), f32), [VM] * 2, 4)(rows, modes_xz)
    rows = exchange(part, "gy")

    wy, wyt, wfin, spread, wx, wxt, lz, lzt, exb, eyz = prepare(
        local_x, local_y, local_z, eig_x[None], eig_y[None], eig_z[None], coarse_y.T, part
    )
    field, out_xlo, out_xhi, out_ylo, out_yhi = solve(
        own, xlo, xhi, ylo, yhi, wy, wyt, wx, wxt, lz, lzt, exb, eyz, part
    )

    rxlo = shift(out_xhi, "gx", 1)
    rxhi = shift(out_xlo, "gx", -1)
    shape = call(coarse_kernel, sds((2 * CX * MODES, NZ), bf16), [VM] * 8, 8)(
        rows, modes_xz, mode_y, coarse_eig_x[None], coarse_eig_y[None], coarse_eig_z[None],
        coarse_x.T, coarse_z.T,
    )
    down, up = fold(out_ylo, out_yhi, rxlo, rxhi, shape)
    rylo = shift(up, "gy", 1)
    ryhi = shift(down, "gy", -1)
    fix = call(
        finish_kernel, sds((CELLS, NZ), f32), [ANY] + [VM] * 2 + [ANY], 16,
        scratch=[pltpu.VMEM((BLOCKS * ROWS, NZ), bf16), pltpu.SemaphoreType.DMA((CHUNKS,))],
    )(field, wfin, shape, up)
    out = combine(fix, spread, rxlo, rxhi, rylo, ryhi)
    return out.reshape(CX, CY, NZ)


def solution(mesh):
    placed = (P("gx", "gy", None),) + (P(),) * 15

    return jax.shard_map(
        local, mesh=mesh, in_specs=placed, out_specs=P("gx", "gy", None), check_vma=False
    )
```

```python
import jax
import jax.numpy as jnp
from jax import lax
from jax.experimental import pallas as pl
from jax.experimental.pallas import tpu as pltpu
from jax.sharding import Mesh, PartitionSpec as P


OV = 4
MODES = 4
CX = 128
CY = 32
NZ = 256
EX = 136
EY = 40
GX = 4
ROWS = GX * EY
OWN = GX * CY
RIM = GX * OV
BLOCKS = CX // GX
CELLS = CX * CY
CHUNKS = 8
WIDE_LOAD = 50
WIDE_SOLVE = 48
HI = lax.Precision.HIGHEST
f32 = jnp.float32
bf16 = jnp.bfloat16
sds = jax.ShapeDtypeStruct

VM = pl.BlockSpec(memory_space=pltpu.VMEM)
SM = pl.BlockSpec(memory_space=pltpu.SMEM)
ANY = pl.BlockSpec(memory_space=pl.ANY)
HBM = pl.BlockSpec(memory_space=pltpu.HBM)


def dot(a, b):
    return jnp.dot(a, b, preferred_element_type=f32)


def dot_t(a, b):
    return lax.dot_general(a, b, (((1,), (1,)), ((), ())), preferred_element_type=f32)


def dot_hi(a, b):
    return jnp.dot(a, b, preferred_element_type=f32, precision=HI)


def dot_t_hi(a, b):
    dims = (((1,), (1,)), ((), ()))
    return lax.dot_general(a, b, dims, preferred_element_type=f32, precision=HI)


def split(x):
    high = x.astype(bf16)
    return high, (x - high.astype(f32)).astype(bf16)


def iotas(shape):
    return lax.broadcasted_iota(jnp.int32, shape, 0), lax.broadcasted_iota(jnp.int32, shape, 1)


def pick(mask, kind=bf16):
    return jnp.where(mask, 1.0, 0.0).astype(kind)


def call(kernel, out_shape, in_specs, mib, out_specs=None, scratch=()):
    if out_specs is None:
        out_specs = jax.tree.map(lambda _: VM, out_shape)
    return pl.pallas_call(
        kernel,
        out_shape=out_shape,
        in_specs=in_specs,
        out_specs=out_specs,
        scratch_shapes=list(scratch),
        compiler_params=pltpu.CompilerParams(vmem_limit_bytes=mib << 20),
    )


def tile(ref, k, rows):
    return ref[pl.ds(pl.multiple_of(k * rows, rows), rows), :]


def selection(cyt):
    row, col = iotas((3 * RIM, OWN))
    y, k = iotas((CY, OWN))
    spread = dot(cyt, pick((k & 31) == y)).astype(bf16)
    row4, n = iotas((3 * RIM, MODES))
    modes = dot(pick((row4 & 3) == n), spread)
    plane = ((row >> 2) & 3) == (col >> 5)
    inner = col & 31
    target = jnp.where(row < RIM, row & 3, CY - OV + (row & 3))
    ones = jnp.where(inner == target, 1.0, 0.0)
    value = jnp.where(row < 2 * RIM, ones, modes)
    return jnp.where(plane, value, 0.0).astype(bf16)


def load_kernel(
    residual, cyt, first_x, last_x, rim_lo, rim_hi, along_y, sel, buf, sems, cyt_buf, sem
):
    rows = CELLS // CHUNKS

    def copy(c):
        at = pl.ds(c * rows, rows)
        return pltpu.make_async_copy(residual.at[at, :], buf.at[at, :], sems.at[c])

    for c in range(CHUNKS):
        copy(c).start()
    small = pltpu.make_async_copy(cyt, cyt_buf, sem)
    small.start()
    small.wait()
    take = selection(cyt_buf[...])
    sel[...] = take
    for c in range(CHUNKS):
        copy(c).wait()
        for b in range(rows // OWN):
            k = c * (rows // OWN) + b
            data = buf[k * OWN : (k + 1) * OWN, :].astype(bf16)
            if k == 0:
                first_x[...] = data
            if k == BLOCKS - 1:
                last_x[...] = data
            out = dot(take, data)
            at = slice(k * RIM, (k + 1) * RIM)
            rim_lo[at, :] = out[:RIM].astype(bf16)
            rim_hi[at, :] = out[RIM : 2 * RIM].astype(bf16)
            along_y[at, :] = out[2 * RIM :]


def load(residual, coarse_y):
    rim = sds((CX * OV, NZ), bf16)
    return call(
        load_kernel,
        (
            sds((OWN, NZ), bf16), sds((OWN, NZ), bf16), rim, rim,
            sds((CX * MODES, NZ), f32), sds((3 * RIM, OWN), bf16),
        ),
        [HBM, HBM],
        WIDE_LOAD,
        scratch=[
            pltpu.VMEM((CELLS, NZ), f32), pltpu.SemaphoreType.DMA((CHUNKS,)),
            pltpu.VMEM((MODES, CY), bf16), pltpu.SemaphoreType.DMA,
        ],
    )(residual, coarse_y.T)


def corners_kernel(sel, rim_lo, rim_hi, xlo, xhi, after, down, up):
    down[: CX * OV, :] = rim_lo[...]
    up[: CX * OV, :] = rim_hi[...]
    for i, strip in enumerate((xlo, xhi)):
        out = dot(sel[: 2 * RIM, :], strip[...]).astype(bf16)
        at = slice(CX * OV + i * RIM, CX * OV + (i + 1) * RIM)
        down[at, :] = out[:RIM]
        up[at, :] = out[RIM:]


def corners(*args):
    side = sds((EX * OV, NZ), bf16)
    return call(corners_kernel, (side, side), [VM] * 5 + [ANY], 8)(*args)


PARAMS = (
    ((EX, EX), bf16), ((EY, EY), bf16), ((NZ, NZ), bf16), ((1, EX), f32), ((1, EY), f32),
    ((1, NZ), f32), ((MODES, CY), bf16),
)
WEIGHTS = (
    ((ROWS, ROWS), bf16), ((ROWS, ROWS), bf16), ((OWN, 4 * RIM), bf16), ((EX, EX), bf16),
    ((EX, EX), bf16), ((NZ, NZ), bf16), ((NZ, NZ), bf16), ((EX, NZ), f32), ((EY, NZ), f32),
)


def basis_x(cxt):
    x, row = iotas((CX, CX * MODES))
    by_row = dot(cxt, pick((row >> 2) == x)).astype(bf16)
    col, m = iotas((16, MODES))
    value = dot(pick((col >> 2) == m), by_row)
    col, row = iotas((16, CX * MODES))
    return jnp.where((row & 3) == (col & 3), value, 0.0).astype(bf16)


def modes_a():
    a, col = iotas((32, 128))
    c, col4 = iotas((MODES, 128))
    return pick((col >> 2) == a, f32), pick((col4 & 3) == c, f32)


def prepare_kernel(*refs):
    n = len(PARAMS)
    sources, outs, bufs, sems = (
        refs[:n], refs[n + 1 : n + 1 + len(WEIGHTS)], refs[n + 1 + len(WEIGHTS) : -1], refs[-1]
    )
    copies = [
        pltpu.make_async_copy(source, buf, sems.at[i])
        for i, (source, buf) in enumerate(zip(sources, bufs))
    ]
    for copy in copies:
        copy.start()
    for copy in copies:
        copy.wait()
    lx, ly, lz, eig_x, eig_y, eig_z, cyt = bufs
    wy, wyt, spread, wx, wxt, lz_out, lzt, exb, eyz = outs

    def cell(k):
        y = jnp.where(k < OWN, OV + (k & 31), jnp.where(k < OWN + RIM, k & 3, EY - OV + (k & 3)))
        plane = jnp.where(k < OWN, k >> 5, ((k - OWN) >> 2) & 3)
        return y, plane

    def mode(j):
        plane = (j >= EY).astype(jnp.int32) + (j >= 2 * EY) + (j >= 3 * EY)
        return j - EY * plane, plane

    k, y = iotas((ROWS, EY))
    by_cell = dot(pick(cell(k)[0] == y), ly[...]).astype(bf16)
    b, j = iotas((EY, ROWS))
    k, col = iotas((ROWS, ROWS))
    value = dot(by_cell, pick(mode(j)[0] == b))
    value = jnp.where(cell(k)[1] == mode(col)[1], value, 0.0).astype(bf16)
    wyt[...] = value
    j, b = iotas((ROWS, EY))
    back = dot_t(pick(mode(j)[0] == b), by_cell)
    wy[...] = jnp.where(mode(k)[1] == cell(col)[1], back, 0.0).astype(bf16)

    y, k = iotas((CY, OWN))
    by_k = dot(cyt[...], pick((k & 31) == y)).astype(bf16)
    k, own = iotas((OWN, OWN))
    turned = dot_t(pick(k == own), by_k).astype(bf16)
    n, col = iotas((MODES, 2 * RIM))
    coarse = dot(turned, pick((col & 3) == n))
    k, col = iotas((OWN, 2 * RIM))
    inner = k & 31
    plane = (k >> 5) == ((col >> 2) & 3)
    coarse = jnp.where(plane, coarse, 0.0)
    target = jnp.where(col < RIM, col & 3, CY - OV + (col & 3))
    rims = jnp.where(plane, jnp.where(inner == target, 1.0, 0.0), 0.0)
    spread[...] = jnp.concatenate([coarse, rims], 1).astype(bf16)

    k, x = iotas((EX, EX))
    source = jnp.where(k < CX, k + OV, jnp.where(k < CX + OV, k - CX, k))
    moved = dot(pick(source == x), lx[...]).astype(bf16)
    wxt[...] = moved
    wx[...] = dot_t(pick(k == x), moved).astype(bf16)
    column = jnp.sum(jnp.where(k == x, eig_x[...], 0.0), axis=1, keepdims=True)
    exb[...] = jnp.broadcast_to(column, (EX, NZ))
    b, y = iotas((EY, EY))
    column = jnp.sum(jnp.where(b == y, eig_y[...], 0.0), axis=1, keepdims=True)
    eyz[...] = column + eig_z[...]
    c, z = iotas((NZ, NZ))
    lz_out[...] = lz[...]
    lzt[...] = dot_t(pick(c == z), lz[...]).astype(bf16)


def prepare(*params):
    return call(
        prepare_kernel,
        tuple(sds(*w) for w in WEIGHTS),
        [HBM] * len(PARAMS) + [ANY],
        8,
        scratch=[pltpu.VMEM(*p) for p in PARAMS] + [pltpu.SemaphoreType.DMA((len(PARAMS),))],
    )(*params)


def solve_kernel(
    residual, xlo, xhi, ylo, yhi, wy, wyt, wx, wxt, lz, lzt, exb, eyz, after,
    kept, out_xlo, out_xhi, out_ylo, out_yhi, field, mid, spec, buf, sems,
):
    def put(rows, value):
        field[0, rows, :] = value[:, :128]
        field[1, rows, :] = value[:, 128:]

    def take(rows):
        return jnp.concatenate([field[0, rows, :], field[1, rows, :]], 1)

    def forward_y(main, k):
        data = jnp.concatenate([main, tile(ylo, k, RIM), tile(yhi, k, RIM)], 0)
        put(pl.ds(pl.multiple_of(k * ROWS, ROWS), ROWS), dot(wy[...], data))

    rows = CELLS // CHUNKS
    per = BLOCKS // CHUNKS

    def copy(c):
        at = pl.ds(pl.multiple_of(c * rows, rows), rows)
        return pltpu.make_async_copy(residual.at[at, :], buf.at[at, :], sems.at[c])

    for c in range(CHUNKS):
        copy(c).start()

    def first(c, carry):
        for i in range(2):
            copy(2 * c + i).wait()
        for b in range(2 * per):
            k = c * 2 * per + b
            forward_y(tile(buf, k, OWN).astype(bf16), k)
        return carry

    lax.fori_loop(0, CHUNKS // 2, first, 0)
    forward_y(xlo[...], BLOCKS)
    forward_y(xhi[...], BLOCKS + 1)

    def mid_rows(b):
        return pl.ds(pl.multiple_of(b * EX, 8), EX)

    def forward_x(b, carry):
        plane = take(pl.ds(b, EX, stride=EY)).astype(bf16)
        mid[mid_rows(b), :] = dot(wx[...], plane)
        return carry

    lax.fori_loop(0, EY, forward_x, 0, unroll=20)

    def forward_z(i, carry):
        at = pl.ds(pl.multiple_of(i * 4 * EX, 16), 4 * EX)
        along = dot(mid[at, :].astype(bf16), lz[...])
        parts = []
        for q in range(4):
            scale = exb[...] + eyz[pl.ds(i * 4 + q, 1), :]
            parts.append((along[q * EX : (q + 1) * EX] / scale))
        spec[at, :] = jnp.concatenate(parts, 0).astype(bf16)
        return carry

    lax.fori_loop(0, EY // 4, forward_z, 0, unroll=5)

    def backward_z(i, carry):
        at = pl.ds(pl.multiple_of(i * 4 * EX, 16), 4 * EX)
        mid[at, :] = dot(spec[at, :], lzt[...])
        return carry

    lax.fori_loop(0, EY // 4, backward_z, 0, unroll=5)

    def backward_x(b, carry):
        put(pl.ds(b, EX, stride=EY), dot(wxt[...], mid[mid_rows(b), :].astype(bf16)))
        return carry

    lax.fori_loop(0, EY, backward_x, 0, unroll=20)

    def planes(k):
        return take(pl.ds(pl.multiple_of(k * ROWS, ROWS), ROWS)).astype(bf16)

    out_xlo[...] = dot(wyt[...], planes(BLOCKS)).astype(bf16)
    out_xhi[...] = dot(wyt[...], planes(BLOCKS + 1)).astype(bf16)

    def last(k, carry):
        data = planes(k)
        kept[pl.ds(pl.multiple_of(k * ROWS, ROWS), ROWS), :] = data
        out = dot(wyt[OWN:, :], data).astype(bf16)
        at = pl.ds(pl.multiple_of(k * RIM, RIM), RIM)
        out_ylo[at, :] = out[:RIM]
        out_yhi[at, :] = out[RIM:]
        return carry

    lax.fori_loop(0, BLOCKS, last, 0, unroll=8)


def solve(*args):
    strip = sds((ROWS, NZ), bf16)
    rim = sds((CX * OV, NZ), bf16)
    return call(
        solve_kernel,
        (sds((BLOCKS * ROWS, NZ), bf16), strip, strip, rim, rim),
        [HBM] + [VM] * 12 + [ANY],
        WIDE_SOLVE,
        scratch=[
            pltpu.VMEM((2, EX * EY, NZ // 2), f32), pltpu.VMEM((EX * EY, NZ), f32),
            pltpu.VMEM((EX * EY, NZ), bf16), pltpu.VMEM((CELLS, NZ), f32),
            pltpu.SemaphoreType.DMA((CHUNKS,)),
        ],
    )(*args)


def fold_kernel(out_ylo, out_yhi, rxlo, rxhi, after, down, up):
    end = CX * OV
    for strip, start, out in ((out_ylo, OWN, down), (out_yhi, OWN + RIM, up)):
        rows = slice(start, start + RIM)
        out[...] = strip[...]
        low = strip[:RIM, :].astype(f32) + rxlo[rows, :].astype(f32)
        high = strip[end - RIM :, :].astype(f32) + rxhi[rows, :].astype(f32)
        out[:RIM, :] = low.astype(bf16)
        out[end - RIM :, :] = high.astype(bf16)


def fold(*args):
    rim = sds((CX * OV, NZ), bf16)
    return call(fold_kernel, (rim, rim), [VM] * 4 + [ANY], 8)(*args)


def restrict_kernel(along_y, cxt, czt, mode_x, mode_z, out, modes_xz):
    bx = basis_x(cxt[...])
    high, low = split(along_y[...])
    both = dot(bx, high) + dot(bx, low)
    own = dot_t_hi(both, czt[...].astype(f32))
    flat = jnp.concatenate([own[m * MODES : (m + 1) * MODES] for m in range(MODES)], 1)
    for i in range(out.shape[0]):
        out[i] = flat
    to_a, to_c = modes_a()
    r, i = iotas((128, 32))
    part_x = dot_hi(dot_hi(pick((r >> 2) == i, f32), mode_x[...]), to_a)
    r, p = iotas((128, MODES))
    part_z = dot_hi(dot_hi(pick((r & 3) == p, f32), mode_z[...]), to_c)
    modes_xz[...] = part_x * part_z


def coarse_x_kernel(rows, modes_xz, out):
    part = sum(dot_hi(rows[i], modes_xz[16 * i : 16 * i + 16, :]) for i in range(8))
    for i in range(out.shape[0]):
        out[i] = part


def coarse_y_kernel(rows, after, out):
    both = jnp.concatenate([rows[j] for j in range(rows.shape[0])], 0)
    for i in range(out.shape[0]):
        out[i] = both


def coarse_kernel(rows, modes_xz, mode_y, ceig_x, ceig_y, ceig_z, cxt, czt, out):
    to_a, to_c = modes_a()
    eight_x = jnp.broadcast_to(ceig_x[...], (8, 32))
    eight_z = jnp.broadcast_to(ceig_z[...], (8, MODES))
    row = (dot_hi(eight_x, to_a) + dot_hi(eight_z, to_c))[:1]
    r, b = iotas((128, 128))
    column = jnp.sum(jnp.where(r == b, ceig_y[...], 0.0), axis=1, keepdims=True)
    columns = rows[...].reshape(128, 128)
    hat = dot_hi(mode_y[...].T, columns) / (column + row)
    row, col = iotas((8, 128))
    place_y = lax.axis_index("gz") * 4 + lax.axis_index("gw")
    mine = pick(col == place_y * MODES + row, f32)
    rows_y = dot_hi(mine, mode_y[...])
    rows_xz = modes_xz[pl.ds(pl.multiple_of(lax.axis_index("gx") * 16, 16), 16), :]
    sol = dot_t_hi(dot_hi(rows_y, hat), rows_xz)
    levels = czt[...].astype(f32)
    shape = jnp.concatenate(
        [dot_hi(sol[:, m * MODES : (m + 1) * MODES], levels)[:MODES] for m in range(MODES)], 0
    )
    high, low = split(shape)
    col, i = iotas((32, 16))
    twice = dot(pick((col & 15) == i), basis_x(cxt[...]))
    value = dot(twice.T.astype(bf16), jnp.concatenate([high, low], 0))
    high, low = split(value)
    for k in range(BLOCKS):
        at = slice(k * RIM, (k + 1) * RIM)
        out[2 * k * RIM : (2 * k + 1) * RIM, :] = high[at]
        out[(2 * k + 1) * RIM : (2 * k + 2) * RIM, :] = low[at]


def finish_kernel(field, wyt, fix):
    def step(k, carry):
        planes = tile(field, k, ROWS)
        fix[pl.ds(pl.multiple_of(k * OWN, OWN), OWN), :] = dot(wyt[:OWN, :], planes)
        return carry

    lax.fori_loop(0, BLOCKS, step, 0, unroll=8)


def combine_kernel(fix, spread, shape, rxlo, rxhi, rylo, ryhi, out, buf, sems):
    rows = CELLS // CHUNKS

    def copy(c):
        at = pl.ds(c * rows, rows)
        return pltpu.make_async_copy(buf.at[at, :], out.at[at, :], sems.at[c])

    for c in range(CHUNKS):
        for b in range(rows // OWN):
            k = c * (rows // OWN) + b
            rim = slice(k * RIM, (k + 1) * RIM)
            data = jnp.concatenate(
                [shape[2 * k * RIM : 2 * (k + 1) * RIM, :], rylo[rim, :], ryhi[rim, :]], 0
            )
            total = fix[k * OWN : (k + 1) * OWN, :] + dot(spread[...], data)
            if k == 0:
                total = total + rxlo[:OWN, :].astype(f32)
            if k == BLOCKS - 1:
                total = total + rxhi[:OWN, :].astype(f32)
            buf[k * OWN : (k + 1) * OWN, :] = total
        copy(c).start()
    for c in range(CHUNKS):
        copy(c).wait()


def combine(*args):
    return call(
        combine_kernel,
        sds((CELLS, NZ), f32),
        [VM] * 7,
        16,
        out_specs=HBM,
        scratch=[pltpu.VMEM((CELLS, NZ), f32), pltpu.SemaphoreType.DMA((CHUNKS,))],
    )(*args)


GY = ("gz", "gw")


def shift(x, axis, step):
    size = lax.axis_size(axis)
    return lax.ppermute(x, axis, [(i, (i + step) % size) for i in range(size)])


def exchange(x, axis):
    return lax.all_to_all(x, axis, 0, 0)


def local(
    residual, local_x, local_y, local_z, eig_x, eig_y, eig_z, coarse_x, coarse_y, coarse_z,
    mode_x, mode_y, mode_z, coarse_eig_x, coarse_eig_y, coarse_eig_z,
):
    cells = residual.reshape(CELLS, NZ)
    first_x, last_x, rim_lo, rim_hi, along_y, sel = load(cells, coarse_y)
    xlo = shift(last_x, "gx", 1)
    xhi = shift(first_x, "gx", -1)
    own_coarse, modes_xz = call(
        restrict_kernel, (sds((8, MODES, 16), f32), sds((128, 128), f32)), [VM] * 5, 8
    )(along_y, coarse_x.T, coarse_z.T, mode_x, mode_z)
    rows = exchange(own_coarse, "gx")
    down, up = corners(sel, rim_lo, rim_hi, xlo, xhi, own_coarse)
    ylo = shift(up, GY, 1)
    yhi = shift(down, GY, -1)
    part = call(coarse_x_kernel, sds((4, MODES, 128), f32), [VM] * 2, 4)(
        rows, modes_xz
    )
    rows = exchange(part, "gw")

    wy, wyt, spread, wx, wxt, lz, lzt, exb, eyz = prepare(
        local_x, local_y, local_z, eig_x[None], eig_y[None], eig_z[None], coarse_y.T, part
    )
    field, out_xlo, out_xhi, out_ylo, out_yhi = solve(
        cells, xlo, xhi, ylo, yhi, wy, wyt, wx, wxt, lz, lzt, exb, eyz, rows
    )

    rxlo = shift(out_xhi, "gx", 1)
    rxhi = shift(out_xlo, "gx", -1)
    fix = call(finish_kernel, sds((CELLS, NZ), f32), [VM] * 2, 8)(field, wyt)
    down, up = fold(out_ylo, out_yhi, rxlo, rxhi, fix)
    rylo = shift(up, GY, 1)
    ryhi = shift(down, GY, -1)
    rows = call(coarse_y_kernel, sds((8, 16, 128), f32), [VM, ANY], 4)(rows, up)
    rows = exchange(rows, "gz")
    shape = call(coarse_kernel, sds((2 * CX * MODES, NZ), bf16), [VM] * 8, 8)(
        rows, modes_xz, mode_y, coarse_eig_x[None], coarse_eig_y[None], coarse_eig_z[None],
        coarse_x.T, coarse_z.T,
    )
    out = combine(fix, spread, shape, rxlo, rxhi, rylo, ryhi)
    return out.reshape(CX, CY, NZ)


def solution(mesh):
    fine = Mesh(mesh.devices.reshape(8, 8, 4), ("gx", "gz", "gw"))
    cells = P("gx", GY, None)

    return jax.shard_map(
        local, mesh=fine, in_specs=(cells,) + (P(),) * 15, out_specs=cells, check_vma=False
    )
```

```python
import jax
import jax.numpy as jnp
from jax import lax
from jax.experimental import pallas as pl
from jax.experimental.pallas import tpu as pltpu
from jax.sharding import PartitionSpec as P


OV = 4
MODES = 4
CX = 128
CY = 32
NZ = 256
EX = 136
EY = 40
GX = 4
ROWS = GX * EY
OWN = GX * CY
RIM = GX * OV
BLOCKS = CX // GX
CELLS = CX * CY
CHUNKS = 8
WIDE_LOAD = 50
WIDE_SOLVE = 48
HI = lax.Precision.HIGHEST
f32 = jnp.float32
bf16 = jnp.bfloat16
sds = jax.ShapeDtypeStruct

VM = pl.BlockSpec(memory_space=pltpu.VMEM)
SM = pl.BlockSpec(memory_space=pltpu.SMEM)
ANY = pl.BlockSpec(memory_space=pl.ANY)
HBM = pl.BlockSpec(memory_space=pltpu.HBM)


def dot(a, b):
    return jnp.dot(a, b, preferred_element_type=f32)


def dot_t(a, b):
    return lax.dot_general(a, b, (((1,), (1,)), ((), ())), preferred_element_type=f32)


def dot_hi(a, b):
    return jnp.dot(a, b, preferred_element_type=f32, precision=HI)


def dot_t_hi(a, b):
    dims = (((1,), (1,)), ((), ()))
    return lax.dot_general(a, b, dims, preferred_element_type=f32, precision=HI)


def split(x):
    high = x.astype(bf16)
    return high, (x - high.astype(f32)).astype(bf16)


def split3(x):
    high = x.astype(bf16)
    rest = x - high.astype(f32)
    middle = rest.astype(bf16)
    return high, middle, (rest - middle.astype(f32)).astype(bf16)


def expand(x, rows=None, cols=None):
    parts = split3(x)
    if rows is not None:
        return dot(jnp.concatenate([rows] * 3, 1), jnp.concatenate(parts, 0))
    return dot(jnp.concatenate(parts, 1), jnp.concatenate([cols] * 3, 0))


def iotas(shape):
    return lax.broadcasted_iota(jnp.int32, shape, 0), lax.broadcasted_iota(jnp.int32, shape, 1)


def pick(mask, kind=bf16):
    return jnp.where(mask, 1.0, 0.0).astype(kind)


def call(kernel, out_shape, in_specs, mib, out_specs=None, scratch=()):
    if out_specs is None:
        out_specs = jax.tree.map(lambda _: VM, out_shape)
    return pl.pallas_call(
        kernel,
        out_shape=out_shape,
        in_specs=in_specs,
        out_specs=out_specs,
        scratch_shapes=list(scratch),
        compiler_params=pltpu.CompilerParams(vmem_limit_bytes=mib << 20),
    )


def tile(ref, k, rows):
    return ref[pl.ds(pl.multiple_of(k * rows, rows), rows), :]


def selection(cyt):
    row, col = iotas((3 * RIM, OWN))
    y, k = iotas((CY, OWN))
    spread = dot(cyt, pick((k & 31) == y)).astype(bf16)
    row4, n = iotas((3 * RIM, MODES))
    modes = dot(pick((row4 & 3) == n), spread)
    plane = ((row >> 2) & 3) == (col >> 5)
    inner = col & 31
    target = jnp.where(row < RIM, row & 3, CY - OV + (row & 3))
    ones = jnp.where(inner == target, 1.0, 0.0)
    value = jnp.where(row < 2 * RIM, ones, modes)
    return jnp.where(plane, value, 0.0).astype(bf16)


def load_kernel(
    residual, cyt, first_x, last_x, rim_lo, rim_hi, along_y, sel, buf, sems, cyt_buf, sem
):
    rows = CELLS // CHUNKS

    def copy(c):
        at = pl.ds(c * rows, rows)
        return pltpu.make_async_copy(residual.at[at, :], buf.at[at, :], sems.at[c])

    for c in range(CHUNKS):
        copy(c).start()
    small = pltpu.make_async_copy(cyt, cyt_buf, sem)
    small.start()
    small.wait()
    take = selection(cyt_buf[...])
    sel[...] = take
    for c in range(CHUNKS):
        copy(c).wait()
        for b in range(rows // OWN):
            k = c * (rows // OWN) + b
            data = buf[k * OWN : (k + 1) * OWN, :].astype(bf16)
            if k == 0:
                first_x[...] = data
            if k == BLOCKS - 1:
                last_x[...] = data
            out = dot(take, data)
            at = slice(k * RIM, (k + 1) * RIM)
            rim_lo[at, :] = out[:RIM].astype(bf16)
            rim_hi[at, :] = out[RIM : 2 * RIM].astype(bf16)
            along_y[at, :] = out[2 * RIM :]


def load(residual, coarse_y):
    rim = sds((CX * OV, NZ), bf16)
    return call(
        load_kernel,
        (
            sds((OWN, NZ), bf16), sds((OWN, NZ), bf16), rim, rim,
            sds((CX * MODES, NZ), f32), sds((3 * RIM, OWN), bf16),
        ),
        [HBM, HBM],
        WIDE_LOAD,
        scratch=[
            pltpu.VMEM((CELLS, NZ), f32), pltpu.SemaphoreType.DMA((CHUNKS,)),
            pltpu.VMEM((MODES, CY), bf16), pltpu.SemaphoreType.DMA,
        ],
    )(residual, coarse_y.T)


def corners_kernel(sel, rim_lo, rim_hi, xlo, xhi, after, down, up):
    down[: CX * OV, :] = rim_lo[...]
    up[: CX * OV, :] = rim_hi[...]
    for i, strip in enumerate((xlo, xhi)):
        out = dot(sel[: 2 * RIM, :], strip[...]).astype(bf16)
        at = slice(CX * OV + i * RIM, CX * OV + (i + 1) * RIM)
        down[at, :] = out[:RIM]
        up[at, :] = out[RIM:]


def corners(*args):
    side = sds((EX * OV, NZ), bf16)
    return call(corners_kernel, (side, side), [VM] * 5 + [ANY], 8)(*args)


PARAMS = (
    ((EX, EX), bf16), ((EY, EY), bf16), ((NZ, NZ), bf16), ((1, EX), f32), ((1, EY), f32),
    ((1, NZ), f32), ((MODES, CY), bf16),
)
WEIGHTS = (
    ((ROWS, ROWS), bf16), ((ROWS, ROWS), bf16), ((OWN, ROWS + 2 * RIM), bf16),
    ((OWN // 2, 2 * RIM), bf16), ((EX, EX), bf16),
    ((EX, EX), bf16), ((NZ, NZ), bf16), ((NZ, NZ), bf16), ((EX, NZ), f32), ((EY, NZ), f32),
)


def basis_x(cxt):
    x, row = iotas((CX, CX * MODES))
    by_row = dot(cxt, pick((row >> 2) == x)).astype(bf16)
    col, m = iotas((16, MODES))
    value = dot(pick((col >> 2) == m), by_row)
    col, row = iotas((16, CX * MODES))
    return jnp.where((row & 3) == (col & 3), value, 0.0).astype(bf16)


def spread_z(mode_z):
    row, col = iotas((128, 128))
    out = jnp.zeros((128, 128), f32)
    for p in range(MODES):
        for c in range(MODES):
            here = ((row & 3) == p) & ((col & 3) == c)
            out = jnp.where(here, mode_z[p : p + 1, c : c + 1], out)
    return out


def modes_a():
    a, col = iotas((32, 128))
    c, col4 = iotas((MODES, 128))
    return pick((col >> 2) == a), pick((col4 & 3) == c)


def prepare_kernel(*refs):
    n = len(PARAMS)
    sources, outs, bufs, sems = (
        refs[:n], refs[n + 1 : n + 1 + len(WEIGHTS)], refs[n + 1 + len(WEIGHTS) : -1], refs[-1]
    )
    copies = [
        pltpu.make_async_copy(source, buf, sems.at[i])
        for i, (source, buf) in enumerate(zip(sources, bufs))
    ]
    for copy in copies:
        copy.start()
    for copy in copies:
        copy.wait()
    lx, ly, lz, eig_x, eig_y, eig_z, cyt = bufs
    wy, wyt, wfin, spread, wx, wxt, lz_out, lzt, exb, eyz = outs

    def cell(k):
        y = jnp.where(k < OWN, OV + (k & 31), jnp.where(k < OWN + RIM, k & 3, EY - OV + (k & 3)))
        plane = jnp.where(k < OWN, k >> 5, ((k - OWN) >> 2) & 3)
        return y, plane

    def mode(j):
        plane = (j >= EY).astype(jnp.int32) + (j >= 2 * EY) + (j >= 3 * EY)
        return j - EY * plane, plane

    k, y = iotas((ROWS, EY))
    by_cell = dot(pick(cell(k)[0] == y), ly[...]).astype(bf16)
    b, j = iotas((EY, ROWS))
    k, col = iotas((ROWS, ROWS))
    value = dot(by_cell, pick(mode(j)[0] == b))
    value = jnp.where(cell(k)[1] == mode(col)[1], value, 0.0).astype(bf16)
    wyt[...] = value
    j, b = iotas((ROWS, EY))
    back = dot_t(pick(mode(j)[0] == b), by_cell)
    wy[...] = jnp.where(mode(k)[1] == cell(col)[1], back, 0.0).astype(bf16)

    y, k = iotas((CY, OWN))
    by_k = dot(cyt[...], pick((k & 31) == y)).astype(bf16)
    k, own = iotas((OWN, OWN))
    turned = dot_t(pick(k == own), by_k).astype(bf16)
    n, col = iotas((MODES, 2 * RIM))
    coarse = dot(turned, pick((col & 3) == n))
    k, col = iotas((OWN, 2 * RIM))
    inner = k & 31
    plane = (k >> 5) == ((col >> 2) & 3)
    coarse = jnp.where(plane, coarse, 0.0).astype(bf16)
    wfin[...] = jnp.concatenate([value[:OWN], coarse], 1)
    k, col = iotas((OWN // 2, 2 * RIM))
    inner = (k & 15) + jnp.where((k & 15) < 8, 0, CY - 16)
    target = jnp.where(col < RIM, col & 3, CY - OV + (col & 3))
    ones = jnp.where(inner == target, 1.0, 0.0)
    spread[...] = jnp.where((k >> 4) == ((col >> 2) & 3), ones, 0.0).astype(bf16)

    k, x = iotas((EX, EX))
    source = jnp.where(k < CX, k + OV, jnp.where(k < CX + OV, k - CX, k))
    moved = dot(pick(source == x), lx[...]).astype(bf16)
    wxt[...] = moved
    wx[...] = dot_t(pick(k == x), moved).astype(bf16)
    column = jnp.sum(jnp.where(k == x, eig_x[...], 0.0), axis=1, keepdims=True)
    exb[...] = jnp.broadcast_to(column, (EX, NZ))
    b, y = iotas((EY, EY))
    column = jnp.sum(jnp.where(b == y, eig_y[...], 0.0), axis=1, keepdims=True)
    eyz[...] = column + eig_z[...]
    c, z = iotas((NZ, NZ))
    lz_out[...] = lz[...]
    lzt[...] = dot_t(pick(c == z), lz[...]).astype(bf16)


def prepare(*params):
    return call(
        prepare_kernel,
        tuple(sds(*w) for w in WEIGHTS),
        [HBM] * len(PARAMS) + [ANY],
        8,
        scratch=[pltpu.VMEM(*p) for p in PARAMS] + [pltpu.SemaphoreType.DMA((len(PARAMS),))],
    )(*params)


def solve_kernel(
    residual, xlo, xhi, ylo, yhi, wy, wyt, wx, wxt, lz, lzt, exb, eyz, after,
    kept, out_xlo, out_xhi, out_ylo, out_yhi, field, mid, spec, buf, sems,
):
    def put(rows, value):
        field[0, rows, :] = value[:, :128]
        field[1, rows, :] = value[:, 128:]

    def take(rows):
        return jnp.concatenate([field[0, rows, :], field[1, rows, :]], 1)

    def forward_y(main, k):
        data = jnp.concatenate([main, tile(ylo, k, RIM), tile(yhi, k, RIM)], 0)
        put(pl.ds(pl.multiple_of(k * ROWS, ROWS), ROWS), dot(wy[...], data))

    rows = CELLS // CHUNKS
    per = BLOCKS // CHUNKS

    def copy(c):
        at = pl.ds(pl.multiple_of(c * rows, rows), rows)
        return pltpu.make_async_copy(residual.at[at, :], buf.at[at, :], sems.at[c])

    for c in range(CHUNKS):
        copy(c).start()

    def first(c, carry):
        for i in range(2):
            copy(2 * c + i).wait()
        for b in range(2 * per):
            k = c * 2 * per + b
            forward_y(tile(buf, k, OWN).astype(bf16), k)
        return carry

    lax.fori_loop(0, CHUNKS // 2, first, 0)
    forward_y(xlo[...], BLOCKS)
    forward_y(xhi[...], BLOCKS + 1)

    def mid_rows(b):
        return pl.ds(pl.multiple_of(b * EX, 8), EX)

    def forward_x(b, carry):
        plane = take(pl.ds(b, EX, stride=EY)).astype(bf16)
        mid[mid_rows(b), :] = dot(wx[...], plane)
        return carry

    lax.fori_loop(0, EY, forward_x, 0, unroll=40)

    def forward_z(i, carry):
        at = pl.ds(pl.multiple_of(i * 4 * EX, 16), 4 * EX)
        along = dot(mid[at, :].astype(bf16), lz[...])
        parts = []
        for q in range(4):
            scale = exb[...] + eyz[pl.ds(i * 4 + q, 1), :]
            parts.append((along[q * EX : (q + 1) * EX] / scale))
        spec[at, :] = jnp.concatenate(parts, 0).astype(bf16)
        return carry

    lax.fori_loop(0, EY // 4, forward_z, 0, unroll=10)

    def backward_z(i, carry):
        at = pl.ds(pl.multiple_of(i * 4 * EX, 16), 4 * EX)
        mid[at, :] = dot(spec[at, :], lzt[...])
        return carry

    lax.fori_loop(0, EY // 4, backward_z, 0, unroll=10)

    def backward_x(b, carry):
        put(pl.ds(b, EX, stride=EY), dot(wxt[...], mid[mid_rows(b), :].astype(bf16)))
        return carry

    lax.fori_loop(0, EY, backward_x, 0, unroll=40)

    def planes(k):
        return take(pl.ds(pl.multiple_of(k * ROWS, ROWS), ROWS)).astype(bf16)

    out_xlo[...] = dot(wyt[...], planes(BLOCKS)).astype(bf16)
    out_xhi[...] = dot(wyt[...], planes(BLOCKS + 1)).astype(bf16)

    def last(k, carry):
        data = planes(k)
        kept[pl.ds(pl.multiple_of(k * ROWS, ROWS), ROWS), :] = data
        out = dot(wyt[OWN:, :], data).astype(bf16)
        at = pl.ds(pl.multiple_of(k * RIM, RIM), RIM)
        out_ylo[at, :] = out[:RIM]
        out_yhi[at, :] = out[RIM:]
        return carry

    lax.fori_loop(0, BLOCKS, last, 0, unroll=16)


def solve(*args):
    strip = sds((ROWS, NZ), bf16)
    rim = sds((CX * OV, NZ), bf16)
    return call(
        solve_kernel,
        (sds((BLOCKS * ROWS, NZ), bf16), strip, strip, rim, rim),
        [HBM] + [VM] * 12 + [ANY],
        WIDE_SOLVE,
        scratch=[
            pltpu.VMEM((2, EX * EY, NZ // 2), f32), pltpu.VMEM((EX * EY, NZ), f32),
            pltpu.VMEM((EX * EY, NZ), bf16), pltpu.VMEM((CELLS, NZ), f32),
            pltpu.SemaphoreType.DMA((CHUNKS,)),
        ],
    )(*args)


def fold_kernel(out_ylo, out_yhi, rxlo, rxhi, down, up):
    end = CX * OV
    for strip, start, out in ((out_ylo, OWN, down), (out_yhi, OWN + RIM, up)):
        rows = slice(start, start + RIM)
        out[...] = strip[...]
        low = strip[:RIM, :].astype(f32) + rxlo[rows, :].astype(f32)
        high = strip[end - RIM :, :].astype(f32) + rxhi[rows, :].astype(f32)
        out[:RIM, :] = low.astype(bf16)
        out[end - RIM :, :] = high.astype(bf16)


def fold(*args):
    rim = sds((CX * OV, NZ), bf16)
    return call(fold_kernel, (rim, rim), [VM] * 4, 8)(*args)


def restrict_kernel(along_y, cxt, czt, mode_x, mode_z, out, modes_xz):
    bx = basis_x(cxt[...])
    high, low = split(along_y[...])
    both = dot(bx, high) + dot(bx, low)
    own = dot_t_hi(both, czt[...].astype(f32))
    flat = jnp.concatenate([own[m * MODES : (m + 1) * MODES] for m in range(MODES)], 1)
    for i in range(out.shape[0]):
        out[i] = flat
    to_a, _ = modes_a()
    r, i = iotas((128, 32))
    part_x = expand(expand(mode_x[...], rows=pick((r >> 2) == i)), cols=to_a)
    part_z = spread_z(mode_z[...])
    modes_xz[...] = part_x * part_z


def coarse_x_kernel(rows, modes_xz, out):
    part = dot_hi(jnp.concatenate([rows[i] for i in range(8)], 1), modes_xz[...])
    for i in range(out.shape[0]):
        out[i] = part


def coarse_kernel(rows, modes_xz, mode_y, ceig_x, ceig_y, ceig_z, cxt, czt, after, out):
    to_a, to_c = modes_a()
    eight_x = jnp.broadcast_to(ceig_x[...], (8, 32))
    eight_z = jnp.broadcast_to(ceig_z[...], (8, MODES))
    row = (dot_hi(eight_x, to_a.astype(f32)) + dot_hi(eight_z, to_c.astype(f32)))[:1]
    r, b = iotas((128, 128))
    column = jnp.sum(jnp.where(r == b, ceig_y[...], 0.0), axis=1, keepdims=True)
    columns = jnp.concatenate([rows[j] for j in range(rows.shape[0])], 0)
    hat = dot_hi(mode_y[...].T, columns) / (column + row)
    row, col = iotas((8, 128))
    mine = pick(col == lax.axis_index("gy") * MODES + row, f32)
    rows_y = dot_hi(mine, mode_y[...])
    rows_xz = modes_xz[pl.ds(pl.multiple_of(lax.axis_index("gx") * 16, 16), 16), :]
    sol = dot_t_hi(dot_hi(rows_y, hat), rows_xz)
    levels = czt[...].astype(f32)
    shape = jnp.concatenate(
        [dot_hi(sol[:, m * MODES : (m + 1) * MODES], levels)[:MODES] for m in range(MODES)], 0
    )
    high, low = split(shape)
    col, i = iotas((32, 16))
    twice = dot(pick((col & 15) == i), basis_x(cxt[...]))
    value = dot(twice.T.astype(bf16), jnp.concatenate([high, low], 0))
    high, low = split(value)
    for k in range(BLOCKS):
        at = slice(k * RIM, (k + 1) * RIM)
        out[2 * k * RIM : (2 * k + 1) * RIM, :] = high[at]
        out[(2 * k + 1) * RIM : (2 * k + 2) * RIM, :] = low[at]


def inner_copy(buf, out, sems, c):
    at = pl.ds(pl.multiple_of(c * (CX // CHUNKS), CX // CHUNKS), CX // CHUNKS)
    inner = pl.ds(8, CY - 16)
    return pltpu.make_async_copy(buf.at[at, inner, :], out.at[at, inner, :], sems.at[c])


def finish_kernel(field, wfin, shape, rxlo, rxhi, after, out, rims, buf, sems):
    per = BLOCKS // CHUNKS

    def block(k, extra):
        data = jnp.concatenate([tile(field, k, ROWS), tile(shape, k, 2 * RIM)], 0)
        total = dot(wfin[...], data)
        if extra is not None:
            total = total + extra[:OWN, :].astype(f32)
        total = total.reshape(GX, CY, NZ)
        planes = pl.ds(pl.multiple_of(k * GX, GX), GX)
        buf[planes, :, :] = total
        rims[planes, :8, :] = total[:, :8]
        rims[planes, 8:, :] = total[:, CY - 8 :]

    def step(c, carry):
        for b in range(per):
            block(c * per + b, None)
        inner_copy(buf, out, sems, c).start()
        return carry

    for b in range(per):
        block(b, rxlo if b == 0 else None)
    inner_copy(buf, out, sems, 0).start()
    lax.fori_loop(1, CHUNKS - 1, step, 0, unroll=2)
    for b in range(per):
        block(BLOCKS - per + b, rxhi if b == per - 1 else None)
    inner_copy(buf, out, sems, CHUNKS - 1).start()
    for c in range(CHUNKS):
        inner_copy(buf, out, sems, c).wait()


def finish(*args):
    return call(
        finish_kernel,
        (sds((CX, CY, NZ), f32), sds((CX, 16, NZ), f32)),
        [VM] * 5 + [ANY],
        16,
        out_specs=(HBM, VM),
        scratch=[pltpu.VMEM((CX, CY, NZ), f32), pltpu.SemaphoreType.DMA((CHUNKS,))],
    )(*args)


def combine_kernel(partial, rims, spread, rylo, ryhi, out, buf, sems):
    planes = CX // CHUNKS
    per = BLOCKS // CHUNKS

    def copies(c):
        at = pl.ds(c * planes, planes)
        return [
            pltpu.make_async_copy(
                buf.at[at, pl.ds(8 * i, 8), :], out.at[at, pl.ds(i * (CY - 8), 8), :],
                sems.at[2 * c + i],
            )
            for i in range(2)
        ]

    for c in range(CHUNKS):
        for b in range(per):
            k = c * per + b
            rim = slice(k * RIM, (k + 1) * RIM)
            data = jnp.concatenate([rylo[rim, :], ryhi[rim, :]], 0)
            strips = dot(spread[...], data).reshape(GX, 16, NZ)
            at = slice(k * GX, (k + 1) * GX)
            buf[at] = rims[at] + strips
        for copy in copies(c):
            copy.start()
    for c in range(CHUNKS):
        for copy in copies(c):
            copy.wait()


def combine(*args):
    return pl.pallas_call(
        combine_kernel,
        out_shape=sds((CX, CY, NZ), f32),
        in_specs=[HBM] + [VM] * 4,
        out_specs=HBM,
        scratch_shapes=[pltpu.VMEM((CX, 16, NZ), f32), pltpu.SemaphoreType.DMA((2 * CHUNKS,))],
        input_output_aliases={0: 0},
        compiler_params=pltpu.CompilerParams(vmem_limit_bytes=16 << 20),
        name="combine",
    )(*args)


def shift(x, axis, step):
    size = lax.axis_size(axis)
    return lax.ppermute(x, axis, [(i, (i + step) % size) for i in range(size)])


def exchange(x, axis):
    return lax.all_to_all(x, axis, 0, 0)


def local(
    residual, local_x, local_y, local_z, eig_x, eig_y, eig_z, coarse_x, coarse_y, coarse_z,
    mode_x, mode_y, mode_z, coarse_eig_x, coarse_eig_y, coarse_eig_z,
):
    cells = residual.reshape(CELLS, NZ)
    first_x, last_x, rim_lo, rim_hi, along_y, sel = load(cells, coarse_y)
    xlo = shift(last_x, "gx", 1)
    xhi = shift(first_x, "gx", -1)
    own_coarse, modes_xz = call(
        restrict_kernel, (sds((8, MODES, 16), f32), sds((128, 128), f32)), [VM] * 5, 8
    )(along_y, coarse_x.T, coarse_z.T, mode_x, mode_z)
    rows = exchange(own_coarse, "gx")
    down, up = corners(sel, rim_lo, rim_hi, xlo, xhi, own_coarse)
    ylo = shift(up, "gy", 1)
    yhi = shift(down, "gy", -1)
    part = call(coarse_x_kernel, sds((32, MODES, 128), f32), [VM] * 2, 4)(rows, modes_xz)
    rows = exchange(part, "gy")

    wy, wyt, wfin, spread, wx, wxt, lz, lzt, exb, eyz = prepare(
        local_x, local_y, local_z, eig_x[None], eig_y[None], eig_z[None], coarse_y.T, part
    )
    field, out_xlo, out_xhi, out_ylo, out_yhi = solve(
        cells, xlo, xhi, ylo, yhi, wy, wyt, wx, wxt, lz, lzt, exb, eyz, part
    )

    rxlo = shift(out_xhi, "gx", 1)
    rxhi = shift(out_xlo, "gx", -1)
    down, up = fold(out_ylo, out_yhi, rxlo, rxhi)
    rylo = shift(up, "gy", 1)
    ryhi = shift(down, "gy", -1)
    shape = call(coarse_kernel, sds((2 * CX * MODES, NZ), bf16), [VM] * 8 + [ANY], 8)(
        rows, modes_xz, mode_y, coarse_eig_x[None], coarse_eig_y[None], coarse_eig_z[None],
        coarse_x.T, coarse_z.T, up,
    )
    partial, rims = finish(field, wfin, shape, rxlo, rxhi, up)
    return combine(partial, rims, spread, rylo, ryhi)


def solution(mesh):
    cells = P("gx", "gy", None)

    return jax.shard_map(
        local, mesh=mesh, in_specs=(cells,) + (P(),) * 15, out_specs=cells, check_vma=False
    )
```

```python
import jax
import jax.numpy as jnp
from jax import lax
from jax.experimental import pallas as pl
from jax.experimental.pallas import tpu as pltpu
from jax.sharding import PartitionSpec as P


OV = 4
MODES = 4
CX = 128
CY = 32
NZ = 256
EX = 136
EY = 40
GX = 4
ROWS = GX * EY
OWN = GX * CY
RIM = GX * OV
BLOCKS = CX // GX
CELLS = CX * CY
CHUNKS = 8
WIDE_LOAD = 50
WIDE_SOLVE = 48
HI = lax.Precision.HIGHEST
f32 = jnp.float32
bf16 = jnp.bfloat16
sds = jax.ShapeDtypeStruct

VM = pl.BlockSpec(memory_space=pltpu.VMEM)
SM = pl.BlockSpec(memory_space=pltpu.SMEM)
ANY = pl.BlockSpec(memory_space=pl.ANY)
HBM = pl.BlockSpec(memory_space=pltpu.HBM)


def dot(a, b):
    return jnp.dot(a, b, preferred_element_type=f32)


def dot_t(a, b):
    return lax.dot_general(a, b, (((1,), (1,)), ((), ())), preferred_element_type=f32)


def dot_hi(a, b):
    return jnp.dot(a, b, preferred_element_type=f32, precision=HI)


def dot_t_hi(a, b):
    dims = (((1,), (1,)), ((), ()))
    return lax.dot_general(a, b, dims, preferred_element_type=f32, precision=HI)


def split(x):
    high = x.astype(bf16)
    return high, (x - high.astype(f32)).astype(bf16)


def split3(x):
    high = x.astype(bf16)
    rest = x - high.astype(f32)
    middle = rest.astype(bf16)
    return high, middle, (rest - middle.astype(f32)).astype(bf16)


def expand(x, rows=None, cols=None):
    parts = split3(x)
    if rows is not None:
        return dot(jnp.concatenate([rows] * 3, 1), jnp.concatenate(parts, 0))
    return dot(jnp.concatenate(parts, 1), jnp.concatenate([cols] * 3, 0))


def iotas(shape):
    return lax.broadcasted_iota(jnp.int32, shape, 0), lax.broadcasted_iota(jnp.int32, shape, 1)


def pick(mask, kind=bf16):
    return jnp.where(mask, 1.0, 0.0).astype(kind)


def call(kernel, out_shape, in_specs, mib, out_specs=None, scratch=()):
    if out_specs is None:
        out_specs = jax.tree.map(lambda _: VM, out_shape)
    return pl.pallas_call(
        kernel,
        out_shape=out_shape,
        in_specs=in_specs,
        out_specs=out_specs,
        scratch_shapes=list(scratch),
        compiler_params=pltpu.CompilerParams(vmem_limit_bytes=mib << 20),
    )


def tile(ref, k, rows):
    return ref[pl.ds(pl.multiple_of(k * rows, rows), rows), :]


def selection(cyt):
    row, col = iotas((3 * RIM, OWN))
    y, k = iotas((CY, OWN))
    spread = dot(cyt, pick((k & 31) == y)).astype(bf16)
    row4, n = iotas((3 * RIM, MODES))
    modes = dot(pick((row4 & 3) == n), spread)
    plane = ((row >> 2) & 3) == (col >> 5)
    inner = col & 31
    target = jnp.where(row < RIM, row & 3, CY - OV + (row & 3))
    ones = jnp.where(inner == target, 1.0, 0.0)
    value = jnp.where(row < 2 * RIM, ones, modes)
    return jnp.where(plane, value, 0.0).astype(bf16)


def load_kernel(
    residual, cyt, first_x, last_x, rim_lo, rim_hi, along_y, sel, buf, sems, cyt_buf, sem
):
    rows = CELLS // CHUNKS

    def copy(c):
        at = pl.ds(c * rows, rows)
        return pltpu.make_async_copy(residual.at[at, :], buf.at[at, :], sems.at[c])

    for c in range(CHUNKS):
        copy(c).start()
    small = pltpu.make_async_copy(cyt, cyt_buf, sem)
    small.start()
    small.wait()
    take = selection(cyt_buf[...])
    sel[...] = take
    for c in range(CHUNKS):
        copy(c).wait()
        for b in range(rows // OWN):
            k = c * (rows // OWN) + b
            data = buf[k * OWN : (k + 1) * OWN, :].astype(bf16)
            if k == 0:
                first_x[...] = data
            if k == BLOCKS - 1:
                last_x[...] = data
            out = dot(take, data)
            at = slice(k * RIM, (k + 1) * RIM)
            rim_lo[at, :] = out[:RIM].astype(bf16)
            rim_hi[at, :] = out[RIM : 2 * RIM].astype(bf16)
            along_y[at, :] = out[2 * RIM :]


def load(residual, coarse_y):
    rim = sds((CX * OV, NZ), bf16)
    return call(
        load_kernel,
        (
            sds((OWN, NZ), bf16), sds((OWN, NZ), bf16), rim, rim,
            sds((CX * MODES, NZ), f32), sds((3 * RIM, OWN), bf16),
        ),
        [HBM, HBM],
        WIDE_LOAD,
        scratch=[
            pltpu.VMEM((CELLS, NZ), f32), pltpu.SemaphoreType.DMA((CHUNKS,)),
            pltpu.VMEM((MODES, CY), bf16), pltpu.SemaphoreType.DMA,
        ],
    )(residual, pltpu.with_memory_space_constraint(coarse_y.T, pltpu.HBM))


def corners_kernel(sel, rim_lo, rim_hi, xlo, xhi, after, down, up):
    down[: CX * OV, :] = rim_lo[...]
    up[: CX * OV, :] = rim_hi[...]
    for i, strip in enumerate((xlo, xhi)):
        out = dot(sel[: 2 * RIM, :], strip[...]).astype(bf16)
        at = slice(CX * OV + i * RIM, CX * OV + (i + 1) * RIM)
        down[at, :] = out[:RIM]
        up[at, :] = out[RIM:]


def corners(*args):
    side = sds((EX * OV, NZ), bf16)
    return call(corners_kernel, (side, side), [VM] * 5 + [ANY], 8)(*args)


PARAMS = (
    ((EX, EX), bf16), ((EY, EY), bf16), ((NZ, NZ), bf16), ((1, EX), f32), ((1, EY), f32),
    ((1, NZ), f32), ((MODES, CY), bf16),
)
WEIGHTS = (
    ((ROWS, ROWS), bf16), ((ROWS, ROWS), bf16), ((OWN, ROWS + 2 * RIM), bf16),
    ((OWN // 2, 2 * RIM), bf16), ((EX, EX), bf16),
    ((EX, EX), bf16), ((NZ, NZ), bf16), ((NZ, NZ), bf16), ((EX, NZ), f32), ((EY, NZ), f32),
)


def basis_x(cxt):
    x, row = iotas((CX, CX * MODES))
    by_row = dot(cxt, pick((row >> 2) == x)).astype(bf16)
    col, m = iotas((16, MODES))
    value = dot(pick((col >> 2) == m), by_row)
    col, row = iotas((16, CX * MODES))
    return jnp.where((row & 3) == (col & 3), value, 0.0).astype(bf16)


def spread_z(mode_z):
    row, col = iotas((128, 128))
    out = jnp.zeros((128, 128), f32)
    for p in range(MODES):
        for c in range(MODES):
            here = ((row & 3) == p) & ((col & 3) == c)
            out = jnp.where(here, mode_z[p : p + 1, c : c + 1], out)
    return out


def modes_a():
    a, col = iotas((32, 128))
    c, col4 = iotas((MODES, 128))
    return pick((col >> 2) == a), pick((col4 & 3) == c)


def prepare_kernel(*refs):
    n = len(PARAMS)
    bufs, outs = refs[:n], refs[n + 1 :]
    lx, ly, lz, eig_x, eig_y, eig_z, cyt = bufs
    wy, wyt, wfin, spread, wx, wxt, lz_out, lzt, exb, eyz = outs

    def cell(k):
        y = jnp.where(k < OWN, OV + (k & 31), jnp.where(k < OWN + RIM, k & 3, EY - OV + (k & 3)))
        plane = jnp.where(k < OWN, k >> 5, ((k - OWN) >> 2) & 3)
        return y, plane

    def mode(j):
        plane = (j >= EY).astype(jnp.int32) + (j >= 2 * EY) + (j >= 3 * EY)
        return j - EY * plane, plane

    k, y = iotas((ROWS, EY))
    by_cell = dot(pick(cell(k)[0] == y), ly[...]).astype(bf16)
    b, j = iotas((EY, ROWS))
    k, col = iotas((ROWS, ROWS))
    value = dot(by_cell, pick(mode(j)[0] == b))
    value = jnp.where(cell(k)[1] == mode(col)[1], value, 0.0).astype(bf16)
    wyt[...] = value
    j, b = iotas((ROWS, EY))
    back = dot_t(pick(mode(j)[0] == b), by_cell)
    wy[...] = jnp.where(mode(k)[1] == cell(col)[1], back, 0.0).astype(bf16)

    y, k = iotas((CY, OWN))
    by_k = dot(cyt[...], pick((k & 31) == y)).astype(bf16)
    k, own = iotas((OWN, OWN))
    turned = dot_t(pick(k == own), by_k).astype(bf16)
    n, col = iotas((MODES, 2 * RIM))
    coarse = dot(turned, pick((col & 3) == n))
    k, col = iotas((OWN, 2 * RIM))
    inner = k & 31
    plane = (k >> 5) == ((col >> 2) & 3)
    coarse = jnp.where(plane, coarse, 0.0).astype(bf16)
    wfin[...] = jnp.concatenate([value[:OWN], coarse], 1)
    k, col = iotas((OWN // 2, 2 * RIM))
    inner = (k & 15) + jnp.where((k & 15) < 8, 0, CY - 16)
    target = jnp.where(col < RIM, col & 3, CY - OV + (col & 3))
    ones = jnp.where(inner == target, 1.0, 0.0)
    spread[...] = jnp.where((k >> 4) == ((col >> 2) & 3), ones, 0.0).astype(bf16)

    k, x = iotas((EX, EX))
    source = jnp.where(k < CX, k + OV, jnp.where(k < CX + OV, k - CX, k))
    moved = dot(pick(source == x), lx[...]).astype(bf16)
    wxt[...] = moved
    wx[...] = dot_t(pick(k == x), moved).astype(bf16)
    column = jnp.sum(jnp.where(k == x, eig_x[...], 0.0), axis=1, keepdims=True)
    exb[...] = jnp.broadcast_to(column, (EX, NZ))
    b, y = iotas((EY, EY))
    column = jnp.sum(jnp.where(b == y, eig_y[...], 0.0), axis=1, keepdims=True)
    eyz[...] = column + eig_z[...]
    c, z = iotas((NZ, NZ))
    lz_out[...] = lz[...]
    lzt[...] = dot_t(pick(c == z), lz[...]).astype(bf16)


def prepare(*params):
    return call(
        prepare_kernel, tuple(sds(*w) for w in WEIGHTS), [VM] * len(PARAMS) + [ANY], 8
    )(*params)


def solve_kernel(
    residual, xlo, xhi, ylo, yhi, wy, wyt, wx, wxt, lz, lzt, exb, eyz, after,
    kept, out_xlo, out_xhi, out_ylo, out_yhi, field, mid, spec, buf, sems,
):
    def put(rows, value):
        field[0, rows, :] = value[:, :128]
        field[1, rows, :] = value[:, 128:]

    def take(rows):
        return jnp.concatenate([field[0, rows, :], field[1, rows, :]], 1)

    def forward_y(main, k):
        data = jnp.concatenate([main, tile(ylo, k, RIM), tile(yhi, k, RIM)], 0)
        put(pl.ds(pl.multiple_of(k * ROWS, ROWS), ROWS), dot(wy[...], data))

    rows = CELLS // CHUNKS
    per = BLOCKS // CHUNKS

    def copy(c):
        at = pl.ds(pl.multiple_of(c * rows, rows), rows)
        return pltpu.make_async_copy(residual.at[at, :], buf.at[at, :], sems.at[c])

    for c in range(CHUNKS):
        copy(c).start()

    def first(c, carry):
        for i in range(2):
            copy(2 * c + i).wait()
        for b in range(2 * per):
            k = c * 2 * per + b
            forward_y(tile(buf, k, OWN).astype(bf16), k)
        return carry

    lax.fori_loop(0, CHUNKS // 2, first, 0)
    forward_y(xlo[...], BLOCKS)
    forward_y(xhi[...], BLOCKS + 1)

    def mid_rows(b):
        return pl.ds(pl.multiple_of(b * EX, 8), EX)

    def forward_x(b, carry):
        plane = take(pl.ds(b, EX, stride=EY)).astype(bf16)
        mid[mid_rows(b), :] = dot(wx[...], plane)
        return carry

    lax.fori_loop(0, EY, forward_x, 0, unroll=40)

    def forward_z(i, carry):
        at = pl.ds(pl.multiple_of(i * 4 * EX, 16), 4 * EX)
        along = dot(mid[at, :].astype(bf16), lz[...])
        parts = []
        for q in range(4):
            scale = exb[...] + eyz[pl.ds(i * 4 + q, 1), :]
            parts.append((along[q * EX : (q + 1) * EX] / scale))
        spec[at, :] = jnp.concatenate(parts, 0).astype(bf16)
        return carry

    lax.fori_loop(0, EY // 4, forward_z, 0, unroll=10)

    def backward_z(i, carry):
        at = pl.ds(pl.multiple_of(i * 4 * EX, 16), 4 * EX)
        mid[at, :] = dot(spec[at, :], lzt[...])
        return carry

    lax.fori_loop(0, EY // 4, backward_z, 0, unroll=10)

    def backward_x(b, carry):
        put(pl.ds(b, EX, stride=EY), dot(wxt[...], mid[mid_rows(b), :].astype(bf16)))
        return carry

    lax.fori_loop(0, EY, backward_x, 0, unroll=40)

    def planes(k):
        return take(pl.ds(pl.multiple_of(k * ROWS, ROWS), ROWS)).astype(bf16)

    out_xlo[...] = dot(wyt[...], planes(BLOCKS)).astype(bf16)
    out_xhi[...] = dot(wyt[...], planes(BLOCKS + 1)).astype(bf16)

    def last(k, carry):
        data = planes(k)
        kept[pl.ds(pl.multiple_of(k * ROWS, ROWS), ROWS), :] = data
        out = dot(wyt[OWN:, :], data).astype(bf16)
        at = pl.ds(pl.multiple_of(k * RIM, RIM), RIM)
        out_ylo[at, :] = out[:RIM]
        out_yhi[at, :] = out[RIM:]
        return carry

    lax.fori_loop(0, BLOCKS, last, 0, unroll=16)


def solve(*args):
    strip = sds((ROWS, NZ), bf16)
    rim = sds((CX * OV, NZ), bf16)
    return call(
        solve_kernel,
        (sds((BLOCKS * ROWS, NZ), bf16), strip, strip, rim, rim),
        [HBM] + [VM] * 12 + [ANY],
        WIDE_SOLVE,
        scratch=[
            pltpu.VMEM((2, EX * EY, NZ // 2), f32), pltpu.VMEM((EX * EY, NZ), f32),
            pltpu.VMEM((EX * EY, NZ), bf16), pltpu.VMEM((CELLS, NZ), f32),
            pltpu.SemaphoreType.DMA((CHUNKS,)),
        ],
    )(*args)


def turn_kernel(rxlo, rxhi, down, up):
    for start, out in ((OWN, down), (OWN + RIM, up)):
        out[:RIM, :] = rxlo[start : start + RIM, :]
        out[RIM:, :] = rxhi[start : start + RIM, :]


def turn(*args):
    both = sds((2 * RIM, NZ), bf16)
    return call(turn_kernel, (both, both), [VM] * 2, 4)(*args)


def restrict_kernel(along_y, cxt, czt, mode_x, mode_z, out, modes_xz):
    bx = basis_x(cxt[...])
    high, low = split(along_y[...])
    both = dot(bx, high) + dot(bx, low)
    own = dot_t_hi(both, czt[...].astype(f32))
    flat = jnp.concatenate([own[m * MODES : (m + 1) * MODES] for m in range(MODES)], 1)
    for i in range(out.shape[0]):
        out[i] = flat
    to_a, _ = modes_a()
    r, i = iotas((128, 32))
    part_x = expand(expand(mode_x[...], rows=pick((r >> 2) == i)), cols=to_a)
    part_z = spread_z(mode_z[...])
    modes_xz[...] = part_x * part_z


def coarse_x_kernel(rows, modes_xz, out):
    part = dot_hi(jnp.concatenate([rows[i] for i in range(8)], 1), modes_xz[...])
    for i in range(out.shape[0]):
        out[i] = part


COARSE = (
    ((128, 128), f32), ((1, 32), f32), ((1, 128), f32), ((1, MODES), f32), ((MODES, CX), bf16),
    ((MODES, NZ), bf16),
)


def coarse_kernel(rows, modes_xz, *refs):
    n = len(COARSE)
    sources, out, bufs, sems = refs[:n], refs[n + 1], refs[n + 2 : -1], refs[-1]
    copies = [
        pltpu.make_async_copy(source, buf, sems.at[i])
        for i, (source, buf) in enumerate(zip(sources, bufs))
    ]
    for copy in copies:
        copy.start()
    for copy in copies:
        copy.wait()
    mode_y, ceig_x, ceig_y, ceig_z, cxt, czt = bufs
    to_a, to_c = modes_a()
    eight_x = jnp.broadcast_to(ceig_x[...], (8, 32))
    eight_z = jnp.broadcast_to(ceig_z[...], (8, MODES))
    row = (dot_hi(eight_x, to_a.astype(f32)) + dot_hi(eight_z, to_c.astype(f32)))[:1]
    r, b = iotas((128, 128))
    column = jnp.sum(jnp.where(r == b, ceig_y[...], 0.0), axis=1, keepdims=True)
    columns = jnp.concatenate([rows[j] for j in range(rows.shape[0])], 0)
    hat = dot_hi(mode_y[...].T, columns) / (column + row)
    row, col = iotas((8, 128))
    mine = pick(col == lax.axis_index("gy") * MODES + row, f32)
    rows_y = dot_hi(mine, mode_y[...])
    rows_xz = modes_xz[pl.ds(pl.multiple_of(lax.axis_index("gx") * 16, 16), 16), :]
    sol = dot_t_hi(dot_hi(rows_y, hat), rows_xz)
    levels = czt[...].astype(f32)
    shape = jnp.concatenate(
        [dot_hi(sol[:, m * MODES : (m + 1) * MODES], levels)[:MODES] for m in range(MODES)], 0
    )
    high, low = split(shape)
    col, i = iotas((32, 16))
    twice = dot(pick((col & 15) == i), basis_x(cxt[...]))
    value = dot(twice.T.astype(bf16), jnp.concatenate([high, low], 0))
    high, low = split(value)
    for k in range(BLOCKS):
        at = slice(k * RIM, (k + 1) * RIM)
        out[2 * k * RIM : (2 * k + 1) * RIM, :] = high[at]
        out[(2 * k + 1) * RIM : (2 * k + 2) * RIM, :] = low[at]


def inner_copy(buf, out, sems, c):
    at = pl.ds(pl.multiple_of(c * (CX // CHUNKS), CX // CHUNKS), CX // CHUNKS)
    inner = pl.ds(8, CY - 16)
    return pltpu.make_async_copy(buf.at[at, inner, :], out.at[at, inner, :], sems.at[c])


def finish_kernel(field, wfin, shape, rxlo, rxhi, after, out, rims, buf, sems):
    per = BLOCKS // CHUNKS

    def block(k, extra):
        data = jnp.concatenate([tile(field, k, ROWS), tile(shape, k, 2 * RIM)], 0)
        total = dot(wfin[...], data)
        if extra is not None:
            total = total + extra[:OWN, :].astype(f32)
        total = total.reshape(GX, CY, NZ)
        planes = pl.ds(pl.multiple_of(k * GX, GX), GX)
        buf[planes, :, :] = total
        rims[planes, :8, :] = total[:, :8]
        rims[planes, 8:, :] = total[:, CY - 8 :]

    def step(c, carry):
        for b in range(per):
            block(c * per + b, None)
        inner_copy(buf, out, sems, c).start()
        return carry

    for b in range(per):
        block(b, rxlo if b == 0 else None)
    inner_copy(buf, out, sems, 0).start()
    lax.fori_loop(1, CHUNKS - 1, step, 0, unroll=2)
    for b in range(per):
        block(BLOCKS - per + b, rxhi if b == per - 1 else None)
    inner_copy(buf, out, sems, CHUNKS - 1).start()
    for c in range(CHUNKS):
        inner_copy(buf, out, sems, c).wait()


def finish(*args):
    return call(
        finish_kernel,
        (sds((CX, CY, NZ), f32), sds((CX, 16, NZ), f32)),
        [VM] * 5 + [ANY],
        16,
        out_specs=(HBM, VM),
        scratch=[pltpu.VMEM((CX, CY, NZ), f32), pltpu.SemaphoreType.DMA((CHUNKS,))],
    )(*args)


def combine_kernel(partial, rims, spread, rylo, ryhi, cornlo, cornhi, out, buf, sems):
    planes = CX // CHUNKS
    per = BLOCKS // CHUNKS

    def copies(c):
        at = pl.ds(c * planes, planes)
        return [
            pltpu.make_async_copy(
                buf.at[at, pl.ds(8 * i, 8), :], out.at[at, pl.ds(i * (CY - 8), 8), :],
                sems.at[2 * c + i],
            )
            for i in range(2)
        ]

    for c in range(CHUNKS):
        for b in range(per):
            k = c * per + b
            rim = slice(k * RIM, (k + 1) * RIM)
            data = jnp.concatenate([rylo[rim, :], ryhi[rim, :]], 0)
            strips = dot(spread[...], data)
            if k in (0, BLOCKS - 1):
                at = slice(0, RIM) if k == 0 else slice(RIM, 2 * RIM)
                data = jnp.concatenate([cornlo[at, :], cornhi[at, :]], 0)
                strips = strips + dot(spread[...], data)
            strips = strips.reshape(GX, 16, NZ)
            at = slice(k * GX, (k + 1) * GX)
            buf[at] = rims[at] + strips
        for copy in copies(c):
            copy.start()
    for c in range(CHUNKS):
        for copy in copies(c):
            copy.wait()


def combine(*args):
    return pl.pallas_call(
        combine_kernel,
        out_shape=sds((CX, CY, NZ), f32),
        in_specs=[HBM] + [VM] * 6,
        out_specs=HBM,
        scratch_shapes=[pltpu.VMEM((CX, 16, NZ), f32), pltpu.SemaphoreType.DMA((2 * CHUNKS,))],
        input_output_aliases={0: 0},
        compiler_params=pltpu.CompilerParams(vmem_limit_bytes=16 << 20),
        name="combine",
    )(*args)


def shift(x, axis, step):
    size = lax.axis_size(axis)
    return lax.ppermute(x, axis, [(i, (i + step) % size) for i in range(size)])


def exchange(x, axis):
    return lax.all_to_all(x, axis, 0, 0)


def local(
    residual, local_x, local_y, local_z, eig_x, eig_y, eig_z, coarse_x, coarse_y, coarse_z,
    mode_x, mode_y, mode_z, coarse_eig_x, coarse_eig_y, coarse_eig_z,
):
    cells = residual.reshape(CELLS, NZ)
    first_x, last_x, rim_lo, rim_hi, along_y, sel = load(cells, coarse_y)
    xlo = shift(last_x, "gx", 1)
    xhi = shift(first_x, "gx", -1)
    own_coarse, modes_xz = call(
        restrict_kernel, (sds((8, MODES, 16), f32), sds((128, 128), f32)), [VM] * 5, 8
    )(along_y, coarse_x.T, coarse_z.T, mode_x, mode_z)
    rows = exchange(own_coarse, "gx")
    down, up = corners(sel, rim_lo, rim_hi, xlo, xhi, own_coarse)
    ylo = shift(up, "gy", 1)
    yhi = shift(down, "gy", -1)
    part = call(coarse_x_kernel, sds((32, MODES, 128), f32), [VM] * 2, 4)(rows, modes_xz)
    rows = exchange(part, "gy")

    wy, wyt, wfin, spread, wx, wxt, lz, lzt, exb, eyz = prepare(
        local_x, local_y, local_z, eig_x[None], eig_y[None], eig_z[None], coarse_y.T, part
    )
    field, out_xlo, out_xhi, out_ylo, out_yhi = solve(
        cells, xlo, xhi, ylo, yhi, wy, wyt, wx, wxt, lz, lzt, exb, eyz, part
    )

    rylo = shift(out_yhi, "gy", 1)
    ryhi = shift(out_ylo, "gy", -1)
    rxlo = shift(out_xhi, "gx", 1)
    rxhi = shift(out_xlo, "gx", -1)
    down, up = turn(rxlo, rxhi)
    cornlo = shift(up, "gy", 1)
    cornhi = shift(down, "gy", -1)
    far = [
        pltpu.with_memory_space_constraint(x, pltpu.HBM)
        for x in (
            mode_y, coarse_eig_x[None], coarse_eig_y[None], coarse_eig_z[None], coarse_x.T,
            coarse_z.T,
        )
    ]
    shape = call(
        coarse_kernel,
        sds((2 * CX * MODES, NZ), bf16),
        [VM] * 2 + [HBM] * len(far) + [ANY],
        8,
        scratch=[pltpu.VMEM(*c) for c in COARSE] + [pltpu.SemaphoreType.DMA((len(COARSE),))],
    )(rows, modes_xz, *far, out_ylo)
    partial, rims = finish(field, wfin, shape, rxlo, rxhi, up)
    return combine(partial, rims, spread, rylo, ryhi, cornlo, cornhi)


def solution(mesh):
    cells = P("gx", "gy", None)

    return jax.shard_map(
        local, mesh=mesh, in_specs=(cells,) + (P(),) * 15, out_specs=cells, check_vma=False
    )
```

```python
import jax
import jax.numpy as jnp
from jax import lax
from jax.experimental import pallas as pl
from jax.experimental.pallas import tpu as pltpu
from jax.sharding import PartitionSpec as P


OV = 4
MODES = 4
CX = 128
CY = 32
NZ = 256
EX = 136
EY = 40
GX = 4
ROWS = GX * EY
OWN = GX * CY
RIM = GX * OV
BLOCKS = CX // GX
CELLS = CX * CY
CHUNKS = 8
WIDE_LOAD = 50
WIDE_SOLVE = 48
HI = lax.Precision.HIGHEST
f32 = jnp.float32
bf16 = jnp.bfloat16
sds = jax.ShapeDtypeStruct

VM = pl.BlockSpec(memory_space=pltpu.VMEM)
SM = pl.BlockSpec(memory_space=pltpu.SMEM)
ANY = pl.BlockSpec(memory_space=pl.ANY)
HBM = pl.BlockSpec(memory_space=pltpu.HBM)


def dot(a, b):
    return jnp.dot(a, b, preferred_element_type=f32)


def dot_t(a, b):
    return lax.dot_general(a, b, (((1,), (1,)), ((), ())), preferred_element_type=f32)


def dot_hi(a, b):
    return jnp.dot(a, b, preferred_element_type=f32, precision=HI)


def dot_t_hi(a, b):
    dims = (((1,), (1,)), ((), ()))
    return lax.dot_general(a, b, dims, preferred_element_type=f32, precision=HI)


def split(x):
    high = x.astype(bf16)
    return high, (x - high.astype(f32)).astype(bf16)


def split3(x):
    high = x.astype(bf16)
    rest = x - high.astype(f32)
    middle = rest.astype(bf16)
    return high, middle, (rest - middle.astype(f32)).astype(bf16)


def expand(x, rows=None, cols=None):
    parts = split3(x)
    if rows is not None:
        return dot(jnp.concatenate([rows] * 3, 1), jnp.concatenate(parts, 0))
    return dot(jnp.concatenate(parts, 1), jnp.concatenate([cols] * 3, 0))


def iotas(shape):
    return lax.broadcasted_iota(jnp.int32, shape, 0), lax.broadcasted_iota(jnp.int32, shape, 1)


def pick(mask, kind=bf16):
    return jnp.where(mask, 1.0, 0.0).astype(kind)


def call(kernel, out_shape, in_specs, mib, out_specs=None, scratch=()):
    if out_specs is None:
        out_specs = jax.tree.map(lambda _: VM, out_shape)
    return pl.pallas_call(
        kernel,
        out_shape=out_shape,
        in_specs=in_specs,
        out_specs=out_specs,
        scratch_shapes=list(scratch),
        compiler_params=pltpu.CompilerParams(vmem_limit_bytes=mib << 20),
    )


def tile(ref, k, rows):
    return ref[pl.ds(pl.multiple_of(k * rows, rows), rows), :]


def selection(cyt):
    row, col = iotas((3 * RIM, OWN))
    y, k = iotas((CY, OWN))
    spread = dot(cyt, pick((k & 31) == y)).astype(bf16)
    row4, n = iotas((3 * RIM, MODES))
    modes = dot(pick((row4 & 3) == n), spread)
    plane = ((row >> 2) & 3) == (col >> 5)
    inner = col & 31
    target = jnp.where(row < RIM, row & 3, CY - OV + (row & 3))
    ones = jnp.where(inner == target, 1.0, 0.0)
    value = jnp.where(row < 2 * RIM, ones, modes)
    return jnp.where(plane, value, 0.0).astype(bf16)


def load_kernel(
    residual, cyt, first_x, last_x, rim_lo, rim_hi, along_y, sel, buf, sems, cyt_buf, sem
):
    rows = CELLS // CHUNKS

    def copy(c):
        at = pl.ds(c * rows, rows)
        return pltpu.make_async_copy(residual.at[at, :], buf.at[at, :], sems.at[c])

    small = pltpu.make_async_copy(cyt, cyt_buf, sem)
    small.start()
    for c in range(CHUNKS):
        copy(c).start()
    small.wait()
    take = selection(cyt_buf[...])
    sel[...] = take
    for c in range(CHUNKS):
        copy(c).wait()
        for b in range(rows // OWN):
            k = c * (rows // OWN) + b
            data = buf[k * OWN : (k + 1) * OWN, :].astype(bf16)
            if k == 0:
                first_x[...] = data
            if k == BLOCKS - 1:
                last_x[...] = data
            out = dot(take, data)
            at = slice(k * RIM, (k + 1) * RIM)
            rim_lo[at, :] = out[:RIM].astype(bf16)
            rim_hi[at, :] = out[RIM : 2 * RIM].astype(bf16)
            along_y[at, :] = out[2 * RIM :]


def load(residual, coarse_y):
    rim = sds((CX * OV, NZ), bf16)
    return call(
        load_kernel,
        (
            sds((OWN, NZ), bf16), sds((OWN, NZ), bf16), rim, rim,
            sds((CX * MODES, NZ), f32), sds((3 * RIM, OWN), bf16),
        ),
        [HBM, HBM],
        WIDE_LOAD,
        scratch=[
            pltpu.VMEM((CELLS, NZ), f32), pltpu.SemaphoreType.DMA((CHUNKS,)),
            pltpu.VMEM((MODES, CY), bf16), pltpu.SemaphoreType.DMA,
        ],
    )(residual, pltpu.with_memory_space_constraint(coarse_y.T, pltpu.HBM))


def corners_kernel(sel, rim_lo, rim_hi, xlo, xhi, after, down, up):
    down[: CX * OV, :] = rim_lo[...]
    up[: CX * OV, :] = rim_hi[...]
    for i, strip in enumerate((xlo, xhi)):
        out = dot(sel[: 2 * RIM, :], strip[...]).astype(bf16)
        at = slice(CX * OV + i * RIM, CX * OV + (i + 1) * RIM)
        down[at, :] = out[:RIM]
        up[at, :] = out[RIM:]


def corners(*args):
    side = sds((EX * OV, NZ), bf16)
    return call(corners_kernel, (side, side), [VM] * 5 + [ANY], 8)(*args)


PARAMS = (
    ((EX, EX), bf16), ((EY, EY), bf16), ((NZ, NZ), bf16), ((1, EX), f32), ((1, EY), f32),
    ((1, NZ), f32), ((MODES, CY), bf16),
)
WEIGHTS = (
    ((ROWS, ROWS), bf16), ((ROWS, ROWS), bf16), ((OWN, ROWS + 2 * RIM), bf16),
    ((OWN // 2, 2 * RIM), bf16), ((EX, EX), bf16),
    ((EX, EX), bf16), ((NZ, NZ), bf16), ((NZ, NZ), bf16), ((EX, NZ), f32), ((EY, NZ), f32),
)


def basis_x(cxt):
    x, row = iotas((CX, CX * MODES))
    by_row = dot(cxt, pick((row >> 2) == x)).astype(bf16)
    col, m = iotas((16, MODES))
    value = dot(pick((col >> 2) == m), by_row)
    col, row = iotas((16, CX * MODES))
    return jnp.where((row & 3) == (col & 3), value, 0.0).astype(bf16)


def spread_z(mode_z):
    row, col = iotas((128, 128))
    out = jnp.zeros((128, 128), f32)
    for p in range(MODES):
        for c in range(MODES):
            here = ((row & 3) == p) & ((col & 3) == c)
            out = jnp.where(here, mode_z[p : p + 1, c : c + 1], out)
    return out


def modes_a():
    a, col = iotas((32, 128))
    c, col4 = iotas((MODES, 128))
    return pick((col >> 2) == a), pick((col4 & 3) == c)


def prepare_kernel(*refs):
    n = len(PARAMS)
    bufs, outs = refs[:n], refs[n + 1 :]
    lx, ly, lz, eig_x, eig_y, eig_z, cyt = bufs
    wy, wyt, wfin, spread, wx, wxt, lz_out, lzt, exb, eyz = outs

    def cell(k):
        y = jnp.where(k < OWN, OV + (k & 31), jnp.where(k < OWN + RIM, k & 3, EY - OV + (k & 3)))
        plane = jnp.where(k < OWN, k >> 5, ((k - OWN) >> 2) & 3)
        return y, plane

    def mode(j):
        plane = (j >= EY).astype(jnp.int32) + (j >= 2 * EY) + (j >= 3 * EY)
        return j - EY * plane, plane

    k, y = iotas((ROWS, EY))
    by_cell = dot(pick(cell(k)[0] == y), ly[...]).astype(bf16)
    b, j = iotas((EY, ROWS))
    k, col = iotas((ROWS, ROWS))
    value = dot(by_cell, pick(mode(j)[0] == b))
    value = jnp.where(cell(k)[1] == mode(col)[1], value, 0.0).astype(bf16)
    wyt[...] = value
    j, b = iotas((ROWS, EY))
    back = dot_t(pick(mode(j)[0] == b), by_cell)
    wy[...] = jnp.where(mode(k)[1] == cell(col)[1], back, 0.0).astype(bf16)

    y, k = iotas((CY, OWN))
    by_k = dot(cyt[...], pick((k & 31) == y)).astype(bf16)
    k, own = iotas((OWN, OWN))
    turned = dot_t(pick(k == own), by_k).astype(bf16)
    n, col = iotas((MODES, 2 * RIM))
    coarse = dot(turned, pick((col & 3) == n))
    k, col = iotas((OWN, 2 * RIM))
    inner = k & 31
    plane = (k >> 5) == ((col >> 2) & 3)
    coarse = jnp.where(plane, coarse, 0.0).astype(bf16)
    wfin[...] = jnp.concatenate([value[:OWN], coarse], 1)
    k, col = iotas((OWN // 2, 2 * RIM))
    inner = (k & 15) + jnp.where((k & 15) < 8, 0, CY - 16)
    target = jnp.where(col < RIM, col & 3, CY - OV + (col & 3))
    ones = jnp.where(inner == target, 1.0, 0.0)
    spread[...] = jnp.where((k >> 4) == ((col >> 2) & 3), ones, 0.0).astype(bf16)

    k, x = iotas((EX, EX))
    source = jnp.where(k < CX, k + OV, jnp.where(k < CX + OV, k - CX, k))
    moved = dot(pick(source == x), lx[...]).astype(bf16)
    wxt[...] = moved
    wx[...] = dot_t(pick(k == x), moved).astype(bf16)
    column = jnp.sum(jnp.where(k == x, eig_x[...], 0.0), axis=1, keepdims=True)
    exb[...] = jnp.broadcast_to(column, (EX, NZ))
    b, y = iotas((EY, EY))
    column = jnp.sum(jnp.where(b == y, eig_y[...], 0.0), axis=1, keepdims=True)
    eyz[...] = column + eig_z[...]
    c, z = iotas((NZ, NZ))
    lz_out[...] = lz[...]
    lzt[...] = dot_t(pick(c == z), lz[...]).astype(bf16)


def prepare(*params):
    return call(
        prepare_kernel, tuple(sds(*w) for w in WEIGHTS), [VM] * len(PARAMS) + [ANY], 8
    )(*params)


def solve_kernel(
    residual, xlo, xhi, ylo, yhi, wy, wyt, wx, wxt, lz, lzt, exb, eyz, after,
    kept, out_xlo, out_xhi, out_ylo, out_yhi, field, mid, spec, buf, sems,
):
    def put(rows, value):
        field[0, rows, :] = value[:, :128]
        field[1, rows, :] = value[:, 128:]

    def take(rows):
        return jnp.concatenate([field[0, rows, :], field[1, rows, :]], 1)

    def forward_y(main, k):
        data = jnp.concatenate([main, tile(ylo, k, RIM), tile(yhi, k, RIM)], 0)
        put(pl.ds(pl.multiple_of(k * ROWS, ROWS), ROWS), dot(wy[...], data))

    rows = CELLS // CHUNKS
    per = BLOCKS // CHUNKS

    def copy(c):
        at = pl.ds(pl.multiple_of(c * rows, rows), rows)
        return pltpu.make_async_copy(residual.at[at, :], buf.at[at, :], sems.at[c])

    for c in range(CHUNKS):
        copy(c).start()

    def first(c, carry):
        for i in range(2):
            copy(2 * c + i).wait()
        for b in range(2 * per):
            k = c * 2 * per + b
            forward_y(tile(buf, k, OWN).astype(bf16), k)
        return carry

    lax.fori_loop(0, CHUNKS // 2, first, 0)
    forward_y(xlo[...], BLOCKS)
    forward_y(xhi[...], BLOCKS + 1)

    def mid_rows(b):
        return pl.ds(pl.multiple_of(b * EX, 8), EX)

    def forward_x(b, carry):
        plane = take(pl.ds(b, EX, stride=EY)).astype(bf16)
        mid[mid_rows(b), :] = dot(wx[...], plane)
        return carry

    lax.fori_loop(0, EY, forward_x, 0, unroll=40)

    def forward_z(i, carry):
        at = pl.ds(pl.multiple_of(i * 4 * EX, 16), 4 * EX)
        along = dot(mid[at, :].astype(bf16), lz[...])
        parts = []
        for q in range(4):
            scale = exb[...] + eyz[pl.ds(i * 4 + q, 1), :]
            parts.append((along[q * EX : (q + 1) * EX] / scale))
        spec[at, :] = jnp.concatenate(parts, 0).astype(bf16)
        return carry

    lax.fori_loop(0, EY // 4, forward_z, 0, unroll=10)

    def backward_z(i, carry):
        at = pl.ds(pl.multiple_of(i * 4 * EX, 16), 4 * EX)
        mid[at, :] = dot(spec[at, :], lzt[...])
        return carry

    lax.fori_loop(0, EY // 4, backward_z, 0, unroll=10)

    def backward_x(b, carry):
        put(pl.ds(b, EX, stride=EY), dot(wxt[...], mid[mid_rows(b), :].astype(bf16)))
        return carry

    lax.fori_loop(0, EY, backward_x, 0, unroll=40)

    def planes(k):
        return take(pl.ds(pl.multiple_of(k * ROWS, ROWS), ROWS)).astype(bf16)

    out_xlo[...] = dot(wyt[...], planes(BLOCKS)).astype(bf16)
    out_xhi[...] = dot(wyt[...], planes(BLOCKS + 1)).astype(bf16)

    def last(k, carry):
        data = planes(k)
        kept[pl.ds(pl.multiple_of(k * ROWS, ROWS), ROWS), :] = data
        out = dot(wyt[OWN:, :], data).astype(bf16)
        at = pl.ds(pl.multiple_of(k * RIM, RIM), RIM)
        out_ylo[at, :] = out[:RIM]
        out_yhi[at, :] = out[RIM:]
        return carry

    lax.fori_loop(0, BLOCKS, last, 0, unroll=16)


def solve(*args):
    strip = sds((ROWS, NZ), bf16)
    rim = sds((CX * OV, NZ), bf16)
    return call(
        solve_kernel,
        (sds((BLOCKS * ROWS, NZ), bf16), strip, strip, rim, rim),
        [HBM] + [VM] * 12 + [ANY],
        WIDE_SOLVE,
        scratch=[
            pltpu.VMEM((2, EX * EY, NZ // 2), f32), pltpu.VMEM((EX * EY, NZ), f32),
            pltpu.VMEM((EX * EY, NZ), bf16), pltpu.VMEM((CELLS, NZ), f32),
            pltpu.SemaphoreType.DMA((CHUNKS,)),
        ],
    )(*args)


def turn_kernel(rxlo, rxhi, after, down, up):
    for start, out in ((OWN, down), (OWN + RIM, up)):
        out[:RIM, :] = rxlo[start : start + RIM, :]
        out[RIM:, :] = rxhi[start : start + RIM, :]


def turn(*args):
    both = sds((2 * RIM, NZ), bf16)
    return call(turn_kernel, (both, both), [VM] * 2 + [ANY], 4)(*args)


def restrict_kernel(along_y, cxt, czt, mode_x, mode_z, out, modes_xz):
    bx = basis_x(cxt[...])
    high, low = split(along_y[...])
    both = dot(bx, high) + dot(bx, low)
    own = dot_t_hi(both, czt[...].astype(f32))
    flat = jnp.concatenate([own[m * MODES : (m + 1) * MODES] for m in range(MODES)], 1)
    for i in range(out.shape[0]):
        out[i] = flat
    to_a, _ = modes_a()
    r, i = iotas((128, 32))
    part_x = expand(expand(mode_x[...], rows=pick((r >> 2) == i)), cols=to_a)
    part_z = spread_z(mode_z[...])
    modes_xz[...] = part_x * part_z


def coarse_x_kernel(rows, modes_xz, out):
    part = dot_hi(jnp.concatenate([rows[i] for i in range(8)], 1), modes_xz[...])
    for i in range(out.shape[0]):
        out[i] = part


COARSE = (
    ((128, 128), f32), ((1, 32), f32), ((1, 128), f32), ((1, MODES), f32), ((MODES, CX), bf16),
    ((MODES, NZ), bf16),
)


def coarse_kernel(rows, modes_xz, *refs):
    n = len(COARSE)
    sources, out, bufs, sems = refs[:n], refs[n + 1], refs[n + 2 : -1], refs[-1]
    copies = [
        pltpu.make_async_copy(source, buf, sems.at[i])
        for i, (source, buf) in enumerate(zip(sources, bufs))
    ]
    for copy in copies:
        copy.start()
    for copy in copies:
        copy.wait()
    mode_y, ceig_x, ceig_y, ceig_z, cxt, czt = bufs
    to_a, to_c = modes_a()
    eight_x = jnp.broadcast_to(ceig_x[...], (8, 32))
    eight_z = jnp.broadcast_to(ceig_z[...], (8, MODES))
    row = (dot_hi(eight_x, to_a.astype(f32)) + dot_hi(eight_z, to_c.astype(f32)))[:1]
    r, b = iotas((128, 128))
    column = jnp.sum(jnp.where(r == b, ceig_y[...], 0.0), axis=1, keepdims=True)
    columns = jnp.concatenate([rows[j] for j in range(rows.shape[0])], 0)
    hat = dot_hi(mode_y[...].T, columns) / (column + row)
    row, col = iotas((8, 128))
    mine = pick(col == lax.axis_index("gy") * MODES + row, f32)
    rows_y = dot_hi(mine, mode_y[...])
    rows_xz = modes_xz[pl.ds(pl.multiple_of(lax.axis_index("gx") * 16, 16), 16), :]
    sol = dot_t_hi(dot_hi(rows_y, hat), rows_xz)
    levels = czt[...].astype(f32)
    shape = jnp.concatenate(
        [dot_hi(sol[:, m * MODES : (m + 1) * MODES], levels)[:MODES] for m in range(MODES)], 0
    )
    high, low = split(shape)
    col, i = iotas((32, 16))
    twice = dot(pick((col & 15) == i), basis_x(cxt[...]))
    value = dot(twice.T.astype(bf16), jnp.concatenate([high, low], 0))
    high, low = split(value)
    for k in range(BLOCKS):
        at = slice(k * RIM, (k + 1) * RIM)
        out[2 * k * RIM : (2 * k + 1) * RIM, :] = high[at]
        out[(2 * k + 1) * RIM : (2 * k + 2) * RIM, :] = low[at]


def inner_copy(buf, out, sems, c):
    at = pl.ds(pl.multiple_of(c * (CX // CHUNKS), CX // CHUNKS), CX // CHUNKS)
    inner = pl.ds(8, CY - 16)
    return pltpu.make_async_copy(buf.at[at, inner, :], out.at[at, inner, :], sems.at[c])


def finish_kernel(field, wfin, shape, rxlo, rxhi, after, out, rims, buf, sems):
    per = BLOCKS // CHUNKS

    def block(k, extra):
        data = jnp.concatenate([tile(field, k, ROWS), tile(shape, k, 2 * RIM)], 0)
        total = dot(wfin[...], data)
        if extra is not None:
            total = total + extra[:OWN, :].astype(f32)
        total = total.reshape(GX, CY, NZ)
        planes = pl.ds(pl.multiple_of(k * GX, GX), GX)
        buf[planes, :, :] = total
        rims[planes, :8, :] = total[:, :8]
        rims[planes, 8:, :] = total[:, CY - 8 :]

    def step(c, carry):
        for b in range(per):
            block(c * per + b, None)
        inner_copy(buf, out, sems, c).start()
        return carry

    for b in range(per):
        block(b, rxlo if b == 0 else None)
    inner_copy(buf, out, sems, 0).start()
    lax.fori_loop(1, CHUNKS - 1, step, 0, unroll=2)
    for b in range(per):
        block(BLOCKS - per + b, rxhi if b == per - 1 else None)
    inner_copy(buf, out, sems, CHUNKS - 1).start()
    for c in range(CHUNKS):
        inner_copy(buf, out, sems, c).wait()


def finish(*args):
    return call(
        finish_kernel,
        (sds((CX, CY, NZ), f32), sds((CX, 16, NZ), f32)),
        [VM] * 5 + [ANY],
        16,
        out_specs=(HBM, VM),
        scratch=[pltpu.VMEM((CX, CY, NZ), f32), pltpu.SemaphoreType.DMA((CHUNKS,))],
    )(*args)


def combine_kernel(partial, rims, spread, rylo, ryhi, cornlo, cornhi, out, buf, sems):
    planes = CX // CHUNKS
    per = BLOCKS // CHUNKS

    def copies(c):
        at = pl.ds(c * planes, planes)
        return [
            pltpu.make_async_copy(
                buf.at[at, pl.ds(8 * i, 8), :], out.at[at, pl.ds(i * (CY - 8), 8), :],
                sems.at[2 * c + i],
            )
            for i in range(2)
        ]

    for c in range(CHUNKS):
        for b in range(per):
            k = c * per + b
            rim = slice(k * RIM, (k + 1) * RIM)
            data = jnp.concatenate([rylo[rim, :], ryhi[rim, :]], 0)
            strips = dot(spread[...], data)
            if k in (0, BLOCKS - 1):
                at = slice(0, RIM) if k == 0 else slice(RIM, 2 * RIM)
                data = jnp.concatenate([cornlo[at, :], cornhi[at, :]], 0)
                strips = strips + dot(spread[...], data)
            strips = strips.reshape(GX, 16, NZ)
            at = slice(k * GX, (k + 1) * GX)
            buf[at] = rims[at] + strips
        for copy in copies(c):
            copy.start()
    for c in range(CHUNKS):
        for copy in copies(c):
            copy.wait()


def combine(*args):
    return pl.pallas_call(
        combine_kernel,
        out_shape=sds((CX, CY, NZ), f32),
        in_specs=[HBM] + [VM] * 6,
        out_specs=HBM,
        scratch_shapes=[pltpu.VMEM((CX, 16, NZ), f32), pltpu.SemaphoreType.DMA((2 * CHUNKS,))],
        input_output_aliases={0: 0},
        compiler_params=pltpu.CompilerParams(vmem_limit_bytes=16 << 20),
        name="combine",
    )(*args)


def shift(x, axis, step):
    size = lax.axis_size(axis)
    return lax.ppermute(x, axis, [(i, (i + step) % size) for i in range(size)])


def exchange(x, axis):
    return lax.all_to_all(x, axis, 0, 0)


def local(
    residual, local_x, local_y, local_z, eig_x, eig_y, eig_z, coarse_x, coarse_y, coarse_z,
    mode_x, mode_y, mode_z, coarse_eig_x, coarse_eig_y, coarse_eig_z,
):
    cells = residual.reshape(CELLS, NZ)
    first_x, last_x, rim_lo, rim_hi, along_y, sel = load(cells, coarse_y)
    xlo = shift(last_x, "gx", 1)
    xhi = shift(first_x, "gx", -1)
    own_coarse, modes_xz = call(
        restrict_kernel, (sds((8, MODES, 16), f32), sds((128, 128), f32)), [VM] * 5, 8
    )(along_y, coarse_x.T, coarse_z.T, mode_x, mode_z)
    rows = exchange(own_coarse, "gx")
    down, up = corners(sel, rim_lo, rim_hi, xlo, xhi, own_coarse)
    ylo = shift(up, "gy", 1)
    yhi = shift(down, "gy", -1)
    part = call(coarse_x_kernel, sds((32, MODES, 128), f32), [VM] * 2, 4)(rows, modes_xz)
    rows = exchange(part, "gy")

    wy, wyt, wfin, spread, wx, wxt, lz, lzt, exb, eyz = prepare(
        local_x, local_y, local_z, eig_x[None], eig_y[None], eig_z[None], coarse_y.T, part
    )
    field, out_xlo, out_xhi, out_ylo, out_yhi = solve(
        cells, xlo, xhi, ylo, yhi, wy, wyt, wx, wxt, lz, lzt, exb, eyz, part
    )

    rylo = shift(out_yhi, "gy", 1)
    ryhi = shift(out_ylo, "gy", -1)
    rxlo = shift(out_xhi, "gx", 1)
    rxhi = shift(out_xlo, "gx", -1)
    far = [
        pltpu.with_memory_space_constraint(x, pltpu.HBM)
        for x in (
            mode_y, coarse_eig_x[None], coarse_eig_y[None], coarse_eig_z[None], coarse_x.T,
            coarse_z.T,
        )
    ]
    shape = call(
        coarse_kernel,
        sds((2 * CX * MODES, NZ), bf16),
        [VM] * 2 + [HBM] * len(far) + [ANY],
        8,
        scratch=[pltpu.VMEM(*c) for c in COARSE] + [pltpu.SemaphoreType.DMA((len(COARSE),))],
    )(rows, modes_xz, *far, out_ylo)
    down, up = turn(rxlo, rxhi, shape)
    cornlo = shift(up, "gy", 1)
    cornhi = shift(down, "gy", -1)
    partial, rims = finish(field, wfin, shape, rxlo, rxhi, up)
    return combine(partial, rims, spread, rylo, ryhi, cornlo, cornhi)


def solution(mesh):
    cells = P("gx", "gy", None)

    return jax.shard_map(
        local, mesh=mesh, in_specs=(cells,) + (P(),) * 15, out_specs=cells, check_vma=False
    )
```

```python
import jax
import jax.numpy as jnp
from jax import lax
from jax.experimental import pallas as pl
from jax.experimental.pallas import tpu as pltpu
from jax.sharding import PartitionSpec as P


OV = 4
MODES = 4
CX = 128
CY = 32
NZ = 256
EX = 136
EY = 40
GX = 4
ROWS = GX * EY
OWN = GX * CY
RIM = GX * OV
BLOCKS = CX // GX
CELLS = CX * CY
CHUNKS = 8
WIDE_LOAD = 50
WIDE_SOLVE = 48
HI = lax.Precision.HIGHEST
f32 = jnp.float32
bf16 = jnp.bfloat16
sds = jax.ShapeDtypeStruct

VM = pl.BlockSpec(memory_space=pltpu.VMEM)
SM = pl.BlockSpec(memory_space=pltpu.SMEM)
ANY = pl.BlockSpec(memory_space=pl.ANY)
HBM = pl.BlockSpec(memory_space=pltpu.HBM)


def dot(a, b):
    return jnp.dot(a, b, preferred_element_type=f32)


def dot_t(a, b):
    return lax.dot_general(a, b, (((1,), (1,)), ((), ())), preferred_element_type=f32)


def dot_hi(a, b):
    return jnp.dot(a, b, preferred_element_type=f32, precision=HI)


def dot_t_hi(a, b):
    dims = (((1,), (1,)), ((), ()))
    return lax.dot_general(a, b, dims, preferred_element_type=f32, precision=HI)


def split(x):
    high = x.astype(bf16)
    return high, (x - high.astype(f32)).astype(bf16)


def split3(x):
    high = x.astype(bf16)
    rest = x - high.astype(f32)
    middle = rest.astype(bf16)
    return high, middle, (rest - middle.astype(f32)).astype(bf16)


def expand(x, rows=None, cols=None):
    parts = split3(x)
    if rows is not None:
        return dot(jnp.concatenate([rows] * 3, 1), jnp.concatenate(parts, 0))
    return dot(jnp.concatenate(parts, 1), jnp.concatenate([cols] * 3, 0))


def iotas(shape):
    return lax.broadcasted_iota(jnp.int32, shape, 0), lax.broadcasted_iota(jnp.int32, shape, 1)


def pick(mask, kind=bf16):
    return jnp.where(mask, 1.0, 0.0).astype(kind)


def call(kernel, out_shape, in_specs, mib, out_specs=None, scratch=()):
    if out_specs is None:
        out_specs = jax.tree.map(lambda _: VM, out_shape)
    return pl.pallas_call(
        kernel,
        out_shape=out_shape,
        in_specs=in_specs,
        out_specs=out_specs,
        scratch_shapes=list(scratch),
        compiler_params=pltpu.CompilerParams(vmem_limit_bytes=mib << 20),
    )


def tile(ref, k, rows):
    return ref[pl.ds(pl.multiple_of(k * rows, rows), rows), :]


def selection(cyt):
    row, col = iotas((3 * RIM, OWN))
    modes = jnp.concatenate([cyt.astype(f32)] * GX, 1)
    modes = jnp.concatenate([jnp.concatenate([modes] * 2, 0)] * (3 * RIM // 8), 0)
    plane = ((row >> 2) & 3) == (col >> 5)
    inner = col & 31
    target = jnp.where(row < RIM, row & 3, CY - OV + (row & 3))
    ones = jnp.where(inner == target, 1.0, 0.0)
    value = jnp.where(row < 2 * RIM, ones, modes)
    return jnp.where(plane, value, 0.0).astype(bf16)


def load_kernel(
    residual, cyt, first_x, last_x, rim_lo, rim_hi, along_y, sel, buf, sems, cyt_buf, sem
):
    rows = CELLS // CHUNKS

    def copy(c):
        at = pl.ds(c * rows, rows)
        return pltpu.make_async_copy(residual.at[at, :], buf.at[at, :], sems.at[c])

    small = pltpu.make_async_copy(cyt, cyt_buf, sem)
    small.start()
    for c in range(CHUNKS):
        copy(c).start()
    small.wait()
    take = selection(cyt_buf[...])
    sel[...] = take
    for c in range(CHUNKS):
        copy(c).wait()
        for b in range(rows // OWN):
            k = c * (rows // OWN) + b
            data = buf[k * OWN : (k + 1) * OWN, :].astype(bf16)
            if k == 0:
                first_x[...] = data
            if k == BLOCKS - 1:
                last_x[...] = data
            out = dot(take, data)
            at = slice(k * RIM, (k + 1) * RIM)
            rim_lo[at, :] = out[:RIM].astype(bf16)
            rim_hi[at, :] = out[RIM : 2 * RIM].astype(bf16)
            along_y[at, :] = out[2 * RIM :]


def load(residual, coarse_y):
    rim = sds((CX * OV, NZ), bf16)
    return call(
        load_kernel,
        (
            sds((OWN, NZ), bf16), sds((OWN, NZ), bf16), rim, rim,
            sds((CX * MODES, NZ), f32), sds((3 * RIM, OWN), bf16),
        ),
        [HBM, HBM],
        WIDE_LOAD,
        scratch=[
            pltpu.VMEM((CELLS, NZ), f32), pltpu.SemaphoreType.DMA((CHUNKS,)),
            pltpu.VMEM((MODES, CY), bf16), pltpu.SemaphoreType.DMA,
        ],
    )(residual, pltpu.with_memory_space_constraint(coarse_y.T, pltpu.HBM))


def corners_kernel(sel, rim_lo, rim_hi, xlo, xhi, after, down, up):
    down[: CX * OV, :] = rim_lo[...]
    up[: CX * OV, :] = rim_hi[...]
    for i, strip in enumerate((xlo, xhi)):
        out = dot(sel[: 2 * RIM, :], strip[...]).astype(bf16)
        at = slice(CX * OV + i * RIM, CX * OV + (i + 1) * RIM)
        down[at, :] = out[:RIM]
        up[at, :] = out[RIM:]


def corners(*args):
    side = sds((EX * OV, NZ), bf16)
    return call(corners_kernel, (side, side), [VM] * 5 + [ANY], 8)(*args)


PARAMS = (
    ((EX, EX), bf16), ((EY, EY), bf16), ((NZ, NZ), bf16), ((1, EX), f32), ((1, EY), f32),
    ((1, NZ), f32), ((MODES, CY), bf16),
)
WEIGHTS = (
    ((ROWS, ROWS), bf16), ((ROWS, ROWS), bf16), ((OWN, ROWS + 2 * RIM), bf16),
    ((OWN // 2, 2 * RIM), bf16), ((EX, EX), bf16),
    ((EX, EX), bf16), ((NZ, NZ), bf16), ((NZ, NZ), bf16), ((EX, NZ), f32), ((EY, NZ), f32),
)


def basis_x(cxt):
    x, row = iotas((CX, CX * MODES))
    by_row = dot(cxt, pick((row >> 2) == x)).astype(bf16)
    col, m = iotas((16, MODES))
    value = dot(pick((col >> 2) == m), by_row)
    col, row = iotas((16, CX * MODES))
    return jnp.where((row & 3) == (col & 3), value, 0.0).astype(bf16)


def spread_z(mode_z):
    row, col = iotas((128, 128))
    out = jnp.zeros((128, 128), f32)
    for p in range(MODES):
        for c in range(MODES):
            here = ((row & 3) == p) & ((col & 3) == c)
            out = jnp.where(here, mode_z[p : p + 1, c : c + 1], out)
    return out


def modes_a():
    a, col = iotas((32, 128))
    c, col4 = iotas((MODES, 128))
    return pick((col >> 2) == a), pick((col4 & 3) == c)


def prepare_kernel(*refs):
    n = len(PARAMS)
    bufs, outs = refs[:n], refs[n + 1 :]
    lx, ly, lz, eig_x, eig_y, eig_z, cyt = bufs
    wy, wyt, wfin, spread, wx, wxt, lz_out, lzt, exb, eyz = outs

    def cell(k):
        y = jnp.where(k < OWN, OV + (k & 31), jnp.where(k < OWN + RIM, k & 3, EY - OV + (k & 3)))
        plane = jnp.where(k < OWN, k >> 5, ((k - OWN) >> 2) & 3)
        return y, plane

    def mode(j):
        plane = (j >= EY).astype(jnp.int32) + (j >= 2 * EY) + (j >= 3 * EY)
        return j - EY * plane, plane

    k, y = iotas((ROWS, EY))
    by_cell = dot(pick(cell(k)[0] == y), ly[...]).astype(bf16)
    b, j = iotas((EY, ROWS))
    k, col = iotas((ROWS, ROWS))
    value = dot(by_cell, pick(mode(j)[0] == b))
    value = jnp.where(cell(k)[1] == mode(col)[1], value, 0.0).astype(bf16)
    wyt[...] = value
    j, b = iotas((ROWS, EY))
    back = dot_t(pick(mode(j)[0] == b), by_cell)
    wy[...] = jnp.where(mode(k)[1] == cell(col)[1], back, 0.0).astype(bf16)

    y, k = iotas((CY, OWN))
    by_k = dot(cyt[...], pick((k & 31) == y)).astype(bf16)
    k, own = iotas((OWN, OWN))
    turned = dot_t(pick(k == own), by_k).astype(bf16)
    n, col = iotas((MODES, 2 * RIM))
    coarse = dot(turned, pick((col & 3) == n))
    k, col = iotas((OWN, 2 * RIM))
    inner = k & 31
    plane = (k >> 5) == ((col >> 2) & 3)
    coarse = jnp.where(plane, coarse, 0.0).astype(bf16)
    wfin[...] = jnp.concatenate([value[:OWN], coarse], 1)
    k, col = iotas((OWN // 2, 2 * RIM))
    inner = (k & 15) + jnp.where((k & 15) < 8, 0, CY - 16)
    target = jnp.where(col < RIM, col & 3, CY - OV + (col & 3))
    ones = jnp.where(inner == target, 1.0, 0.0)
    spread[...] = jnp.where((k >> 4) == ((col >> 2) & 3), ones, 0.0).astype(bf16)

    k, x = iotas((EX, EX))
    source = jnp.where(k < CX, k + OV, jnp.where(k < CX + OV, k - CX, k))
    moved = dot(pick(source == x), lx[...]).astype(bf16)
    wxt[...] = moved
    wx[...] = dot_t(pick(k == x), moved).astype(bf16)
    column = jnp.sum(jnp.where(k == x, eig_x[...], 0.0), axis=1, keepdims=True)
    exb[...] = jnp.broadcast_to(column, (EX, NZ))
    b, y = iotas((EY, EY))
    column = jnp.sum(jnp.where(b == y, eig_y[...], 0.0), axis=1, keepdims=True)
    eyz[...] = column + eig_z[...]
    c, z = iotas((NZ, NZ))
    lz_out[...] = lz[...]
    lzt[...] = dot_t(pick(c == z), lz[...]).astype(bf16)


def prepare(*params):
    return call(
        prepare_kernel, tuple(sds(*w) for w in WEIGHTS), [VM] * len(PARAMS) + [ANY], 8
    )(*params)


def solve_kernel(
    residual, xlo, xhi, ylo, yhi, wy, wyt, wx, wxt, lz, lzt, exb, eyz, after,
    kept, far_xlo, far_xhi, far_ylo, far_yhi, field, mid, spec, buf, sems,
    out_xlo, out_xhi, out_ylo, out_yhi, sems_out,
):
    def put(rows, value):
        field[0, rows, :] = value[:, :128]
        field[1, rows, :] = value[:, 128:]

    def take(rows):
        return jnp.concatenate([field[0, rows, :], field[1, rows, :]], 1)

    def forward_y(main, k):
        data = jnp.concatenate([main, tile(ylo, k, RIM), tile(yhi, k, RIM)], 0)
        put(pl.ds(pl.multiple_of(k * ROWS, ROWS), ROWS), dot(wy[...], data))

    rows = CELLS // CHUNKS
    per = BLOCKS // CHUNKS

    def copy(c):
        at = pl.ds(pl.multiple_of(c * rows, rows), rows)
        return pltpu.make_async_copy(residual.at[at, :], buf.at[at, :], sems.at[c])

    for c in range(CHUNKS):
        copy(c).start()

    def first(c, carry):
        for i in range(2):
            copy(2 * c + i).wait()
        for b in range(2 * per):
            k = c * 2 * per + b
            forward_y(tile(buf, k, OWN).astype(bf16), k)
        return carry

    lax.fori_loop(0, CHUNKS // 2, first, 0)
    forward_y(xlo[...], BLOCKS)
    forward_y(xhi[...], BLOCKS + 1)

    def mid_rows(b):
        return pl.ds(pl.multiple_of(b * EX, 8), EX)

    def forward_x(b, carry):
        plane = take(pl.ds(b, EX, stride=EY)).astype(bf16)
        mid[mid_rows(b), :] = dot(wx[...], plane)
        return carry

    lax.fori_loop(0, EY, forward_x, 0, unroll=40)

    def forward_z(i, carry):
        at = pl.ds(pl.multiple_of(i * 4 * EX, 16), 4 * EX)
        along = dot(mid[at, :].astype(bf16), lz[...])
        parts = []
        for q in range(4):
            scale = exb[...] + eyz[pl.ds(i * 4 + q, 1), :]
            parts.append((along[q * EX : (q + 1) * EX] / scale))
        spec[at, :] = jnp.concatenate(parts, 0).astype(bf16)
        return carry

    lax.fori_loop(0, EY // 4, forward_z, 0, unroll=10)

    def backward_z(i, carry):
        at = pl.ds(pl.multiple_of(i * 4 * EX, 16), 4 * EX)
        mid[at, :] = dot(spec[at, :], lzt[...])
        return carry

    lax.fori_loop(0, EY // 4, backward_z, 0, unroll=10)

    def backward_x(b, carry):
        put(pl.ds(b, EX, stride=EY), dot(wxt[...], mid[mid_rows(b), :].astype(bf16)))
        return carry

    lax.fori_loop(0, EY, backward_x, 0, unroll=40)

    def planes(k):
        return take(pl.ds(pl.multiple_of(k * ROWS, ROWS), ROWS)).astype(bf16)

    out_xlo[...] = dot(wyt[...], planes(BLOCKS)).astype(bf16)
    out_xhi[...] = dot(wyt[...], planes(BLOCKS + 1)).astype(bf16)

    def last(k, carry):
        data = planes(k)
        kept[pl.ds(pl.multiple_of(k * ROWS, ROWS), ROWS), :] = data
        out = dot(wyt[OWN:, :], data).astype(bf16)
        at = pl.ds(pl.multiple_of(k * RIM, RIM), RIM)
        out_ylo[at, :] = out[:RIM]
        out_yhi[at, :] = out[RIM:]
        return carry

    copies = [
        pltpu.make_async_copy(out_xlo, far_xlo, sems_out.at[0]),
        pltpu.make_async_copy(out_xhi, far_xhi, sems_out.at[1]),
    ]
    for copy in copies:
        copy.start()
    half = BLOCKS // 2
    for i in range(2):
        lax.fori_loop(i * half, (i + 1) * half, last, 0, unroll=half)
        at = pl.ds(i * half * RIM, half * RIM)
        for j, (near, far) in enumerate(((out_ylo, far_ylo), (out_yhi, far_yhi))):
            sem = sems_out.at[2 + 2 * i + j]
            copy = pltpu.make_async_copy(near.at[at, :], far.at[at, :], sem)
            copy.start()
            copies.append(copy)
    for copy in copies:
        copy.wait()


def solve(*args):
    strip = sds((ROWS, NZ), bf16)
    rim = sds((CX * OV, NZ), bf16)
    return call(
        solve_kernel,
        (sds((BLOCKS * ROWS, NZ), bf16), strip, strip, rim, rim),
        [HBM] + [VM] * 12 + [ANY],
        WIDE_SOLVE,
        out_specs=(VM, ANY, ANY, ANY, ANY),
        scratch=[
            pltpu.VMEM((2, EX * EY, NZ // 2), f32), pltpu.VMEM((EX * EY, NZ), f32),
            pltpu.VMEM((EX * EY, NZ), bf16), pltpu.VMEM((CELLS, NZ), f32),
            pltpu.SemaphoreType.DMA((CHUNKS,)), pltpu.VMEM((ROWS, NZ), bf16),
            pltpu.VMEM((ROWS, NZ), bf16), pltpu.VMEM((CX * OV, NZ), bf16),
            pltpu.VMEM((CX * OV, NZ), bf16), pltpu.SemaphoreType.DMA((6,)),
        ],
    )(*args)


def turn_kernel(rxlo, rxhi, after, down, up):
    for start, out in ((OWN, down), (OWN + RIM, up)):
        out[:RIM, :] = rxlo[start : start + RIM, :]
        out[RIM:, :] = rxhi[start : start + RIM, :]


def turn(*args):
    both = sds((2 * RIM, NZ), bf16)
    return call(turn_kernel, (both, both), [VM] * 2 + [ANY], 4)(*args)


def restrict_kernel(along_y, cxt, czt, out):
    bx = basis_x(cxt[...])
    high, low = split(along_y[...])
    both = dot(bx, high) + dot(bx, low)
    own = dot_t_hi(both, czt[...].astype(f32))
    flat = jnp.concatenate([own[m * MODES : (m + 1) * MODES] for m in range(MODES)], 1)
    for i in range(out.shape[0]):
        out[i] = flat


def modes_kernel(mode_x, mode_z, after, modes_xz):
    to_a, _ = modes_a()
    r, i = iotas((128, 32))
    part_x = expand(expand(mode_x[...], rows=pick((r >> 2) == i)), cols=to_a)
    part_z = spread_z(mode_z[...])
    modes_xz[...] = part_x * part_z


def coarse_x_kernel(rows, modes_xz, out):
    part = dot_hi(jnp.concatenate([rows[i] for i in range(8)], 1), modes_xz[...])
    for i in range(out.shape[0]):
        out[i] = part


COARSE = (
    ((128, 128), f32), ((1, 32), f32), ((1, 128), f32), ((1, MODES), f32), ((MODES, CX), bf16),
    ((MODES, NZ), bf16),
)


def coarse_kernel(rows, modes_xz, *refs):
    n = len(COARSE)
    sources, out, bufs, sems = refs[:n], refs[n + 1], refs[n + 2 : -1], refs[-1]
    copies = [
        pltpu.make_async_copy(source, buf, sems.at[i])
        for i, (source, buf) in enumerate(zip(sources, bufs))
    ]
    for copy in copies:
        copy.start()
    for copy in copies:
        copy.wait()
    mode_y, ceig_x, ceig_y, ceig_z, cxt, czt = bufs
    to_a, to_c = modes_a()
    eight_x = jnp.broadcast_to(ceig_x[...], (8, 32))
    eight_z = jnp.broadcast_to(ceig_z[...], (8, MODES))
    row = (dot_hi(eight_x, to_a.astype(f32)) + dot_hi(eight_z, to_c.astype(f32)))[:1]
    r, b = iotas((128, 128))
    column = jnp.sum(jnp.where(r == b, ceig_y[...], 0.0), axis=1, keepdims=True)
    columns = jnp.concatenate([rows[j] for j in range(rows.shape[0])], 0)
    hat = dot_hi(mode_y[...].T, columns) / (column + row)
    row, col = iotas((8, 128))
    mine = pick(col == lax.axis_index("gy") * MODES + row, f32)
    rows_y = dot_hi(mine, mode_y[...])
    rows_xz = modes_xz[pl.ds(pl.multiple_of(lax.axis_index("gx") * 16, 16), 16), :]
    sol = dot_t_hi(dot_hi(rows_y, hat), rows_xz)
    levels = czt[...].astype(f32)
    shape = jnp.concatenate(
        [dot_hi(sol[:, m * MODES : (m + 1) * MODES], levels)[:MODES] for m in range(MODES)], 0
    )
    high, low = split(shape)
    col, i = iotas((32, 16))
    twice = dot(pick((col & 15) == i), basis_x(cxt[...]))
    value = dot(twice.T.astype(bf16), jnp.concatenate([high, low], 0))
    high, low = split(value)
    for k in range(BLOCKS):
        at = slice(k * RIM, (k + 1) * RIM)
        out[2 * k * RIM : (2 * k + 1) * RIM, :] = high[at]
        out[(2 * k + 1) * RIM : (2 * k + 2) * RIM, :] = low[at]


def inner_copy(buf, out, sems, c):
    at = pl.ds(pl.multiple_of(c * (CX // CHUNKS), CX // CHUNKS), CX // CHUNKS)
    inner = pl.ds(8, CY - 16)
    return pltpu.make_async_copy(buf.at[at, inner, :], out.at[at, inner, :], sems.at[c])


def finish_kernel(field, wfin, shape, rxlo, rxhi, after, out, rims, buf, sems):
    per = BLOCKS // CHUNKS

    def block(k, extra):
        data = jnp.concatenate([tile(field, k, ROWS), tile(shape, k, 2 * RIM)], 0)
        total = dot(wfin[...], data)
        if extra is not None:
            total = total + extra[:OWN, :].astype(f32)
        total = total.reshape(GX, CY, NZ)
        planes = pl.ds(pl.multiple_of(k * GX, GX), GX)
        buf[planes, :, :] = total
        rims[planes, :8, :] = total[:, :8]
        rims[planes, 8:, :] = total[:, CY - 8 :]

    def step(c, carry):
        for b in range(per):
            block(c * per + b, None)
        inner_copy(buf, out, sems, c).start()
        return carry

    for b in range(per):
        block(b, rxlo if b == 0 else None)
    inner_copy(buf, out, sems, 0).start()
    lax.fori_loop(1, CHUNKS - 1, step, 0, unroll=2)
    for b in range(per):
        block(BLOCKS - per + b, rxhi if b == per - 1 else None)
    inner_copy(buf, out, sems, CHUNKS - 1).start()
    for c in range(CHUNKS):
        inner_copy(buf, out, sems, c).wait()


def finish(*args):
    return call(
        finish_kernel,
        (sds((CX, CY, NZ), f32), sds((CX, 16, NZ), f32)),
        [VM] * 5 + [ANY],
        16,
        out_specs=(HBM, VM),
        scratch=[pltpu.VMEM((CX, CY, NZ), f32), pltpu.SemaphoreType.DMA((CHUNKS,))],
    )(*args)


def combine_kernel(partial, rims, spread, rylo, ryhi, cornlo, cornhi, out, buf, sems):
    planes = CX // CHUNKS
    per = BLOCKS // CHUNKS

    def copies(c):
        at = pl.ds(c * planes, planes)
        return [
            pltpu.make_async_copy(
                buf.at[at, pl.ds(8 * i, 8), :], out.at[at, pl.ds(i * (CY - 8), 8), :],
                sems.at[2 * c + i],
            )
            for i in range(2)
        ]

    for c in range(CHUNKS):
        for b in range(per):
            k = c * per + b
            rim = slice(k * RIM, (k + 1) * RIM)
            data = jnp.concatenate([rylo[rim, :], ryhi[rim, :]], 0)
            strips = dot(spread[...], data)
            if k in (0, BLOCKS - 1):
                at = slice(0, RIM) if k == 0 else slice(RIM, 2 * RIM)
                data = jnp.concatenate([cornlo[at, :], cornhi[at, :]], 0)
                strips = strips + dot(spread[...], data)
            strips = strips.reshape(GX, 16, NZ)
            at = slice(k * GX, (k + 1) * GX)
            buf[at] = rims[at] + strips
        for copy in copies(c):
            copy.start()
    for c in range(CHUNKS):
        for copy in copies(c):
            copy.wait()


def combine(*args):
    return pl.pallas_call(
        combine_kernel,
        out_shape=sds((CX, CY, NZ), f32),
        in_specs=[HBM] + [VM] * 6,
        out_specs=HBM,
        scratch_shapes=[pltpu.VMEM((CX, 16, NZ), f32), pltpu.SemaphoreType.DMA((2 * CHUNKS,))],
        input_output_aliases={0: 0},
        compiler_params=pltpu.CompilerParams(vmem_limit_bytes=16 << 20),
        name="combine",
    )(*args)


def shift(x, axis, step):
    size = lax.axis_size(axis)
    return lax.ppermute(x, axis, [(i, (i + step) % size) for i in range(size)])


def exchange(x, axis):
    return lax.all_to_all(x, axis, 0, 0)


def local(
    residual, local_x, local_y, local_z, eig_x, eig_y, eig_z, coarse_x, coarse_y, coarse_z,
    mode_x, mode_y, mode_z, coarse_eig_x, coarse_eig_y, coarse_eig_z,
):
    cells = residual.reshape(CELLS, NZ)
    first_x, last_x, rim_lo, rim_hi, along_y, sel = load(cells, coarse_y)
    xlo = shift(last_x, "gx", 1)
    xhi = shift(first_x, "gx", -1)
    own_coarse = call(restrict_kernel, sds((8, MODES, 16), f32), [VM] * 3, 8)(
        along_y, coarse_x.T, coarse_z.T
    )
    rows = exchange(own_coarse, "gx")
    down, up = corners(sel, rim_lo, rim_hi, xlo, xhi, own_coarse)
    ylo = shift(up, "gy", 1)
    yhi = shift(down, "gy", -1)
    modes_xz = call(modes_kernel, sds((128, 128), f32), [VM, VM, ANY], 4)(mode_x, mode_z, up)
    part = call(coarse_x_kernel, sds((32, MODES, 128), f32), [VM] * 2, 4)(rows, modes_xz)
    rows = exchange(part, "gy")

    wy, wyt, wfin, spread, wx, wxt, lz, lzt, exb, eyz = prepare(
        local_x, local_y, local_z, eig_x[None], eig_y[None], eig_z[None], coarse_y.T, part
    )
    field, out_xlo, out_xhi, out_ylo, out_yhi = solve(
        cells, xlo, xhi, ylo, yhi, wy, wyt, wx, wxt, lz, lzt, exb, eyz, part
    )

    rylo = shift(out_yhi, "gy", 1)
    ryhi = shift(out_ylo, "gy", -1)
    rxlo = shift(out_xhi, "gx", 1)
    rxhi = shift(out_xlo, "gx", -1)
    far = [
        pltpu.with_memory_space_constraint(x, pltpu.HBM)
        for x in (
            mode_y, coarse_eig_x[None], coarse_eig_y[None], coarse_eig_z[None], coarse_x.T,
            coarse_z.T,
        )
    ]
    shape = call(
        coarse_kernel,
        sds((2 * CX * MODES, NZ), bf16),
        [VM] * 2 + [HBM] * len(far) + [ANY],
        8,
        scratch=[pltpu.VMEM(*c) for c in COARSE] + [pltpu.SemaphoreType.DMA((len(COARSE),))],
    )(rows, modes_xz, *far, out_ylo)
    down, up = turn(rxlo, rxhi, shape)
    cornlo = shift(up, "gy", 1)
    cornhi = shift(down, "gy", -1)
    partial, rims = finish(field, wfin, shape, rxlo, rxhi, up)
    return combine(partial, rims, spread, rylo, ryhi, cornlo, cornhi)


def solution(mesh):
    cells = P("gx", "gy", None)

    return jax.shard_map(
        local, mesh=mesh, in_specs=(cells,) + (P(),) * 15, out_specs=cells, check_vma=False
    )
```

```python
import jax
import jax.numpy as jnp
from jax import lax
from jax.experimental import pallas as pl
from jax.experimental.pallas import tpu as pltpu
from jax.sharding import PartitionSpec as P


OV = 4
MODES = 4
CX = 128
CY = 32
NZ = 256
EX = 136
EY = 40
GX = 4
ROWS = GX * EY
OWN = GX * CY
RIM = GX * OV
BLOCKS = CX // GX
CELLS = CX * CY
CHUNKS = 8
WIDE_LOAD = 50
WIDE_SOLVE = 48
HI = lax.Precision.HIGHEST
f32 = jnp.float32
bf16 = jnp.bfloat16
sds = jax.ShapeDtypeStruct

VM = pl.BlockSpec(memory_space=pltpu.VMEM)
SM = pl.BlockSpec(memory_space=pltpu.SMEM)
ANY = pl.BlockSpec(memory_space=pl.ANY)
HBM = pl.BlockSpec(memory_space=pltpu.HBM)


def dot(a, b):
    return jnp.dot(a, b, preferred_element_type=f32)


def dot_t(a, b):
    return lax.dot_general(a, b, (((1,), (1,)), ((), ())), preferred_element_type=f32)


def dot_hi(a, b):
    return jnp.dot(a, b, preferred_element_type=f32, precision=HI)


def dot_t_hi(a, b):
    dims = (((1,), (1,)), ((), ()))
    return lax.dot_general(a, b, dims, preferred_element_type=f32, precision=HI)


def split(x):
    high = x.astype(bf16)
    return high, (x - high.astype(f32)).astype(bf16)


def split3(x):
    high = x.astype(bf16)
    rest = x - high.astype(f32)
    middle = rest.astype(bf16)
    return high, middle, (rest - middle.astype(f32)).astype(bf16)


def expand(x, rows=None, cols=None):
    parts = split3(x)
    if rows is not None:
        return dot(jnp.concatenate([rows] * 3, 1), jnp.concatenate(parts, 0))
    return dot(jnp.concatenate(parts, 1), jnp.concatenate([cols] * 3, 0))


def iotas(shape):
    return lax.broadcasted_iota(jnp.int32, shape, 0), lax.broadcasted_iota(jnp.int32, shape, 1)


def pick(mask, kind=bf16):
    return jnp.where(mask, 1.0, 0.0).astype(kind)


def call(kernel, out_shape, in_specs, mib, out_specs=None, scratch=()):
    if out_specs is None:
        out_specs = jax.tree.map(lambda _: VM, out_shape)
    return pl.pallas_call(
        kernel,
        out_shape=out_shape,
        in_specs=in_specs,
        out_specs=out_specs,
        scratch_shapes=list(scratch),
        compiler_params=pltpu.CompilerParams(vmem_limit_bytes=mib << 20),
    )


def tile(ref, k, rows):
    return ref[pl.ds(pl.multiple_of(k * rows, rows), rows), :]


def selection(cyt):
    row, col = iotas((3 * RIM, OWN))
    modes = jnp.concatenate([cyt.astype(f32)] * GX, 1)
    modes = jnp.concatenate([jnp.concatenate([modes] * 2, 0)] * (3 * RIM // 8), 0)
    plane = ((row >> 2) & 3) == (col >> 5)
    inner = col & 31
    target = jnp.where(row < RIM, row & 3, CY - OV + (row & 3))
    ones = jnp.where(inner == target, 1.0, 0.0)
    value = jnp.where(row < 2 * RIM, ones, modes)
    return jnp.where(plane, value, 0.0).astype(bf16)


def load_kernel(
    residual, cyt, first_x, last_x, rim_lo, rim_hi, along_y, sel, buf, sems, cyt_buf, sem
):
    rows = CELLS // CHUNKS

    def copy(c):
        at = pl.ds(c * rows, rows)
        return pltpu.make_async_copy(residual.at[at, :], buf.at[at, :], sems.at[c])

    small = pltpu.make_async_copy(cyt, cyt_buf, sem)
    small.start()
    for c in range(CHUNKS):
        copy(c).start()
    early = 2
    per = rows // OWN
    rims = selection(jnp.zeros((MODES, CY), bf16))[: 2 * RIM]

    def block(k):
        return buf[k * OWN : (k + 1) * OWN, :].astype(bf16)

    def put_rims(k, out):
        at = slice(k * RIM, (k + 1) * RIM)
        rim_lo[at, :] = out[:RIM].astype(bf16)
        rim_hi[at, :] = out[RIM : 2 * RIM].astype(bf16)

    for c in range(early):
        copy(c).wait()
        for k in range(c * per, (c + 1) * per):
            put_rims(k, dot(rims, block(k)))
    small.wait()
    take = selection(cyt_buf[...])
    sel[...] = take
    for c in range(early, CHUNKS):
        copy(c).wait()
        for k in range(c * per, (c + 1) * per):
            out = dot(take, block(k))
            put_rims(k, out)
            along_y[k * RIM : (k + 1) * RIM, :] = out[2 * RIM :]
    for k in range(early * per):
        along_y[k * RIM : (k + 1) * RIM, :] = dot(take[2 * RIM :], block(k))
    first_x[...] = block(0)
    last_x[...] = block(BLOCKS - 1)


def load(residual, coarse_y):
    rim = sds((CX * OV, NZ), bf16)
    return call(
        load_kernel,
        (
            sds((OWN, NZ), bf16), sds((OWN, NZ), bf16), rim, rim,
            sds((CX * MODES, NZ), f32), sds((3 * RIM, OWN), bf16),
        ),
        [HBM, HBM],
        WIDE_LOAD,
        scratch=[
            pltpu.VMEM((CELLS, NZ), f32), pltpu.SemaphoreType.DMA((CHUNKS,)),
            pltpu.VMEM((MODES, CY), bf16), pltpu.SemaphoreType.DMA,
        ],
    )(residual, pltpu.with_memory_space_constraint(coarse_y.T, pltpu.HBM))


def corners_kernel(sel, rim_lo, rim_hi, xlo, xhi, after, down, up):
    down[: CX * OV, :] = rim_lo[...]
    up[: CX * OV, :] = rim_hi[...]
    for i, strip in enumerate((xlo, xhi)):
        out = dot(sel[: 2 * RIM, :], strip[...]).astype(bf16)
        at = slice(CX * OV + i * RIM, CX * OV + (i + 1) * RIM)
        down[at, :] = out[:RIM]
        up[at, :] = out[RIM:]


def corners(*args):
    side = sds((EX * OV, NZ), bf16)
    return call(corners_kernel, (side, side), [VM] * 5 + [ANY], 8)(*args)


PARAMS = (
    ((EX, EX), bf16), ((EY, EY), bf16), ((NZ, NZ), bf16), ((1, EX), f32), ((1, EY), f32),
    ((1, NZ), f32), ((MODES, CY), bf16),
)
WEIGHTS = (
    ((ROWS, ROWS), bf16), ((ROWS, ROWS), bf16), ((OWN, ROWS + 2 * RIM), bf16),
    ((OWN // 2, 2 * RIM), bf16), ((EX, EX), bf16),
    ((EX, EX), bf16), ((NZ, NZ), bf16), ((NZ, NZ), bf16), ((EX, NZ), f32), ((EY, NZ), f32),
)


def basis_x(cxt):
    x, row = iotas((CX, CX * MODES))
    by_row = dot(cxt, pick((row >> 2) == x)).astype(bf16)
    col, m = iotas((16, MODES))
    value = dot(pick((col >> 2) == m), by_row)
    col, row = iotas((16, CX * MODES))
    return jnp.where((row & 3) == (col & 3), value, 0.0).astype(bf16)


def spread_z(mode_z):
    row, col = iotas((128, 128))
    out = jnp.zeros((128, 128), f32)
    for p in range(MODES):
        for c in range(MODES):
            here = ((row & 3) == p) & ((col & 3) == c)
            out = jnp.where(here, mode_z[p : p + 1, c : c + 1], out)
    return out


def modes_a():
    a, col = iotas((32, 128))
    c, col4 = iotas((MODES, 128))
    return pick((col >> 2) == a), pick((col4 & 3) == c)


def prepare_kernel(*refs):
    n = len(PARAMS)
    bufs, outs = refs[:n], refs[n + 1 :]
    lx, ly, lz, eig_x, eig_y, eig_z, cyt = bufs
    wy, wyt, wfin, spread, wx, wxt, lz_out, lzt, exb, eyz = outs

    def cell(k):
        y = jnp.where(k < OWN, OV + (k & 31), jnp.where(k < OWN + RIM, k & 3, EY - OV + (k & 3)))
        plane = jnp.where(k < OWN, k >> 5, ((k - OWN) >> 2) & 3)
        return y, plane

    def mode(j):
        plane = (j >= EY).astype(jnp.int32) + (j >= 2 * EY) + (j >= 3 * EY)
        return j - EY * plane, plane

    k, y = iotas((ROWS, EY))
    by_cell = dot(pick(cell(k)[0] == y), ly[...]).astype(bf16)
    b, j = iotas((EY, ROWS))
    k, col = iotas((ROWS, ROWS))
    value = dot(by_cell, pick(mode(j)[0] == b))
    value = jnp.where(cell(k)[1] == mode(col)[1], value, 0.0).astype(bf16)
    wyt[...] = value
    j, b = iotas((ROWS, EY))
    back = dot_t(pick(mode(j)[0] == b), by_cell)
    wy[...] = jnp.where(mode(k)[1] == cell(col)[1], back, 0.0).astype(bf16)

    y, k = iotas((CY, OWN))
    by_k = dot(cyt[...], pick((k & 31) == y)).astype(bf16)
    k, own = iotas((OWN, OWN))
    turned = dot_t(pick(k == own), by_k).astype(bf16)
    n, col = iotas((MODES, 2 * RIM))
    coarse = dot(turned, pick((col & 3) == n))
    k, col = iotas((OWN, 2 * RIM))
    inner = k & 31
    plane = (k >> 5) == ((col >> 2) & 3)
    coarse = jnp.where(plane, coarse, 0.0).astype(bf16)
    wfin[...] = jnp.concatenate([value[:OWN], coarse], 1)
    k, col = iotas((OWN // 2, 2 * RIM))
    inner = (k & 15) + jnp.where((k & 15) < 8, 0, CY - 16)
    target = jnp.where(col < RIM, col & 3, CY - OV + (col & 3))
    ones = jnp.where(inner == target, 1.0, 0.0)
    spread[...] = jnp.where((k >> 4) == ((col >> 2) & 3), ones, 0.0).astype(bf16)

    k, x = iotas((EX, EX))
    source = jnp.where(k < CX, k + OV, jnp.where(k < CX + OV, k - CX, k))
    moved = dot(pick(source == x), lx[...]).astype(bf16)
    wxt[...] = moved
    wx[...] = dot_t(pick(k == x), moved).astype(bf16)
    column = jnp.sum(jnp.where(k == x, eig_x[...], 0.0), axis=1, keepdims=True)
    exb[...] = jnp.broadcast_to(column, (EX, NZ))
    b, y = iotas((EY, EY))
    column = jnp.sum(jnp.where(b == y, eig_y[...], 0.0), axis=1, keepdims=True)
    eyz[...] = column + eig_z[...]
    c, z = iotas((NZ, NZ))
    lz_out[...] = lz[...]
    lzt[...] = dot_t(pick(c == z), lz[...]).astype(bf16)


def prepare(*params):
    return call(
        prepare_kernel, tuple(sds(*w) for w in WEIGHTS), [VM] * len(PARAMS) + [ANY], 8
    )(*params)


def solve_kernel(
    residual, xlo, xhi, ylo, yhi, wy, wyt, wx, wxt, lz, lzt, exb, eyz, after,
    kept, far_xlo, far_xhi, far_ylo, far_yhi, field, mid, spec, buf, sems,
    out_xlo, out_xhi, out_ylo, out_yhi, sems_out,
):
    def put(rows, value):
        field[0, rows, :] = value[:, :128]
        field[1, rows, :] = value[:, 128:]

    def take(rows):
        return jnp.concatenate([field[0, rows, :], field[1, rows, :]], 1)

    def forward_y(main, k):
        data = jnp.concatenate([main, tile(ylo, k, RIM), tile(yhi, k, RIM)], 0)
        put(pl.ds(pl.multiple_of(k * ROWS, ROWS), ROWS), dot(wy[...], data))

    rows = CELLS // CHUNKS
    per = BLOCKS // CHUNKS

    def copy(c):
        at = pl.ds(pl.multiple_of(c * rows, rows), rows)
        return pltpu.make_async_copy(residual.at[at, :], buf.at[at, :], sems.at[c])

    for c in range(CHUNKS):
        copy(c).start()

    def first(c, carry):
        for i in range(2):
            copy(2 * c + i).wait()
        for b in range(2 * per):
            k = c * 2 * per + b
            forward_y(tile(buf, k, OWN).astype(bf16), k)
        return carry

    lax.fori_loop(0, CHUNKS // 2, first, 0)
    forward_y(xlo[...], BLOCKS)
    forward_y(xhi[...], BLOCKS + 1)

    def mid_rows(b):
        return pl.ds(pl.multiple_of(b * EX, 8), EX)

    def forward_x(b, carry):
        plane = take(pl.ds(b, EX, stride=EY)).astype(bf16)
        mid[mid_rows(b), :] = dot(wx[...], plane)
        return carry

    lax.fori_loop(0, EY, forward_x, 0, unroll=40)

    def forward_z(i, carry):
        at = pl.ds(pl.multiple_of(i * 4 * EX, 16), 4 * EX)
        along = dot(mid[at, :].astype(bf16), lz[...])
        parts = []
        for q in range(4):
            scale = exb[...] + eyz[pl.ds(i * 4 + q, 1), :]
            parts.append((along[q * EX : (q + 1) * EX] / scale))
        spec[at, :] = jnp.concatenate(parts, 0).astype(bf16)
        return carry

    lax.fori_loop(0, EY // 4, forward_z, 0, unroll=10)

    def backward_z(i, carry):
        at = pl.ds(pl.multiple_of(i * 4 * EX, 16), 4 * EX)
        mid[at, :] = dot(spec[at, :], lzt[...])
        return carry

    lax.fori_loop(0, EY // 4, backward_z, 0, unroll=10)

    def backward_x(b, carry):
        put(pl.ds(b, EX, stride=EY), dot(wxt[...], mid[mid_rows(b), :].astype(bf16)))
        return carry

    lax.fori_loop(0, EY, backward_x, 0, unroll=40)

    def planes(k):
        return take(pl.ds(pl.multiple_of(k * ROWS, ROWS), ROWS)).astype(bf16)

    out_xlo[...] = dot(wyt[...], planes(BLOCKS)).astype(bf16)
    out_xhi[...] = dot(wyt[...], planes(BLOCKS + 1)).astype(bf16)

    def last(k, carry):
        data = planes(k)
        kept[pl.ds(pl.multiple_of(k * ROWS, ROWS), ROWS), :] = data
        out = dot(wyt[OWN:, :], data).astype(bf16)
        at = pl.ds(pl.multiple_of(k * RIM, RIM), RIM)
        out_ylo[at, :] = out[:RIM]
        out_yhi[at, :] = out[RIM:]
        return carry

    copies = [
        pltpu.make_async_copy(out_xlo, far_xlo, sems_out.at[0]),
        pltpu.make_async_copy(out_xhi, far_xhi, sems_out.at[1]),
    ]
    for copy in copies:
        copy.start()
    half = BLOCKS // 2
    for i in range(2):
        lax.fori_loop(i * half, (i + 1) * half, last, 0, unroll=half)
        at = pl.ds(i * half * RIM, half * RIM)
        for j, (near, far) in enumerate(((out_ylo, far_ylo), (out_yhi, far_yhi))):
            sem = sems_out.at[2 + 2 * i + j]
            copy = pltpu.make_async_copy(near.at[at, :], far.at[at, :], sem)
            copy.start()
            copies.append(copy)
    for copy in copies:
        copy.wait()


def solve(*args):
    strip = sds((ROWS, NZ), bf16)
    rim = sds((CX * OV, NZ), bf16)
    return call(
        solve_kernel,
        (sds((BLOCKS * ROWS, NZ), bf16), strip, strip, rim, rim),
        [HBM] + [VM] * 12 + [ANY],
        WIDE_SOLVE,
        out_specs=(VM, ANY, ANY, ANY, ANY),
        scratch=[
            pltpu.VMEM((2, EX * EY, NZ // 2), f32), pltpu.VMEM((EX * EY, NZ), f32),
            pltpu.VMEM((EX * EY, NZ), bf16), pltpu.VMEM((CELLS, NZ), f32),
            pltpu.SemaphoreType.DMA((CHUNKS,)), pltpu.VMEM((ROWS, NZ), bf16),
            pltpu.VMEM((ROWS, NZ), bf16), pltpu.VMEM((CX * OV, NZ), bf16),
            pltpu.VMEM((CX * OV, NZ), bf16), pltpu.SemaphoreType.DMA((6,)),
        ],
    )(*args)


def turn_kernel(rxlo, rxhi, after, down, up):
    for start, out in ((OWN, down), (OWN + RIM, up)):
        out[:RIM, :] = rxlo[start : start + RIM, :]
        out[RIM:, :] = rxhi[start : start + RIM, :]


def turn(*args):
    both = sds((2 * RIM, NZ), bf16)
    return call(turn_kernel, (both, both), [VM] * 2 + [ANY], 4)(*args)


def restrict_kernel(along_y, cxt, czt, out):
    bx = basis_x(cxt[...])
    high, low = split(along_y[...])
    both = dot(bx, high) + dot(bx, low)
    own = dot_t_hi(both, czt[...].astype(f32))
    flat = jnp.concatenate([own[m * MODES : (m + 1) * MODES] for m in range(MODES)], 1)
    for i in range(out.shape[0]):
        out[i] = flat


def modes_kernel(mode_x, mode_z, after, modes_xz):
    to_a, _ = modes_a()
    r, i = iotas((128, 32))
    part_x = expand(expand(mode_x[...], rows=pick((r >> 2) == i)), cols=to_a)
    part_z = spread_z(mode_z[...])
    modes_xz[...] = part_x * part_z


def coarse_x_kernel(rows, modes_xz, out):
    part = dot_hi(jnp.concatenate([rows[i] for i in range(8)], 1), modes_xz[...])
    for i in range(out.shape[0]):
        out[i] = part


COARSE = (
    ((128, 128), f32), ((1, 32), f32), ((1, 128), f32), ((1, MODES), f32), ((MODES, CX), bf16),
    ((MODES, NZ), bf16),
)


def coarse_kernel(rows, modes_xz, *refs):
    n = len(COARSE)
    sources, out, bufs, sems = refs[:n], refs[n + 1], refs[n + 2 : -1], refs[-1]
    copies = [
        pltpu.make_async_copy(source, buf, sems.at[i])
        for i, (source, buf) in enumerate(zip(sources, bufs))
    ]
    for copy in copies:
        copy.start()
    for copy in copies:
        copy.wait()
    mode_y, ceig_x, ceig_y, ceig_z, cxt, czt = bufs
    to_a, to_c = modes_a()
    eight_x = jnp.broadcast_to(ceig_x[...], (8, 32))
    eight_z = jnp.broadcast_to(ceig_z[...], (8, MODES))
    row = (dot_hi(eight_x, to_a.astype(f32)) + dot_hi(eight_z, to_c.astype(f32)))[:1]
    r, b = iotas((128, 128))
    column = jnp.sum(jnp.where(r == b, ceig_y[...], 0.0), axis=1, keepdims=True)
    columns = jnp.concatenate([rows[j] for j in range(rows.shape[0])], 0)
    hat = dot_hi(mode_y[...].T, columns) / (column + row)
    row, col = iotas((8, 128))
    mine = pick(col == lax.axis_index("gy") * MODES + row, f32)
    rows_y = dot_hi(mine, mode_y[...])
    rows_xz = modes_xz[pl.ds(pl.multiple_of(lax.axis_index("gx") * 16, 16), 16), :]
    sol = dot_t_hi(dot_hi(rows_y, hat), rows_xz)
    levels = czt[...].astype(f32)
    shape = jnp.concatenate(
        [dot_hi(sol[:, m * MODES : (m + 1) * MODES], levels)[:MODES] for m in range(MODES)], 0
    )
    high, low = split(shape)
    col, i = iotas((32, 16))
    twice = dot(pick((col & 15) == i), basis_x(cxt[...]))
    value = dot(twice.T.astype(bf16), jnp.concatenate([high, low], 0))
    high, low = split(value)
    for k in range(BLOCKS):
        at = slice(k * RIM, (k + 1) * RIM)
        out[2 * k * RIM : (2 * k + 1) * RIM, :] = high[at]
        out[(2 * k + 1) * RIM : (2 * k + 2) * RIM, :] = low[at]


def inner_copy(buf, out, sems, c):
    at = pl.ds(pl.multiple_of(c * (CX // CHUNKS), CX // CHUNKS), CX // CHUNKS)
    inner = pl.ds(8, CY - 16)
    return pltpu.make_async_copy(buf.at[at, inner, :], out.at[at, inner, :], sems.at[c])


def finish_kernel(field, wfin, shape, rxlo, rxhi, after, out, rims, buf, sems):
    per = BLOCKS // CHUNKS

    def block(k, extra):
        data = jnp.concatenate([tile(field, k, ROWS), tile(shape, k, 2 * RIM)], 0)
        total = dot(wfin[...], data)
        if extra is not None:
            total = total + extra[:OWN, :].astype(f32)
        total = total.reshape(GX, CY, NZ)
        planes = pl.ds(pl.multiple_of(k * GX, GX), GX)
        buf[planes, :, :] = total
        rims[planes, :8, :] = total[:, :8]
        rims[planes, 8:, :] = total[:, CY - 8 :]

    def step(c, carry):
        for b in range(per):
            block(c * per + b, None)
        inner_copy(buf, out, sems, c).start()
        return carry

    for b in range(per):
        block(b, rxlo if b == 0 else None)
    inner_copy(buf, out, sems, 0).start()
    lax.fori_loop(1, CHUNKS - 1, step, 0, unroll=2)
    for b in range(per):
        block(BLOCKS - per + b, rxhi if b == per - 1 else None)
    inner_copy(buf, out, sems, CHUNKS - 1).start()
    for c in range(CHUNKS):
        inner_copy(buf, out, sems, c).wait()


def finish(*args):
    return call(
        finish_kernel,
        (sds((CX, CY, NZ), f32), sds((CX, 16, NZ), f32)),
        [VM] * 5 + [ANY],
        16,
        out_specs=(HBM, VM),
        scratch=[pltpu.VMEM((CX, CY, NZ), f32), pltpu.SemaphoreType.DMA((CHUNKS,))],
    )(*args)


def combine_kernel(partial, rims, spread, rylo, ryhi, cornlo, cornhi, out, buf, sems):
    planes = CX // CHUNKS
    per = BLOCKS // CHUNKS

    def copies(c):
        at = pl.ds(c * planes, planes)
        return [
            pltpu.make_async_copy(
                buf.at[at, pl.ds(8 * i, 8), :], out.at[at, pl.ds(i * (CY - 8), 8), :],
                sems.at[2 * c + i],
            )
            for i in range(2)
        ]

    for c in range(CHUNKS):
        for b in range(per):
            k = c * per + b
            rim = slice(k * RIM, (k + 1) * RIM)
            data = jnp.concatenate([rylo[rim, :], ryhi[rim, :]], 0)
            strips = dot(spread[...], data)
            if k in (0, BLOCKS - 1):
                at = slice(0, RIM) if k == 0 else slice(RIM, 2 * RIM)
                data = jnp.concatenate([cornlo[at, :], cornhi[at, :]], 0)
                strips = strips + dot(spread[...], data)
            strips = strips.reshape(GX, 16, NZ)
            at = slice(k * GX, (k + 1) * GX)
            buf[at] = rims[at] + strips
        for copy in copies(c):
            copy.start()
    for c in range(CHUNKS):
        for copy in copies(c):
            copy.wait()


def combine(*args):
    return pl.pallas_call(
        combine_kernel,
        out_shape=sds((CX, CY, NZ), f32),
        in_specs=[HBM] + [VM] * 6,
        out_specs=HBM,
        scratch_shapes=[pltpu.VMEM((CX, 16, NZ), f32), pltpu.SemaphoreType.DMA((2 * CHUNKS,))],
        input_output_aliases={0: 0},
        compiler_params=pltpu.CompilerParams(vmem_limit_bytes=16 << 20),
        name="combine",
    )(*args)


def shift(x, axis, step):
    size = lax.axis_size(axis)
    return lax.ppermute(x, axis, [(i, (i + step) % size) for i in range(size)])


def exchange(x, axis):
    return lax.all_to_all(x, axis, 0, 0)


def local(
    residual, local_x, local_y, local_z, eig_x, eig_y, eig_z, coarse_x, coarse_y, coarse_z,
    mode_x, mode_y, mode_z, coarse_eig_x, coarse_eig_y, coarse_eig_z,
):
    cells = residual.reshape(CELLS, NZ)
    first_x, last_x, rim_lo, rim_hi, along_y, sel = load(cells, coarse_y)
    xlo = shift(last_x, "gx", 1)
    xhi = shift(first_x, "gx", -1)
    own_coarse = call(restrict_kernel, sds((8, MODES, 16), f32), [VM] * 3, 8)(
        along_y, coarse_x.T, coarse_z.T
    )
    rows = exchange(own_coarse, "gx")
    down, up = corners(sel, rim_lo, rim_hi, xlo, xhi, own_coarse)
    ylo = shift(up, "gy", 1)
    yhi = shift(down, "gy", -1)
    modes_xz = call(modes_kernel, sds((128, 128), f32), [VM, VM, ANY], 4)(mode_x, mode_z, up)
    part = call(coarse_x_kernel, sds((32, MODES, 128), f32), [VM] * 2, 4)(rows, modes_xz)
    rows = exchange(part, "gy")

    wy, wyt, wfin, spread, wx, wxt, lz, lzt, exb, eyz = prepare(
        local_x, local_y, local_z, eig_x[None], eig_y[None], eig_z[None], coarse_y.T, part
    )
    field, out_xlo, out_xhi, out_ylo, out_yhi = solve(
        cells, xlo, xhi, ylo, yhi, wy, wyt, wx, wxt, lz, lzt, exb, eyz, part
    )

    rylo = shift(out_yhi, "gy", 1)
    ryhi = shift(out_ylo, "gy", -1)
    rxlo = shift(out_xhi, "gx", 1)
    rxhi = shift(out_xlo, "gx", -1)
    far = [
        pltpu.with_memory_space_constraint(x, pltpu.HBM)
        for x in (
            mode_y, coarse_eig_x[None], coarse_eig_y[None], coarse_eig_z[None], coarse_x.T,
            coarse_z.T,
        )
    ]
    shape = call(
        coarse_kernel,
        sds((2 * CX * MODES, NZ), bf16),
        [VM] * 2 + [HBM] * len(far) + [ANY],
        8,
        scratch=[pltpu.VMEM(*c) for c in COARSE] + [pltpu.SemaphoreType.DMA((len(COARSE),))],
    )(rows, modes_xz, *far, out_ylo)
    down, up = turn(rxlo, rxhi, shape)
    cornlo = shift(up, "gy", 1)
    cornhi = shift(down, "gy", -1)
    partial, rims = finish(field, wfin, shape, rxlo, rxhi, up)
    return combine(partial, rims, spread, rylo, ryhi, cornlo, cornhi)


def solution(mesh):
    cells = P("gx", "gy", None)

    return jax.shard_map(
        local, mesh=mesh, in_specs=(cells,) + (P(),) * 15, out_specs=cells, check_vma=False
    )
```
